512 devices in a mesh: comp: 2 (over z_lo), lat: 16 (over y, core), lon: 16 (over x, z_hi).
Axes of the slice: x: 4, y: 8, z: 8 (z_hi: 4, z_lo: 2; z = z_hi * 2 + z_lo), core: 2. Of those that a mesh axis runs over, the one named last changes fastest.
Arguments:
- state: float32 [2, 12, 256, 2048], P('comp', None, 'lat', 'lon'), may hold values from -6 to 6
- prev_surface: float32 [2, 256, 2048], P(None, 'lat', 'lon'), may hold values from -6 to 6
- mixing: float32 [2, 11, 256, 2048], P('comp', None, 'lat', 'lon'), may hold values from 0.1 to 3
- velocity: float32 [2, 2, 256, 2048], P('comp', None, 'lat', 'lon'), may hold values from -0.3 to 0.3
- coupling: float32 [2, 256, 2048], P('comp', 'lat', 'lon'), may hold values from 0.1 to 1
- sea_mask: int32 [2, 256, 2048], P('comp', 'lat', 'lon'), may hold values 0 or 1
- interp_index: int32 [2, 4, 256, 2048], P('comp', None, 'lat', 'lon'), may hold values from 0 to 2047
- interp_weight: float32 [2, 4, 256, 2048], P('comp', None, 'lat', 'lon'), may hold values from 0.05 to 0.45
Outputs:
- new_state: float32 [2, 12, 256, 2048], P('comp', None, 'lat', 'lon')
- surface_series: float32 [2, 2, 256, 2048], P('comp', None, 'lat', 'lon')
The draws below stay inside these ranges and needn't reach their ends.
Inputs may be any that keep to these rules, and one draw needn't show every extreme that they name: `interp_index`: A tile index, r * 128 + c, of a cell in the same latitude-longitude tile.
All inputs are finite; a program needn't handle non-finite values. No bound on the sum of `sea_mask` on one device may be relied on, other than what follows from the above.
Results may differ from the reference program's by a relative error of at most 0.0001.
Values sent between devices are 32-bit elements; how exact they have to be, the bound alone decides.
No kernel may reach another device: no remote copies, remote signals or barrier semaphores. Data moves between devices by JAX's collectives and lax.ppermute only.
A program may use at most 64 MiB of HBM per device.

```python
import math
import jax
import jax.numpy as jnp

LEV = 12
NSTEP = 2
CLAT = 16
CLON = 128
NLAT = 256
NLON = 2048
CELLS = 2048
N_LAT = 16
N_LON = 16


def with_ends(values, rng, least, largest):
    longest = values.shape.index(max(values.shape))
    spots = []
    for shift in (0, 1):
        where = [jax.random.randint(jax.random.fold_in(rng, axis), (), 0, length) for axis, length in enumerate(values.shape)]
        where[longest] = (where[longest] + shift) % values.shape[longest]
        spots.append(tuple(where))
    return values.at[spots[0]].set(least).at[spots[1]].set(largest)


def shard_levels(stream_key, dims, shards, smallest, high):
    gain = 1.0
    for position, parts in shards:
        steps = jax.random.uniform(jax.random.fold_in(jax.random.fold_in(stream_key, 6), position), (parts,), jnp.float32, smallest / len(shards), high / len(shards))
        gain = gain * jnp.repeat(jnp.exp(steps), dims[position] // parts).reshape((-1,) + (1,) * (len(dims) - 1 - position))
    return gain


def normal_values(rng, dims, scale, reach, shards=(), dtype=jnp.bfloat16):
    level = shard_levels(rng, dims, shards, -0.22, 0.18) if shards else 1.0
    entries = jax.random.normal(rng, dims, jnp.float32) * scale * level
    return jnp.minimum(jnp.maximum(entries, -reach), reach).astype(dtype)


def setup_inputs(seed: int = 0) -> dict:
    seeds = jax.random.split(jax.random.key(seed), 9)
    return {
        "state": normal_values(seeds[0], (2, LEV, NLAT, NLON), 1.0, 6.0, ((0, 2), (2, 16), (3, 16)), jnp.float32),
        "prev_surface": normal_values(seeds[1], (NSTEP, NLAT, NLON), 1.0, 6.0, ((1, 16), (2, 16)), jnp.float32),
        "mixing": jnp.clip(jnp.exp(math.log(3.0) - 3.4011974 * jax.random.uniform(seeds[2], (2, LEV - 1, NLAT, NLON), jnp.float32) ** shard_levels(seeds[2], (2, LEV - 1, NLAT, NLON), ((0, 2), (2, 16), (3, 16)), -0.2, 0.2)), 0.1, 3.0),
        "velocity": jnp.clip(jax.random.uniform(seeds[3], (2, 2, NLAT, NLON), jnp.float32, -0.3, 0.3) * shard_levels(seeds[3], (2, 2, NLAT, NLON), ((0, 2), (2, 16), (3, 16)), -0.4, 0.0), -0.3, 0.3),
        "coupling": jnp.clip(jnp.exp(math.log(1.0) - 2.3025851 * jax.random.uniform(seeds[4], (2, NLAT, NLON), jnp.float32) ** shard_levels(seeds[4], (2, NLAT, NLON), ((0, 2), (1, 16), (2, 16)), -0.2, 0.2)), 0.1, 1.0),
        "sea_mask": with_ends((jax.random.randint(seeds[5], (2, NLAT, NLON), 0, 3) < 2).astype(jnp.int32), jax.random.fold_in(seeds[5], 1), 0, 1),
        "interp_index": with_ends(jax.random.randint(seeds[6], (2, 4, NLAT, NLON), 0, CELLS), jax.random.fold_in(seeds[6], 1), 0, CELLS - 1).astype(jnp.int32),
        "interp_weight": jnp.clip(0.05 + 0.39999999 * jax.random.uniform(seeds[7], (2, 4, NLAT, NLON), jnp.float32) ** shard_levels(seeds[7], (2, 4, NLAT, NLON), ((0, 2), (2, 16), (3, 16)), -0.2, 0.2), 0.05, 0.45),
    }


smoothing = 0.15


def stencil(field, lat_padded, lon_padded, east_speed, north_speed):
    lat_slope = (lat_padded[:, 0:-4] - 8.0 * lat_padded[:, 1:-3] + 8.0 * lat_padded[:, 3:-1] - lat_padded[:, 4:]) / 12.0
    lon_slope = (lon_padded[:, :, 0:-4] - 8.0 * lon_padded[:, :, 1:-3] + 8.0 * lon_padded[:, :, 3:-1] - lon_padded[:, :, 4:]) / 12.0
    lat_curve = lat_padded[:, 1:-3] + lat_padded[:, 3:-1] - 2.0 * field
    lon_curve = lon_padded[:, :, 1:-3] + lon_padded[:, :, 3:-1] - 2.0 * field
    return field + smoothing * (lat_curve + lon_curve) - east_speed * lon_slope - north_speed * lat_slope


def column_solve(rhs, mixing):
    levels = rhs.shape[0]
    nothing = jnp.zeros_like(rhs[0])
    ratios = []
    values = []
    for level in range(levels):
        lower = mixing[level - 1] if level > 0 else nothing
        upper = mixing[level] if level < levels - 1 else nothing
        pivot = 1.0 + lower + upper
        source = rhs[level]
        if level > 0:
            pivot = pivot + lower * ratios[-1]
            source = source + lower * values[-1]
        ratios.append(-upper / pivot)
        values.append(source / pivot)
    result = [values[-1]]
    for level in range(levels - 2, -1, -1):
        result.insert(0, values[level] - ratios[level] * result[0])
    return jnp.stack(result)


def to_tiles(field):
    leading = field.shape[:-2]
    tiled = field.reshape(leading + (N_LAT, CLAT, N_LON, CLON))
    tiled = jnp.moveaxis(tiled, -3, -2)
    return tiled.reshape(leading + (N_LAT, N_LON, CLAT * CLON))


def from_tiles(field):
    leading = field.shape[:-3]
    tiled = field.reshape(leading + (N_LAT, N_LON, CLAT, CLON))
    tiled = jnp.moveaxis(tiled, -2, -3)
    return tiled.reshape(leading + (NLAT, NLON))


def regrid(source, index, weight):
    index_tiles = to_tiles(index)
    source_tiles = jnp.broadcast_to(to_tiles(source)[None], index_tiles.shape)
    picked = jnp.take_along_axis(source_tiles, index_tiles, axis=-1)
    return jnp.sum(weight * from_tiles(picked), axis=0)


def model_step(field, mixing, velocity, coupling, sea, partner, is_atmosphere):
    lat_padded = jnp.pad(field, ((0, 0), (2, 2), (0, 0)))
    lon_padded = jnp.concatenate([field[:, :, -2:], field, field[:, :, :2]], axis=2)
    moved = stencil(field, lat_padded, lon_padded, velocity[0], velocity[1])
    if is_atmosphere:
        forcing = coupling * sea * (partner - field[0])
    else:
        forcing = coupling * sea * partner
    moved = moved.at[0].add(forcing)
    solved = column_solve(moved, mixing)
    if is_atmosphere:
        return solved, forcing
    return solved, solved[0]


def reference(state, prev_surface, mixing, velocity, coupling, sea_mask, interp_index, interp_weight):
    sea = sea_mask.astype(jnp.float32)
    atmos = state[0]
    fluxes = []
    for step_index in range(NSTEP):
        partner = regrid(prev_surface[step_index], interp_index[0], interp_weight[0])
        atmos, flux_now = model_step(atmos, mixing[0], velocity[0], coupling[0], sea[0], partner, True)
        fluxes.append(flux_now)
    ocean = state[1]
    temps = []
    for step_index in range(NSTEP):
        partner = regrid(fluxes[step_index], interp_index[1], interp_weight[1])
        ocean, top_now = model_step(ocean, mixing[1], velocity[1], coupling[1], sea[1], partner, False)
        temps.append(top_now)
    return jnp.stack([atmos, ocean]), jnp.stack([jnp.stack(fluxes), jnp.stack(temps)])
```

```python
import jax
import jax.numpy as jnp
from jax import lax
from jax.experimental import pallas as pl
from jax.experimental.pallas import tpu as pltpu
from jax.sharding import PartitionSpec as P

INTERPRET = False
NSTEP = 2
LEV = 12
ROWS = 16
COLS = 128
smoothing = 0.15

AT_MIX = 4 * LEV
AT_VEL = AT_MIX + 2 * (LEV - 1)
AT_RATE = AT_VEL + 4
AT_WEIGHT = 80
AT_INDEX = 88
AT_WEST = 96
AT_EAST = 100
AT_FLUX = 104
ROW_MESSAGE = AT_FLUX + ROWS
COL_MESSAGE = 2 * ROWS


def lanes(rows):
    return lax.broadcasted_iota(jnp.int32, (rows, COLS), 1)


def sublanes():
    return lax.broadcasted_iota(jnp.int32, (8, COLS), 0)


def roll(x, shift, axis):
    shift %= x.shape[axis]
    return pltpu.roll(x, shift, axis) if shift else x


def gather_cells(table, index):
    row = lax.shift_right_logical(index, 7)
    column = lax.bitwise_and(index, COLS - 1)
    total = jnp.zeros(index.shape, jnp.float32)
    for r in range(ROWS):
        source = jnp.broadcast_to(table[r : r + 1], index.shape)
        picked = jnp.take_along_axis(source, column, axis=1, mode="promise_in_bounds")
        total = jnp.where(row == r, picked, total)
    return total


def regrid_tile(table, index_ref, weight_ref):
    index = index_ref[...].reshape(4 * ROWS, COLS)
    picked = gather_cells(table, index).reshape(4, ROWS, COLS)
    return jnp.sum(picked * weight_ref[...], axis=0)


def pack_columns_kernel(
    state, prev, mix, vel, couple, mask, index, weight, msg0, msg1, flux_out
):
    is_atmosphere = lax.axis_index("comp") == 0
    odd = lax.rem(lax.axis_index("lon"), 2) == 1
    lane = lanes(ROWS)
    rate = couple[...] * mask[...].astype(jnp.float32)

    def packed(last):
        total = jnp.zeros((ROWS, COLS), jnp.float32)

        def put(total, x, at, width):
            shift = at - (COLS - width) if last else at
            return jnp.where((lane >= at) & (lane < at + width), roll(x, shift, 1), total)

        for level in range(LEV):
            total = put(total, state[level], 4 * level, 4)
        for level in range(LEV - 1):
            total = put(total, mix[level], AT_MIX + 2 * level, 2)
        for part in range(2):
            total = put(total, vel[part], AT_VEL + 2 * part, 2)
        total = put(total, rate, AT_RATE, 2)
        for j in range(4):
            total = put(total, weight[j], AT_WEIGHT + 2 * j, 2)
            total = put(total, index[j].astype(jnp.float32), AT_INDEX + 2 * j, 2)
        return total

    first, last = packed(False), packed(True)
    msg0[0:ROWS] = jnp.where(odd, first, last)
    msg1[0:ROWS] = jnp.where(odd, last, first)

    @pl.when(is_atmosphere)
    def _():
        flux = rate * (regrid_tile(prev[0], index, weight) - state[0])
        flux_out[...] = flux
        msg0[ROWS:] = flux
        msg1[ROWS:] = flux

    @pl.when(jnp.logical_not(is_atmosphere))
    def _():
        nothing = jnp.zeros((ROWS, COLS), jnp.float32)
        flux_out[...] = nothing
        msg0[ROWS:] = nothing
        msg1[ROWS:] = nothing


def column_messages(got0, got1):
    odd = lax.rem(lax.axis_index("lon"), 2)
    near = got0[1 - odd]
    far = got1[...]
    return jnp.where(odd == 1, near, far), jnp.where(odd == 1, far, near)


def pack_rows_kernel(
    state, mix, vel, couple, mask, index, weight, flux, got0, got1, msg0, msg1
):
    odd = lax.rem(lax.axis_index("lat"), 2) == 1
    west, east = column_messages(got0, got1)
    rate = couple[...] * mask[...].astype(jnp.float32)

    def put(x, at, width):
        head, tail = x[0:width], x[ROWS - width : ROWS]
        msg0[at : at + width] = jnp.where(odd, head, tail)
        msg1[at : at + width] = jnp.where(odd, tail, head)

    for level in range(LEV):
        put(state[level], 4 * level, 4)
    for level in range(LEV - 1):
        put(mix[level], AT_MIX + 2 * level, 2)
    for part in range(2):
        put(vel[part], AT_VEL + 2 * part, 2)
    put(rate, AT_RATE, 2)
    for j in range(4):
        put(weight[j], AT_WEIGHT + 2 * j, 2)
        put(index[j].astype(jnp.float32), AT_INDEX + 2 * j, 2)
    put(west[0:ROWS], AT_WEST, 4)
    put(east[0:ROWS], AT_EAST, 4)
    for at in (AT_RATE + 2, AT_RATE + 4):
        msg0[at : at + 2] = jnp.zeros((2, COLS), jnp.float32)
        msg1[at : at + 2] = jnp.zeros((2, COLS), jnp.float32)
    msg0[AT_FLUX:] = flux[...]
    msg1[AT_FLUX:] = flux[...]


def row_messages(got0, got1):
    odd = lax.rem(lax.axis_index("lat"), 2)
    near = got0[1 - odd]
    far = got1[...]
    return jnp.where(odd == 1, near, far), jnp.where(odd == 1, far, near)


def east_shift(tile, side, shift, lane):
    rows = side.shape[0]
    moved, moved_side = roll(tile, shift, 1), roll(side, shift, 1)
    cut = lane < shift if shift > 0 else lane >= COLS + shift
    own = jnp.where(cut, moved_side[: tile.shape[0]], moved)
    return own, jnp.where(cut[:rows], moved[:rows], moved_side)


def transport_weights(east, north):
    def weights(v):
        near, far = v * (8.0 / 12.0), v * (1.0 / 12.0)
        return (-far, smoothing + near, smoothing - near, far)

    return weights(east), weights(north)


def horizontal(own, side, own_weights, side_weights, own_rows):
    shifts = (2, 1, -1, -2)
    result = own[:own_rows] * (1.0 - 4.0 * smoothing)
    for shift, factor in zip(shifts, own_weights[1]):
        result = result + factor * roll(own, shift, 0)[:own_rows]
    lane = lanes(own_rows)
    side_result = None
    if side_weights is not None:
        side_result = side[:ROWS] * (1.0 - 4.0 * smoothing)
        for shift, factor in zip(shifts, side_weights[1]):
            side_result = side_result + factor * roll(side, shift, 0)[:ROWS]
    for k, shift in enumerate(shifts):
        moved, moved_side = roll(own[:own_rows], shift, 1), roll(side[:own_rows], shift, 1)
        cut = lane < shift if shift > 0 else lane >= COLS + shift
        result = result + own_weights[0][k] * jnp.where(cut, moved_side, moved)
        if side_weights is not None:
            there = jnp.where(cut[:ROWS], moved[:ROWS], moved_side[:ROWS])
            side_result = side_result + side_weights[0][k] * there
    return result, side_result


def factors(mix):
    inverses, ratios = [], []
    for level in range(LEV):
        pivot = 1.0
        if level < LEV - 1:
            pivot = pivot + mix[level]
        if level > 0:
            pivot = pivot + mix[level - 1] * (1.0 - ratios[-1])
        inverse = 1.0 / pivot
        inverses.append(inverse)
        if level < LEV - 1:
            ratios.append(mix[level] * inverse)
    return inverses, ratios


def solve(rhs, mix, inverses, ratios):
    values = []
    for level in range(LEV):
        source = rhs[level]
        if level > 0:
            source = mix[level - 1] * values[-1] if source is None else source + mix[level - 1] * values[-1]
        values.append(source * inverses[level])
    result = [None] * LEV
    result[-1] = values[-1]
    for level in range(LEV - 2, -1, -1):
        result[level] = values[level] + ratios[level] * result[level + 1]
    return result


def first_step_kernel(
    state, prev, mix, vel, couple, mask, index, weight, flux, col0, col1, row0, row1,
    before, before_side, unit, unit_side, inverse_out, fluxes,
):
    is_atmosphere = lax.axis_index("comp") == 0
    west, east = column_messages(col0, col1)
    north, south = row_messages(row0, row1)
    at_lat = lax.axis_index("lat")
    sub = sublanes()
    valid = ((sub < 4) & (at_lat < lax.axis_size("lat") - 1)) | ((sub >= 4) & (at_lat > 0))

    def rim4(level):
        block, odd = 8 * (level // 2), level % 2
        a, b = south[block : block + 8], north[block : block + 8]
        return jnp.where(sub < 4, roll(a, -4 * odd, 0), roll(b, 4 - 4 * odd, 0))

    def rim2(at):
        block, offset = 8 * (at // 8), at % 8
        a, b = south[block : block + 8], north[block : block + 8]
        a, b = roll(a, -offset, 0), roll(b, 6 - offset, 0)
        return jnp.where(sub < 2, a, jnp.where(sub >= 6, b, 0.0))

    def cornered(packed, at):
        a, b = south[AT_WEST : AT_WEST + 8], north[AT_WEST : AT_WEST + 8]
        if at == AT_WEST:
            rim = jnp.where(sub < 4, a, roll(b, 4, 0))
        else:
            rim = jnp.where(sub < 4, roll(a, 4, 0), b)
        return jnp.concatenate([packed[0:ROWS], rim], axis=0)

    west_tile, east_tile = cornered(west, AT_WEST), cornered(east, AT_EAST)
    wide = lanes(24)

    def side(at, width, rows):
        a, b = roll(east_tile[:rows], -at, 1), roll(west_tile[:rows], COLS - width - at, 1)
        lane = wide[:rows]
        return jnp.where(lane < width, a, jnp.where(lane >= COLS - width, b, 0.0))

    def extended(x, rim):
        return jnp.concatenate([x, rim], axis=0)

    own_mix = [extended(mix[level], rim2(AT_MIX + 2 * level)) for level in range(LEV - 1)]
    side_mix = [side(AT_MIX + 2 * level, 2, ROWS) for level in range(LEV - 1)]
    own_vel = [extended(vel[part], rim2(AT_VEL + 2 * part)) for part in range(2)]
    side_vel = [side(AT_VEL + 2 * part, 2, ROWS) for part in range(2)]
    own_weights, side_weights = transport_weights(*own_vel), transport_weights(*side_vel)

    moved, moved_side = [], []
    for level in range(LEV):
        own = extended(state[level], rim4(level))
        a, b = horizontal(own, side(4 * level, 4, 24), own_weights, side_weights, 24)
        moved.append(a)
        moved_side.append(b)
    inverses, ratios = factors(own_mix)
    solved = solve(moved, own_mix, inverses, ratios)
    impulse = solve([1.0] + [None] * (LEV - 1), own_mix, inverses, ratios)
    rate = couple[...] * mask[...].astype(jnp.float32)

    fluxes[0:ROWS] = flux[...]
    fluxes[ROWS : 2 * ROWS] = west[ROWS:]
    fluxes[2 * ROWS : 3 * ROWS] = east[ROWS:]
    fluxes[3 * ROWS : 4 * ROWS] = north[AT_FLUX:]
    fluxes[4 * ROWS : 5 * ROWS] = south[AT_FLUX:]

    @pl.when(is_atmosphere)
    def _():
        top = solved[0][:ROWS] + flux[...] * impulse[0][:ROWS]
        fluxes[5 * ROWS :] = rate * (regrid_tile(prev[1], index, weight) - top)

    @pl.when(jnp.logical_not(is_atmosphere))
    def _():
        fluxes[5 * ROWS :] = jnp.zeros((ROWS, COLS), jnp.float32)

    for level in range(LEV):
        for out, values in ((before, solved), (unit, impulse)):
            out[level, 0:ROWS] = values[level][:ROWS]
            out[level, ROWS:] = jnp.where(valid, values[level][ROWS:], 0.0)
        inverse_out[level] = inverses[level][:ROWS]
    inverses, ratios = factors(side_mix)
    solved = solve(moved_side, side_mix, inverses, ratios)
    impulse = solve([1.0] + [None] * (LEV - 1), side_mix, inverses, ratios)
    for level in range(LEV):
        before_side[level] = solved[level]
        unit_side[level] = impulse[level]


def second_step_kernel(
    mix, vel, couple, mask, index, weight, col0, col1, row0, row1,
    before, before_side, unit, unit_side, inverse, fluxes, new_state, series, force, force_side, force1,
):
    is_atmosphere = lax.axis_index("comp") == 0
    sub = sublanes()
    lane = lanes(ROWS)
    tables = [fluxes[0, k * ROWS : (k + 1) * ROWS] for k in range(6)]

    @pl.when(is_atmosphere)
    def _():
        force[0:ROWS] = tables[0]
        force[ROWS:] = jnp.where(sub < 4, tables[4][0:8], tables[3][8:16])
        force_side[...] = jnp.where(lane < 64, tables[2], tables[1])
        force1[...] = tables[5]

    @pl.when(jnp.logical_not(is_atmosphere))
    def _():
        rate = couple[...] * mask[...].astype(jnp.float32)
        force[0:ROWS] = rate * regrid_tile(tables[0], index, weight)
        force1[...] = rate * regrid_tile(tables[5], index, weight)
        west, east = column_messages(col0, col1)
        north, south = row_messages(row0, row1)

        def of_rows(message, table, place):
            index8 = message[AT_INDEX : AT_INDEX + 8].astype(jnp.int32)
            total = gather_cells(table, index8) * message[AT_WEIGHT : AT_WEIGHT + 8]
            total = total + roll(total, 4, 0)
            total = total + roll(total, 2, 0)
            block, offset = 8 * (AT_RATE // 8), AT_RATE % 8
            return roll(message[block : block + 8], place - offset, 0) * roll(total, place, 0)

        force[ROWS:] = jnp.where(sub < 4, of_rows(south, tables[4], 0), of_rows(north, tables[3], 6))

        def of_columns(message, table, place):
            tile = message[0:ROWS]
            total = roll(gather_cells(table, tile.astype(jnp.int32)), AT_WEIGHT - AT_INDEX, 1) * tile
            total = total + roll(total, -4, 1)
            total = total + roll(total, -2, 1)
            return roll(tile, place - AT_RATE, 1) * roll(total, place - AT_WEIGHT, 1)

        force_side[...] = jnp.where(
            lane < 64, of_columns(east, tables[2], 0), of_columns(west, tables[1], COLS - 2)
        )

    own_weights = transport_weights(vel[0], vel[1])
    f, f_side = force[...], force_side[...]
    moved = []
    for level in range(LEV):
        own = before[level] + f * unit[level]
        there = before_side[level] + f_side * unit_side[level]
        if level == 0:
            top = own[:ROWS]
        moved.append(horizontal(own, there, own_weights, None, ROWS)[0])
    moved[0] = moved[0] + force1[...]
    own_mix = [mix[level] for level in range(LEV - 1)]
    inverses = [inverse[level] for level in range(LEV)]
    ratios = [own_mix[level] * inverses[level] for level in range(LEV - 1)]
    solved = solve(moved, own_mix, inverses, ratios)
    for level in range(LEV):
        new_state[level] = solved[level]
    series[0] = jnp.where(is_atmosphere, tables[0], top)
    series[1] = jnp.where(is_atmosphere, tables[5], solved[0])


def call(kernel, name, shapes, *args, scratch=()):
    vmem = pl.BlockSpec(memory_space=pltpu.VMEM)
    return pl.pallas_call(
        kernel,
        name=name,
        out_shape=[jax.ShapeDtypeStruct(shape, jnp.float32) for shape in shapes],
        in_specs=[vmem] * len(args),
        out_specs=[vmem] * len(shapes),
        scratch_shapes=[pltpu.VMEM(shape, jnp.float32) for shape in scratch],
        compiler_params=pltpu.CompilerParams(vmem_limit_bytes=16 * 1024 * 1024),
        interpret=INTERPRET,
    )(*args)


def pairs(count, start, wrap):
    found = []
    for i in range(start, count, 2):
        j = i + 1
        if j < count or wrap:
            found += [(i, j % count), (j % count, i)]
    return found


def partners(count):
    return [[i, i + 1] for i in range(0, count, 2)]


def per_device(
    state, prev_surface, mixing, velocity, coupling, sea_mask, interp_index, interp_weight
):
    n_lat, n_lon = lax.axis_size("lat"), lax.axis_size("lon")
    state, mix, vel, couple, mask = state[0], mixing[0], velocity[0], coupling[0], sea_mask[0]
    index, weight = interp_index[0], interp_weight[0]
    tile = (ROWS, COLS)
    column_shape = (COL_MESSAGE, COLS)
    to_near, to_far, flux = call(
        pack_columns_kernel, "pack_columns", [column_shape, column_shape, tile],
        state, prev_surface, mix, vel, couple, mask, index, weight,
    )
    col1 = lax.ppermute(to_far, "lon", pairs(n_lon, 1, True))
    col0 = lax.all_gather(to_near, "lon", axis_index_groups=partners(n_lon))
    row_shape = (ROW_MESSAGE, COLS)
    to_near, to_far = call(
        pack_rows_kernel, "pack_rows", [row_shape, row_shape],
        state, mix, vel, couple, mask, index, weight, flux, col0, col1,
    )
    row1 = lax.ppermute(to_far, "lat", pairs(n_lat, 1, False))
    row0 = lax.all_gather(to_near, "lat", axis_index_groups=partners(n_lat))
    wide, narrow = (LEV, 24, COLS), (LEV, ROWS, COLS)
    *parts, fluxes = call(
        first_step_kernel, "first_step",
        [wide, narrow, wide, narrow, narrow, (6 * ROWS, COLS)],
        state, prev_surface, mix, vel, couple, mask, index, weight, flux, col0, col1, row0, row1,
    )
    fluxes = lax.all_gather(fluxes, "comp")
    new_state, series = call(
        second_step_kernel, "second_step", [(LEV, ROWS, COLS), (NSTEP, ROWS, COLS)],
        mix, vel, couple, mask, index, weight, col0, col1, row0, row1, *parts, fluxes,
        scratch=[(24, COLS), tile, tile],
    )
    return new_state[None], series[None]


def solution(mesh):
    in_specs = (
        P("comp", None, "lat", "lon"),
        P(None, "lat", "lon"),
        P("comp", None, "lat", "lon"),
        P("comp", None, "lat", "lon"),
        P("comp", "lat", "lon"),
        P("comp", "lat", "lon"),
        P("comp", None, "lat", "lon"),
        P("comp", None, "lat", "lon"),
    )
    out_specs = (P("comp", None, "lat", "lon"), P("comp", None, "lat", "lon"))
    return jax.shard_map(
        per_device, mesh=mesh, in_specs=in_specs, out_specs=out_specs, check_vma=False
    )
```

```python
import jax
import jax.numpy as jnp
from jax import lax
from jax.experimental import pallas as pl
from jax.experimental.pallas import tpu as pltpu
from jax.sharding import PartitionSpec as P

INTERPRET = False
NSTEP = 2
LEV = 12
ROWS = 16
COLS = 128
smoothing = 0.15

AT_MIX = 4 * LEV
AT_VEL = AT_MIX + 2 * (LEV - 1)
AT_RATE = AT_VEL + 4
AT_WEIGHT = 80
AT_INDEX = 88
AT_WEST = 96
AT_EAST = 100
AT_FLUX = 104
ROW_MESSAGE = AT_FLUX + ROWS
COL_MESSAGE = 2 * ROWS


def lanes(rows):
    return lax.broadcasted_iota(jnp.int32, (rows, COLS), 1)


def sublanes():
    return lax.broadcasted_iota(jnp.int32, (8, COLS), 0)


def roll(x, shift, axis):
    shift %= x.shape[axis]
    return pltpu.roll(x, shift, axis) if shift else x


def gather_cells(table, index):
    sources = [jnp.broadcast_to(table[r : r + 1], (8, COLS)) for r in range(ROWS)]
    blocks = []
    for at in range(0, index.shape[0], 8):
        cell = index[at : at + 8]
        column = lax.bitwise_and(cell, COLS - 1)
        picked = [
            jnp.take_along_axis(source, column, axis=1, mode="promise_in_bounds")
            for source in sources
        ]
        bit = COLS
        while len(picked) > 1:
            chosen = lax.bitwise_and(cell, bit) != 0
            picked = [jnp.where(chosen, b, a) for a, b in zip(picked[::2], picked[1::2])]
            bit *= 2
        blocks.append(picked[0])
    return jnp.concatenate(blocks, axis=0)


def regrid_tile(table, index_ref, weight_ref):
    index = index_ref[...].reshape(4 * ROWS, COLS)
    picked = gather_cells(table, index).reshape(4, ROWS, COLS)
    return jnp.sum(picked * weight_ref[...], axis=0)


def pack_columns_kernel(
    state_hbm, prev_hbm, mix_hbm, vel_hbm, couple_hbm, mask_hbm, index_hbm, weight_hbm,
    msg0, msg1, flux_out, rate_out, state, prev, mix, vel, index, weight, couple, mask, arrived,
):
    moves = [
        pltpu.make_async_copy(source, target, arrived.at[k])
        for k, (source, target) in enumerate(
            (
                (state_hbm, state),
                (mix_hbm, mix),
                (index_hbm, index),
                (weight_hbm, weight),
                (prev_hbm, prev),
                (vel_hbm, vel),
                (couple_hbm, couple),
                (mask_hbm, mask),
            )
        )
    ]
    for move in moves:
        move.start()
    is_atmosphere = lax.axis_index("comp") == 0
    odd = lax.rem(lax.axis_index("lon"), 2) == 1
    lane = lanes(ROWS)
    for move in moves:
        move.wait()
    rate = couple[...] * mask[...].astype(jnp.float32)
    rate_out[...] = rate

    def packed(last):
        total = jnp.zeros((ROWS, COLS), jnp.float32)

        def put(total, x, at, width):
            shift = at - (COLS - width) if last else at
            return jnp.where((lane >= at) & (lane < at + width), roll(x, shift, 1), total)

        for level in range(LEV):
            total = put(total, state[level], 4 * level, 4)
        for level in range(LEV - 1):
            total = put(total, mix[level], AT_MIX + 2 * level, 2)
        for part in range(2):
            total = put(total, vel[part], AT_VEL + 2 * part, 2)
        total = put(total, rate, AT_RATE, 2)
        for j in range(4):
            total = put(total, weight[j], AT_WEIGHT + 2 * j, 2)
            total = put(total, index[j].astype(jnp.float32), AT_INDEX + 2 * j, 2)
        return total

    first, last = packed(False), packed(True)
    msg0[0:ROWS] = jnp.where(odd, first, last)
    msg1[0:ROWS] = jnp.where(odd, last, first)

    @pl.when(is_atmosphere)
    def _():
        flux = rate * (regrid_tile(prev[0], index, weight) - state[0])
        flux_out[...] = flux
        msg0[ROWS:] = flux
        msg1[ROWS:] = flux

    @pl.when(jnp.logical_not(is_atmosphere))
    def _():
        nothing = jnp.zeros((ROWS, COLS), jnp.float32)
        flux_out[...] = nothing
        msg0[ROWS:] = nothing
        msg1[ROWS:] = nothing


def column_messages(got0, got1):
    odd = lax.rem(lax.axis_index("lon"), 2)
    near = got0[1 - odd]
    far = got1[...]
    return jnp.where(odd == 1, near, far), jnp.where(odd == 1, far, near)


def pack_rows_kernel(
    state, mix, vel, rate_in, index, weight, flux, got0, got1, msg0, msg1
):
    odd = lax.rem(lax.axis_index("lat"), 2) == 1
    west, east = column_messages(got0, got1)
    rate = rate_in[...]

    def put(x, at, width):
        head, tail = x[0:width], x[ROWS - width : ROWS]
        msg0[at : at + width] = jnp.where(odd, head, tail)
        msg1[at : at + width] = jnp.where(odd, tail, head)

    for level in range(LEV):
        put(state[level], 4 * level, 4)
    for level in range(LEV - 1):
        put(mix[level], AT_MIX + 2 * level, 2)
    for part in range(2):
        put(vel[part], AT_VEL + 2 * part, 2)
    put(rate, AT_RATE, 2)
    for j in range(4):
        put(weight[j], AT_WEIGHT + 2 * j, 2)
        put(index[j].astype(jnp.float32), AT_INDEX + 2 * j, 2)
    put(west[0:ROWS], AT_WEST, 4)
    put(east[0:ROWS], AT_EAST, 4)
    for at in (AT_RATE + 2, AT_RATE + 4):
        msg0[at : at + 2] = jnp.zeros((2, COLS), jnp.float32)
        msg1[at : at + 2] = jnp.zeros((2, COLS), jnp.float32)
    msg0[AT_FLUX:] = flux[...]
    msg1[AT_FLUX:] = flux[...]


def row_messages(got0, got1):
    odd = lax.rem(lax.axis_index("lat"), 2)
    near = got0[1 - odd]
    far = got1[...]
    return jnp.where(odd == 1, near, far), jnp.where(odd == 1, far, near)


def east_shift(tile, side, shift, lane):
    rows = side.shape[0]
    moved, moved_side = roll(tile, shift, 1), roll(side, shift, 1)
    cut = lane < shift if shift > 0 else lane >= COLS + shift
    own = jnp.where(cut, moved_side[: tile.shape[0]], moved)
    return own, jnp.where(cut[:rows], moved[:rows], moved_side)


def transport_weights(east, north):
    def weights(v):
        near, far = v * (8.0 / 12.0), v * (1.0 / 12.0)
        return (-far, smoothing + near, smoothing - near, far)

    return weights(east), weights(north)


def horizontal(own, side, own_weights, side_weights, own_rows):
    shifts = (2, 1, -1, -2)
    result = own[:own_rows] * (1.0 - 4.0 * smoothing)
    for shift, factor in zip(shifts, own_weights[1]):
        result = result + factor * roll(own, shift, 0)[:own_rows]
    lane = lanes(own_rows)
    side_result = None
    if side_weights is not None:
        side_result = side[:ROWS] * (1.0 - 4.0 * smoothing)
        for shift, factor in zip(shifts, side_weights[1]):
            side_result = side_result + factor * roll(side, shift, 0)[:ROWS]
    for k, shift in enumerate(shifts):
        moved, moved_side = roll(own[:own_rows], shift, 1), roll(side[:own_rows], shift, 1)
        cut = lane < shift if shift > 0 else lane >= COLS + shift
        result = result + own_weights[0][k] * jnp.where(cut, moved_side, moved)
        if side_weights is not None:
            there = jnp.where(cut[:ROWS], moved[:ROWS], moved_side[:ROWS])
            side_result = side_result + side_weights[0][k] * there
    return result, side_result


def factors(mix):
    inverses, ratios = [], []
    for level in range(LEV):
        pivot = 1.0
        if level < LEV - 1:
            pivot = pivot + mix[level]
        if level > 0:
            pivot = pivot + mix[level - 1] * (1.0 - ratios[-1])
        inverse = 1.0 / pivot
        inverses.append(inverse)
        if level < LEV - 1:
            ratios.append(mix[level] * inverse)
    return inverses, ratios


def solve(rhs, mix, inverses, ratios):
    values = []
    for level in range(LEV):
        source = rhs[level]
        if level > 0:
            source = mix[level - 1] * values[-1] if source is None else source + mix[level - 1] * values[-1]
        values.append(source * inverses[level])
    result = [None] * LEV
    result[-1] = values[-1]
    for level in range(LEV - 2, -1, -1):
        result[level] = values[level] + ratios[level] * result[level + 1]
    return result


def first_step_kernel(
    state, prev, mix, vel, rate_in, index, weight, flux, col0, col1, row0, row1,
    before, before_side, unit, unit_side, inverse_out, fluxes,
):
    is_atmosphere = lax.axis_index("comp") == 0
    west, east = column_messages(col0, col1)
    north, south = row_messages(row0, row1)
    at_lat = lax.axis_index("lat")
    sub = sublanes()
    valid = ((sub < 4) & (at_lat < lax.axis_size("lat") - 1)) | ((sub >= 4) & (at_lat > 0))

    def rim4(level):
        block, odd = 8 * (level // 2), level % 2
        a, b = south[block : block + 8], north[block : block + 8]
        return jnp.where(sub < 4, roll(a, -4 * odd, 0), roll(b, 4 - 4 * odd, 0))

    def rim2(at):
        block, offset = 8 * (at // 8), at % 8
        a, b = south[block : block + 8], north[block : block + 8]
        a, b = roll(a, -offset, 0), roll(b, 6 - offset, 0)
        return jnp.where(sub < 2, a, jnp.where(sub >= 6, b, 0.0))

    def cornered(packed, at):
        a, b = south[AT_WEST : AT_WEST + 8], north[AT_WEST : AT_WEST + 8]
        if at == AT_WEST:
            rim = jnp.where(sub < 4, a, roll(b, 4, 0))
        else:
            rim = jnp.where(sub < 4, roll(a, 4, 0), b)
        return jnp.concatenate([packed[0:ROWS], rim], axis=0)

    west_tile, east_tile = cornered(west, AT_WEST), cornered(east, AT_EAST)
    wide = lanes(24)

    def side(at, width, rows):
        a, b = roll(east_tile[:rows], -at, 1), roll(west_tile[:rows], COLS - width - at, 1)
        lane = wide[:rows]
        return jnp.where(lane < width, a, jnp.where(lane >= COLS - width, b, 0.0))

    def extended(x, rim):
        return jnp.concatenate([x, rim], axis=0)

    own_mix = [extended(mix[level], rim2(AT_MIX + 2 * level)) for level in range(LEV - 1)]
    side_mix = [side(AT_MIX + 2 * level, 2, ROWS) for level in range(LEV - 1)]
    own_vel = [extended(vel[part], rim2(AT_VEL + 2 * part)) for part in range(2)]
    side_vel = [side(AT_VEL + 2 * part, 2, ROWS) for part in range(2)]
    own_weights, side_weights = transport_weights(*own_vel), transport_weights(*side_vel)

    moved, moved_side = [], []
    for level in range(LEV):
        own = extended(state[level], rim4(level))
        a, b = horizontal(own, side(4 * level, 4, 24), own_weights, side_weights, 24)
        moved.append(a)
        moved_side.append(b)
    inverses, ratios = factors(own_mix)
    solved = solve(moved, own_mix, inverses, ratios)
    impulse = solve([1.0] + [None] * (LEV - 1), own_mix, inverses, ratios)
    rate = rate_in[...]

    fluxes[0:ROWS] = flux[...]
    fluxes[ROWS : 2 * ROWS] = west[ROWS:]
    fluxes[2 * ROWS : 3 * ROWS] = east[ROWS:]
    fluxes[3 * ROWS : 4 * ROWS] = north[AT_FLUX:]
    fluxes[4 * ROWS : 5 * ROWS] = south[AT_FLUX:]

    @pl.when(is_atmosphere)
    def _():
        top = solved[0][:ROWS] + flux[...] * impulse[0][:ROWS]
        fluxes[5 * ROWS :] = rate * (regrid_tile(prev[1], index, weight) - top)

    @pl.when(jnp.logical_not(is_atmosphere))
    def _():
        fluxes[5 * ROWS :] = jnp.zeros((ROWS, COLS), jnp.float32)

    for level in range(LEV):
        for out, values in ((before, solved), (unit, impulse)):
            out[level, 0:ROWS] = values[level][:ROWS]
            out[level, ROWS:] = jnp.where(valid, values[level][ROWS:], 0.0)
        inverse_out[level] = inverses[level][:ROWS]
    inverses, ratios = factors(side_mix)
    solved = solve(moved_side, side_mix, inverses, ratios)
    impulse = solve([1.0] + [None] * (LEV - 1), side_mix, inverses, ratios)
    for level in range(LEV):
        before_side[level] = solved[level]
        unit_side[level] = impulse[level]


def second_step_kernel(
    mix, vel, rate_in, index, weight, col0, col1, row0, row1,
    before, before_side, unit, unit_side, inverse, fluxes, new_state, series, force, force_side, force1,
):
    is_atmosphere = lax.axis_index("comp") == 0
    sub = sublanes()
    lane = lanes(ROWS)
    tables = [fluxes[0, k * ROWS : (k + 1) * ROWS] for k in range(6)]

    @pl.when(is_atmosphere)
    def _():
        force[0:ROWS] = tables[0]
        force[ROWS:] = jnp.where(sub < 4, tables[4][0:8], tables[3][8:16])
        force_side[...] = jnp.where(lane < 64, tables[2], tables[1])
        force1[...] = tables[5]

    @pl.when(jnp.logical_not(is_atmosphere))
    def _():
        rate = rate_in[...]
        force[0:ROWS] = rate * regrid_tile(tables[0], index, weight)
        force1[...] = rate * regrid_tile(tables[5], index, weight)
        west, east = column_messages(col0, col1)
        north, south = row_messages(row0, row1)

        def of_rows(message, table, place):
            index8 = message[AT_INDEX : AT_INDEX + 8].astype(jnp.int32)
            total = gather_cells(table, index8) * message[AT_WEIGHT : AT_WEIGHT + 8]
            total = total + roll(total, 4, 0)
            total = total + roll(total, 2, 0)
            block, offset = 8 * (AT_RATE // 8), AT_RATE % 8
            return roll(message[block : block + 8], place - offset, 0) * roll(total, place, 0)

        force[ROWS:] = jnp.where(sub < 4, of_rows(south, tables[4], 0), of_rows(north, tables[3], 6))

        def of_columns(message, table, place):
            tile = message[0:ROWS]
            total = roll(gather_cells(table, tile.astype(jnp.int32)), AT_WEIGHT - AT_INDEX, 1) * tile
            total = total + roll(total, -4, 1)
            total = total + roll(total, -2, 1)
            return roll(tile, place - AT_RATE, 1) * roll(total, place - AT_WEIGHT, 1)

        force_side[...] = jnp.where(
            lane < 64, of_columns(east, tables[2], 0), of_columns(west, tables[1], COLS - 2)
        )

    own_weights = transport_weights(vel[0], vel[1])
    f, f_side = force[...], force_side[...]
    moved = []
    for level in range(LEV):
        own = before[level] + f * unit[level]
        there = before_side[level] + f_side * unit_side[level]
        if level == 0:
            top = own[:ROWS]
        moved.append(horizontal(own, there, own_weights, None, ROWS)[0])
    moved[0] = moved[0] + force1[...]
    own_mix = [mix[level] for level in range(LEV - 1)]
    inverses = [inverse[level] for level in range(LEV)]
    ratios = [own_mix[level] * inverses[level] for level in range(LEV - 1)]
    solved = solve(moved, own_mix, inverses, ratios)
    for level in range(LEV):
        new_state[level] = solved[level]
    series[0] = jnp.where(is_atmosphere, tables[0], top)
    series[1] = jnp.where(is_atmosphere, tables[5], solved[0])


def call(kernel, name, shapes, *args, scratch=(), place=pltpu.VMEM):
    return pl.pallas_call(
        kernel,
        name=name,
        out_shape=[s if hasattr(s, "dtype") else jax.ShapeDtypeStruct(s, jnp.float32) for s in shapes],
        in_specs=[pl.BlockSpec(memory_space=place)] * len(args),
        out_specs=[pl.BlockSpec(memory_space=pltpu.VMEM)] * len(shapes),
        scratch_shapes=list(scratch),
        compiler_params=pltpu.CompilerParams(vmem_limit_bytes=16 * 1024 * 1024),
        interpret=INTERPRET,
    )(*args)


def pairs(count, start, wrap):
    found = []
    for i in range(start, count, 2):
        j = i + 1
        if j < count or wrap:
            found += [(i, j % count), (j % count, i)]
    return found


def partners(count):
    return [[i, i + 1] for i in range(0, count, 2)]


def per_device(
    state, prev_surface, mixing, velocity, coupling, sea_mask, interp_index, interp_weight
):
    n_lat, n_lon = lax.axis_size("lat"), lax.axis_size("lon")
    given = (
        state[0], prev_surface, mixing[0], velocity[0],
        coupling[0], sea_mask[0], interp_index[0], interp_weight[0],
    )
    state, prev, mix, vel, couple, mask, index, weight = given
    tile = (ROWS, COLS)
    column_shape = (COL_MESSAGE, COLS)
    to_near, to_far, flux, rate, state, prev, mix, vel, index, weight = call(
        pack_columns_kernel, "pack_columns",
        [column_shape, column_shape, tile, tile, state, prev, mix, vel, index, weight],
        *given, place=pltpu.HBM,
        scratch=[pltpu.VMEM(tile, couple.dtype), pltpu.VMEM(tile, mask.dtype), pltpu.SemaphoreType.DMA((8,))],
    )
    col1 = lax.ppermute(to_far, "lon", pairs(n_lon, 1, True))
    col0 = lax.all_gather(to_near, "lon", axis_index_groups=partners(n_lon))
    row_shape = (ROW_MESSAGE, COLS)
    to_near, to_far = call(
        pack_rows_kernel, "pack_rows", [row_shape, row_shape],
        state, mix, vel, rate, index, weight, flux, col0, col1,
    )
    row1 = lax.ppermute(to_far, "lat", pairs(n_lat, 1, False))
    row0 = lax.all_gather(to_near, "lat", axis_index_groups=partners(n_lat))
    wide, narrow = (LEV, 24, COLS), (LEV, ROWS, COLS)
    *parts, fluxes = call(
        first_step_kernel, "first_step",
        [wide, narrow, wide, narrow, narrow, (6 * ROWS, COLS)],
        state, prev, mix, vel, rate, index, weight, flux, col0, col1, row0, row1,
    )
    fluxes = lax.all_gather(fluxes, "comp")
    new_state, series = call(
        second_step_kernel, "second_step", [(LEV, ROWS, COLS), (NSTEP, ROWS, COLS)],
        mix, vel, rate, index, weight, col0, col1, row0, row1, *parts, fluxes,
        scratch=[pltpu.VMEM(shape, jnp.float32) for shape in ((24, COLS), tile, tile)],
    )
    return new_state[None], series[None]


def solution(mesh):
    in_specs = (
        P("comp", None, "lat", "lon"),
        P(None, "lat", "lon"),
        P("comp", None, "lat", "lon"),
        P("comp", None, "lat", "lon"),
        P("comp", "lat", "lon"),
        P("comp", "lat", "lon"),
        P("comp", None, "lat", "lon"),
        P("comp", None, "lat", "lon"),
    )
    out_specs = (P("comp", None, "lat", "lon"), P("comp", None, "lat", "lon"))
    return jax.shard_map(
        per_device, mesh=mesh, in_specs=in_specs, out_specs=out_specs, check_vma=False
    )
```

```python
import jax
import jax.numpy as jnp
from jax import lax
from jax.experimental import pallas as pl
from jax.experimental.pallas import tpu as pltpu
from jax.sharding import PartitionSpec as P

INTERPRET = False
NSTEP = 2
LEV = 12
ROWS = 16
COLS = 128
smoothing = 0.15

AT_MIX = 4 * LEV
AT_VEL = AT_MIX + 2 * (LEV - 1)
AT_RATE = AT_VEL + 4
AT_WEIGHT = 80
AT_INDEX = 88
AT_WEST = 96
AT_EAST = 100
AT_FLUX = 104
ROW_MESSAGE = AT_FLUX + ROWS
COL_MESSAGE = 2 * ROWS


def lanes(rows):
    return lax.broadcasted_iota(jnp.int32, (rows, COLS), 1)


def sublanes():
    return lax.broadcasted_iota(jnp.int32, (8, COLS), 0)


def roll(x, shift, axis):
    shift %= x.shape[axis]
    return pltpu.roll(x, shift, axis) if shift else x


def gather_cells(table, index):
    sources = [jnp.broadcast_to(table[r : r + 1], (8, COLS)) for r in range(ROWS)]
    blocks = []
    for at in range(0, index.shape[0], 8):
        cell = index[at : at + 8]
        column = lax.bitwise_and(cell, COLS - 1)
        picked = [
            jnp.take_along_axis(source, column, axis=1, mode="promise_in_bounds")
            for source in sources
        ]
        bit = COLS
        while len(picked) > 1:
            chosen = lax.bitwise_and(cell, bit) != 0
            picked = [jnp.where(chosen, b, a) for a, b in zip(picked[::2], picked[1::2])]
            bit *= 2
        blocks.append(picked[0])
    return jnp.concatenate(blocks, axis=0)


def regrid_tile(table, index_ref, weight_ref):
    index = index_ref[...].reshape(4 * ROWS, COLS)
    picked = gather_cells(table, index).reshape(4, ROWS, COLS)
    return jnp.sum(picked * weight_ref[...], axis=0)


def pack_columns_kernel(
    state_hbm, prev_hbm, mix_hbm, vel_hbm, couple_hbm, mask_hbm, index_hbm, weight_hbm,
    msg0, msg1, flux_out, rate_out, state, prev, mix, vel, index, weight, couple, mask, arrived,
):
    moves = [
        pltpu.make_async_copy(source, target, arrived.at[k])
        for k, (source, target) in enumerate(
            (
                (state_hbm, state),
                (mix_hbm, mix),
                (index_hbm, index),
                (weight_hbm, weight),
                (prev_hbm, prev),
                (vel_hbm, vel),
                (couple_hbm, couple),
                (mask_hbm, mask),
            )
        )
    ]
    for move in moves:
        move.start()
    is_atmosphere = lax.axis_index("comp") == 0
    odd = lax.rem(lax.axis_index("lon"), 2) == 1
    lane = lanes(ROWS)
    for move in moves:
        move.wait()
    rate = couple[...] * mask[...].astype(jnp.float32)
    rate_out[...] = rate

    def packed(last):
        total = jnp.zeros((ROWS, COLS), jnp.float32)

        def put(total, x, at, width):
            shift = at - (COLS - width) if last else at
            return jnp.where((lane >= at) & (lane < at + width), roll(x, shift, 1), total)

        for level in range(LEV):
            total = put(total, state[level], 4 * level, 4)
        for level in range(LEV - 1):
            total = put(total, mix[level], AT_MIX + 2 * level, 2)
        for part in range(2):
            total = put(total, vel[part], AT_VEL + 2 * part, 2)
        total = put(total, rate, AT_RATE, 2)
        for j in range(4):
            total = put(total, weight[j], AT_WEIGHT + 2 * j, 2)
            total = put(total, index[j].astype(jnp.float32), AT_INDEX + 2 * j, 2)
        return total

    first, last = packed(False), packed(True)
    msg0[0:ROWS] = jnp.where(odd, first, last)
    msg1[0:ROWS] = jnp.where(odd, last, first)

    @pl.when(is_atmosphere)
    def _():
        flux = rate * (regrid_tile(prev[0], index, weight) - state[0])
        flux_out[...] = flux
        msg0[ROWS:] = flux
        msg1[ROWS:] = flux

    @pl.when(jnp.logical_not(is_atmosphere))
    def _():
        nothing = jnp.zeros((ROWS, COLS), jnp.float32)
        flux_out[...] = nothing
        msg0[ROWS:] = nothing
        msg1[ROWS:] = nothing


def column_messages(got0, got1):
    odd = lax.rem(lax.axis_index("lon"), 2)
    near = got0[1 - odd]
    far = got1[...]
    return jnp.where(odd == 1, near, far), jnp.where(odd == 1, far, near)


def pack_rows_kernel(
    state, mix, vel, rate_in, index, weight, flux, got0, got1, msg0, msg1
):
    odd = lax.rem(lax.axis_index("lat"), 2) == 1
    west, east = column_messages(got0, got1)
    rate = rate_in[...]

    def put(x, at, width):
        head, tail = x[0:width], x[ROWS - width : ROWS]
        msg0[at : at + width] = jnp.where(odd, head, tail)
        msg1[at : at + width] = jnp.where(odd, tail, head)

    for level in range(LEV):
        put(state[level], 4 * level, 4)
    for level in range(LEV - 1):
        put(mix[level], AT_MIX + 2 * level, 2)
    for part in range(2):
        put(vel[part], AT_VEL + 2 * part, 2)
    put(rate, AT_RATE, 2)
    for j in range(4):
        put(weight[j], AT_WEIGHT + 2 * j, 2)
        put(index[j].astype(jnp.float32), AT_INDEX + 2 * j, 2)
    put(west[0:ROWS], AT_WEST, 4)
    put(east[0:ROWS], AT_EAST, 4)
    for at in (AT_RATE + 2, AT_RATE + 4):
        msg0[at : at + 2] = jnp.zeros((2, COLS), jnp.float32)
        msg1[at : at + 2] = jnp.zeros((2, COLS), jnp.float32)
    msg0[AT_FLUX:] = flux[...]
    msg1[AT_FLUX:] = flux[...]


def row_messages(got0, got1):
    odd = lax.rem(lax.axis_index("lat"), 2)
    near = got0[1 - odd]
    far = got1[...]
    return jnp.where(odd == 1, near, far), jnp.where(odd == 1, far, near)


def east_shift(tile, side, shift, lane):
    rows = side.shape[0]
    moved, moved_side = roll(tile, shift, 1), roll(side, shift, 1)
    cut = lane < shift if shift > 0 else lane >= COLS + shift
    own = jnp.where(cut, moved_side[: tile.shape[0]], moved)
    return own, jnp.where(cut[:rows], moved[:rows], moved_side)


def transport_weights(east, north):
    def weights(v):
        near, far = v * (8.0 / 12.0), v * (1.0 / 12.0)
        return (-far, smoothing + near, smoothing - near, far)

    return weights(east), weights(north)


def horizontal(own, side, own_weights, side_weights, own_rows):
    shifts = (2, 1, -1, -2)
    result = own[:own_rows] * (1.0 - 4.0 * smoothing)
    for shift, factor in zip(shifts, own_weights[1]):
        result = result + factor * roll(own, shift, 0)[:own_rows]
    lane = lanes(own_rows)
    side_result = None
    if side_weights is not None:
        side_result = side[:ROWS] * (1.0 - 4.0 * smoothing)
        for shift, factor in zip(shifts, side_weights[1]):
            side_result = side_result + factor * roll(side, shift, 0)[:ROWS]
    for k, shift in enumerate(shifts):
        moved, moved_side = roll(own[:own_rows], shift, 1), roll(side[:own_rows], shift, 1)
        cut = lane < shift if shift > 0 else lane >= COLS + shift
        result = result + own_weights[0][k] * jnp.where(cut, moved_side, moved)
        if side_weights is not None:
            there = jnp.where(cut[:ROWS], moved[:ROWS], moved_side[:ROWS])
            side_result = side_result + side_weights[0][k] * there
    return result, side_result


def factors(mix):
    inverses, ratios = [], []
    for level in range(LEV):
        pivot = 1.0
        if level < LEV - 1:
            pivot = pivot + mix[level]
        if level > 0:
            pivot = pivot + mix[level - 1] * (1.0 - ratios[-1])
        inverse = 1.0 / pivot
        inverses.append(inverse)
        if level < LEV - 1:
            ratios.append(mix[level] * inverse)
    return inverses, ratios


def solve(rhs, mix, inverses, ratios):
    values = []
    for level in range(LEV):
        source = rhs[level]
        if level > 0:
            source = mix[level - 1] * values[-1] if source is None else source + mix[level - 1] * values[-1]
        values.append(source * inverses[level])
    result = [None] * LEV
    result[-1] = values[-1]
    for level in range(LEV - 2, -1, -1):
        result[level] = values[level] + ratios[level] * result[level + 1]
    return result


def first_step_kernel(
    state, prev, mix, vel, rate_in, index, weight, flux, col0, col1, row0, row1,
    before, before_side, unit, unit_side, inverse_out, fluxes,
):
    is_atmosphere = lax.axis_index("comp") == 0
    west, east = column_messages(col0, col1)
    north, south = row_messages(row0, row1)
    at_lat = lax.axis_index("lat")
    sub = sublanes()
    valid = ((sub < 4) & (at_lat < lax.axis_size("lat") - 1)) | ((sub >= 4) & (at_lat > 0))

    def rim4(level):
        block, odd = 8 * (level // 2), level % 2
        a, b = south[block : block + 8], north[block : block + 8]
        return jnp.where(sub < 4, roll(a, -4 * odd, 0), roll(b, 4 - 4 * odd, 0))

    def rim2(at):
        block, offset = 8 * (at // 8), at % 8
        a, b = south[block : block + 8], north[block : block + 8]
        a, b = roll(a, -offset, 0), roll(b, 6 - offset, 0)
        return jnp.where(sub < 2, a, jnp.where(sub >= 6, b, 0.0))

    def cornered(packed, at):
        a, b = south[AT_WEST : AT_WEST + 8], north[AT_WEST : AT_WEST + 8]
        if at == AT_WEST:
            rim = jnp.where(sub < 4, a, roll(b, 4, 0))
        else:
            rim = jnp.where(sub < 4, roll(a, 4, 0), b)
        return jnp.concatenate([packed[0:ROWS], rim], axis=0)

    west_tile, east_tile = cornered(west, AT_WEST), cornered(east, AT_EAST)
    wide = lanes(24)

    def side(at, width, rows):
        a, b = roll(east_tile[:rows], -at, 1), roll(west_tile[:rows], COLS - width - at, 1)
        lane = wide[:rows]
        return jnp.where(lane < width, a, jnp.where(lane >= COLS - width, b, 0.0))

    def extended(x, rim):
        return jnp.concatenate([x, rim], axis=0)

    own_mix = [extended(mix[level], rim2(AT_MIX + 2 * level)) for level in range(LEV - 1)]
    side_mix = [side(AT_MIX + 2 * level, 2, ROWS) for level in range(LEV - 1)]
    own_vel = [extended(vel[part], rim2(AT_VEL + 2 * part)) for part in range(2)]
    side_vel = [side(AT_VEL + 2 * part, 2, ROWS) for part in range(2)]
    own_weights, side_weights = transport_weights(*own_vel), transport_weights(*side_vel)

    moved, moved_side = [], []
    for level in range(LEV):
        own = extended(state[level], rim4(level))
        a, b = horizontal(own, side(4 * level, 4, 24), own_weights, side_weights, 24)
        moved.append(a)
        moved_side.append(b)
    inverses, ratios = factors(own_mix)
    solved = solve(moved, own_mix, inverses, ratios)
    impulse = solve([1.0] + [None] * (LEV - 1), own_mix, inverses, ratios)
    rate = rate_in[...]

    fluxes[0:ROWS] = flux[...]
    fluxes[ROWS : 2 * ROWS] = west[ROWS:]
    fluxes[2 * ROWS : 3 * ROWS] = east[ROWS:]
    fluxes[3 * ROWS : 4 * ROWS] = north[AT_FLUX:]
    fluxes[4 * ROWS : 5 * ROWS] = south[AT_FLUX:]

    @pl.when(is_atmosphere)
    def _():
        top = solved[0][:ROWS] + flux[...] * impulse[0][:ROWS]
        fluxes[5 * ROWS :] = rate * (regrid_tile(prev[1], index, weight) - top)

    @pl.when(jnp.logical_not(is_atmosphere))
    def _():
        fluxes[5 * ROWS :] = jnp.zeros((ROWS, COLS), jnp.float32)

    for level in range(LEV):
        for out, values in ((before, solved), (unit, impulse)):
            out[level, 0:ROWS] = values[level][:ROWS]
            out[level, ROWS:] = jnp.where(valid, values[level][ROWS:], 0.0)
        inverse_out[level] = inverses[level][:ROWS]
    inverses, ratios = factors(side_mix)
    solved = solve(moved_side, side_mix, inverses, ratios)
    impulse = solve([1.0] + [None] * (LEV - 1), side_mix, inverses, ratios)
    for level in range(LEV):
        before_side[level] = solved[level]
        unit_side[level] = impulse[level]


def second_step_kernel(
    mix, vel, rate_in, index, weight, col0, col1, row0, row1,
    before, before_side, unit, unit_side, inverse, fluxes, new_state, series, force, force_side, force1,
):
    is_atmosphere = lax.axis_index("comp") == 0
    sub = sublanes()
    lane = lanes(ROWS)
    tables = [fluxes[0, k * ROWS : (k + 1) * ROWS] for k in range(6)]

    @pl.when(is_atmosphere)
    def _():
        force[0:ROWS] = tables[0]
        force[ROWS:] = jnp.where(sub < 4, tables[4][0:8], tables[3][8:16])
        force_side[...] = jnp.where(lane < 64, tables[2], tables[1])
        force1[...] = tables[5]

    @pl.when(jnp.logical_not(is_atmosphere))
    def _():
        rate = rate_in[...]
        force[0:ROWS] = rate * regrid_tile(tables[0], index, weight)
        force1[...] = rate * regrid_tile(tables[5], index, weight)
        west, east = column_messages(col0, col1)
        north, south = row_messages(row0, row1)

        def of_rows(message, table, place):
            index8 = message[AT_INDEX : AT_INDEX + 8].astype(jnp.int32)
            total = gather_cells(table, index8) * message[AT_WEIGHT : AT_WEIGHT + 8]
            total = total + roll(total, 4, 0)
            total = total + roll(total, 2, 0)
            block, offset = 8 * (AT_RATE // 8), AT_RATE % 8
            return roll(message[block : block + 8], place - offset, 0) * roll(total, place, 0)

        force[ROWS:] = jnp.where(sub < 4, of_rows(south, tables[4], 0), of_rows(north, tables[3], 6))

        def of_columns(message, table, place):
            tile = message[0:ROWS]
            total = roll(gather_cells(table, tile.astype(jnp.int32)), AT_WEIGHT - AT_INDEX, 1) * tile
            total = total + roll(total, -4, 1)
            total = total + roll(total, -2, 1)
            return roll(tile, place - AT_RATE, 1) * roll(total, place - AT_WEIGHT, 1)

        force_side[...] = jnp.where(
            lane < 64, of_columns(east, tables[2], 0), of_columns(west, tables[1], COLS - 2)
        )

    own_weights = transport_weights(vel[0], vel[1])
    f, f_side = force[...], force_side[...]
    moved = []
    for level in range(LEV):
        own = before[level] + f * unit[level]
        there = before_side[level] + f_side * unit_side[level]
        if level == 0:
            top = own[:ROWS]
        moved.append(horizontal(own, there, own_weights, None, ROWS)[0])
    moved[0] = moved[0] + force1[...]
    own_mix = [mix[level] for level in range(LEV - 1)]
    inverses = [inverse[level] for level in range(LEV)]
    ratios = [own_mix[level] * inverses[level] for level in range(LEV - 1)]
    solved = solve(moved, own_mix, inverses, ratios)
    for level in range(LEV):
        new_state[level] = solved[level]
    series[0] = jnp.where(is_atmosphere, tables[0], top)
    series[1] = jnp.where(is_atmosphere, tables[5], solved[0])


def call(kernel, name, shapes, *args, scratch=(), place=pltpu.VMEM):
    return pl.pallas_call(
        kernel,
        name=name,
        out_shape=[s if hasattr(s, "dtype") else jax.ShapeDtypeStruct(s, jnp.float32) for s in shapes],
        in_specs=[pl.BlockSpec(memory_space=place)] * len(args),
        out_specs=[pl.BlockSpec(memory_space=pltpu.VMEM)] * len(shapes),
        scratch_shapes=list(scratch),
        compiler_params=pltpu.CompilerParams(vmem_limit_bytes=16 * 1024 * 1024),
        interpret=INTERPRET,
    )(*args)


def pairs(count, start, wrap):
    found = []
    for i in range(start, count, 2):
        j = i + 1
        if j < count or wrap:
            found += [(i, j % count), (j % count, i)]
    return found


def partners(count):
    return [[i, i + 1] for i in range(0, count, 2)]


def per_device(
    state, prev_surface, mixing, velocity, coupling, sea_mask, interp_index, interp_weight
):
    n_lat, n_lon = lax.axis_size("lat"), lax.axis_size("lon")
    given = (
        state[0], prev_surface, mixing[0], velocity[0],
        coupling[0], sea_mask[0], interp_index[0], interp_weight[0],
    )
    state, prev, mix, vel, couple, mask, index, weight = given
    tile = (ROWS, COLS)
    column_shape = (COL_MESSAGE, COLS)
    to_near, to_far, flux, rate, state, prev, mix, vel, index, weight = call(
        pack_columns_kernel, "pack_columns",
        [column_shape, column_shape, tile, tile, state, prev, mix, vel, index, weight],
        *(pltpu.with_memory_space_constraint(x, pltpu.HBM) for x in given), place=pltpu.HBM,
        scratch=[pltpu.VMEM(tile, couple.dtype), pltpu.VMEM(tile, mask.dtype), pltpu.SemaphoreType.DMA((8,))],
    )
    col1 = lax.ppermute(to_far, "lon", pairs(n_lon, 1, True))
    col0 = lax.all_gather(to_near, "lon", axis_index_groups=partners(n_lon))
    row_shape = (ROW_MESSAGE, COLS)
    to_near, to_far = call(
        pack_rows_kernel, "pack_rows", [row_shape, row_shape],
        state, mix, vel, rate, index, weight, flux, col0, col1,
    )
    row1 = lax.ppermute(to_far, "lat", pairs(n_lat, 1, False))
    row0 = lax.all_gather(to_near, "lat", axis_index_groups=partners(n_lat))
    wide, narrow = (LEV, 24, COLS), (LEV, ROWS, COLS)
    *parts, fluxes = call(
        first_step_kernel, "first_step",
        [wide, narrow, wide, narrow, narrow, (6 * ROWS, COLS)],
        state, prev, mix, vel, rate, index, weight, flux, col0, col1, row0, row1,
    )
    fluxes = lax.all_gather(fluxes, "comp")
    new_state, series = call(
        second_step_kernel, "second_step", [(LEV, ROWS, COLS), (NSTEP, ROWS, COLS)],
        mix, vel, rate, index, weight, col0, col1, row0, row1, *parts, fluxes,
        scratch=[pltpu.VMEM(shape, jnp.float32) for shape in ((24, COLS), tile, tile)],
    )
    return new_state[None], series[None]


def solution(mesh):
    in_specs = (
        P("comp", None, "lat", "lon"),
        P(None, "lat", "lon"),
        P("comp", None, "lat", "lon"),
        P("comp", None, "lat", "lon"),
        P("comp", "lat", "lon"),
        P("comp", "lat", "lon"),
        P("comp", None, "lat", "lon"),
        P("comp", None, "lat", "lon"),
    )
    out_specs = (P("comp", None, "lat", "lon"), P("comp", None, "lat", "lon"))
    return jax.shard_map(
        per_device, mesh=mesh, in_specs=in_specs, out_specs=out_specs, check_vma=False
    )
```

```python
import jax
import jax.numpy as jnp
from jax import lax
from jax.experimental import pallas as pl
from jax.experimental.pallas import tpu as pltpu
from jax.sharding import PartitionSpec as P


INTERPRET = False
NSTEP = 2
LEV = 12
ROWS = 16
COLS = 128
smoothing = 0.15

AT_MIX = 4 * LEV
AT_VEL = AT_MIX + 2 * (LEV - 1)
AT_RATE = AT_VEL + 4
AT_WEIGHT = 80
AT_INDEX = 88
AT_WEST = 96
AT_EAST = 100
AT_FLUX = 104
ROW_MESSAGE = AT_FLUX + ROWS
COL_MESSAGE = 2 * ROWS


def lanes(rows):
    return lax.broadcasted_iota(jnp.int32, (rows, COLS), 1)


def sublanes():
    return lax.broadcasted_iota(jnp.int32, (8, COLS), 0)


def roll(x, shift, axis):
    shift %= x.shape[axis]
    return pltpu.roll(x, shift, axis) if shift else x


def gather_cells(table, index):
    sources = [jnp.broadcast_to(table[r : r + 1], (8, COLS)) for r in range(ROWS)]
    blocks = []
    for at in range(0, index.shape[0], 8):
        cell = index[at : at + 8]
        column = lax.bitwise_and(cell, COLS - 1)
        picked = [
            jnp.take_along_axis(source, column, axis=1, mode="promise_in_bounds")
            for source in sources
        ]
        bit = COLS
        while len(picked) > 1:
            chosen = lax.bitwise_and(cell, bit) != 0
            picked = [jnp.where(chosen, b, a) for a, b in zip(picked[::2], picked[1::2])]
            bit *= 2
        blocks.append(picked[0])
    return jnp.concatenate(blocks, axis=0)


def regrid_tile(table, index_ref, weight_ref):
    index = index_ref[...].reshape(4 * ROWS, COLS)
    picked = gather_cells(table, index).reshape(4, ROWS, COLS)
    return jnp.sum(picked * weight_ref[...], axis=0)


def pack_columns_kernel(
    state_hbm, prev_hbm, mix_hbm, vel_hbm, couple_hbm, mask_hbm, index_hbm, weight_hbm,
    msg0, msg1, flux_out, rate_out, state, prev, mix, vel, index, weight, couple, mask, arrived,
):
    moves = [
        pltpu.make_async_copy(source, target, arrived.at[k])
        for k, (source, target) in enumerate(
            (
                (state_hbm, state),
                (mix_hbm, mix),
                (index_hbm, index),
                (weight_hbm, weight),
                (prev_hbm, prev),
                (vel_hbm, vel),
                (couple_hbm, couple),
                (mask_hbm, mask),
            )
        )
    ]
    for move in moves:
        move.start()
    is_atmosphere = lax.axis_index("comp") == 0
    odd = lax.rem(lax.axis_index("lon"), 2) == 1
    lane = lanes(ROWS)
    for move in moves:
        move.wait()
    rate = couple[...] * mask[...].astype(jnp.float32)
    rate_out[...] = rate

    def packed(last):
        total = jnp.zeros((ROWS, COLS), jnp.float32)

        def put(total, x, at, width):
            shift = at - (COLS - width) if last else at
            return jnp.where((lane >= at) & (lane < at + width), roll(x, shift, 1), total)

        for level in range(LEV):
            total = put(total, state[level], 4 * level, 4)
        for level in range(LEV - 1):
            total = put(total, mix[level], AT_MIX + 2 * level, 2)
        for part in range(2):
            total = put(total, vel[part], AT_VEL + 2 * part, 2)
        total = put(total, rate, AT_RATE, 2)
        for j in range(4):
            total = put(total, weight[j], AT_WEIGHT + 2 * j, 2)
            total = put(total, index[j].astype(jnp.float32), AT_INDEX + 2 * j, 2)
        return total

    first, last = packed(False), packed(True)
    msg0[0:ROWS] = jnp.where(odd, first, last)
    msg1[0:ROWS] = jnp.where(odd, last, first)

    @pl.when(is_atmosphere)
    def _():
        flux = rate * (regrid_tile(prev[0], index, weight) - state[0])
        flux_out[...] = flux
        msg0[ROWS:] = flux
        msg1[ROWS:] = flux

    @pl.when(jnp.logical_not(is_atmosphere))
    def _():
        nothing = jnp.zeros((ROWS, COLS), jnp.float32)
        flux_out[...] = nothing
        msg0[ROWS:] = nothing
        msg1[ROWS:] = nothing


def column_messages(got0, got1):
    at_lon = lax.axis_index("lon")
    odd = lax.rem(at_lon, 2) == 1
    near = jnp.where(lax.rem(at_lon, 4) < 2, got0[0][...], got0[1][...])
    far = got1[...]
    return jnp.where(odd, near, far), jnp.where(odd, far, near)


def pack_rows_kernel(
    state, mix, vel, rate_in, index, weight, flux, got0a, got0b, got1, msg0, msg1
):
    odd = lax.rem(lax.axis_index("lat"), 2) == 1
    west, east = column_messages((got0a, got0b), got1)
    rate = rate_in[...]

    def put(x, at, width):
        head, tail = x[0:width], x[ROWS - width : ROWS]
        msg0[at : at + width] = jnp.where(odd, head, tail)
        msg1[at : at + width] = jnp.where(odd, tail, head)

    for level in range(LEV):
        put(state[level], 4 * level, 4)
    for level in range(LEV - 1):
        put(mix[level], AT_MIX + 2 * level, 2)
    for part in range(2):
        put(vel[part], AT_VEL + 2 * part, 2)
    put(rate, AT_RATE, 2)
    for j in range(4):
        put(weight[j], AT_WEIGHT + 2 * j, 2)
        put(index[j].astype(jnp.float32), AT_INDEX + 2 * j, 2)
    put(west[0:ROWS], AT_WEST, 4)
    put(east[0:ROWS], AT_EAST, 4)
    for at in (AT_RATE + 2, AT_RATE + 4):
        msg0[at : at + 2] = jnp.zeros((2, COLS), jnp.float32)
        msg1[at : at + 2] = jnp.zeros((2, COLS), jnp.float32)
    msg0[AT_FLUX:] = flux[...]
    msg1[AT_FLUX:] = flux[...]


def row_messages(got0, got1):
    odd = lax.rem(lax.axis_index("lat"), 2)
    near = got0[1 - odd]
    far = got1[...]
    return jnp.where(odd == 1, near, far), jnp.where(odd == 1, far, near)


def transport_weights(east, north):
    def weights(v):
        near, far = v * (8.0 / 12.0), v * (1.0 / 12.0)
        return (-far, smoothing + near, smoothing - near, far)

    return weights(east), weights(north)


def horizontal(own, side, own_weights, side_weights, own_rows):
    shifts = (2, 1, -1, -2)
    result = own[:own_rows] * (1.0 - 4.0 * smoothing)
    for shift, factor in zip(shifts, own_weights[1]):
        result = result + factor * roll(own, shift, 0)[:own_rows]
    lane = lanes(own_rows)
    side_result = None
    if side_weights is not None:
        side_result = side[:ROWS] * (1.0 - 4.0 * smoothing)
        for shift, factor in zip(shifts, side_weights[1]):
            side_result = side_result + factor * roll(side, shift, 0)[:ROWS]
    for k, shift in enumerate(shifts):
        moved, moved_side = roll(own[:own_rows], shift, 1), roll(side[:own_rows], shift, 1)
        cut = lane < shift if shift > 0 else lane >= COLS + shift
        result = result + own_weights[0][k] * jnp.where(cut, moved_side, moved)
        if side_weights is not None:
            there = jnp.where(cut[:ROWS], moved[:ROWS], moved_side[:ROWS])
            side_result = side_result + side_weights[0][k] * there
    return result, side_result


def factors(mix):
    inverses, ratios = [], []
    for level in range(LEV):
        pivot = 1.0
        if level < LEV - 1:
            pivot = pivot + mix[level]
        if level > 0:
            pivot = pivot + mix[level - 1] * (1.0 - ratios[-1])
        inverse = 1.0 / pivot
        inverses.append(inverse)
        if level < LEV - 1:
            ratios.append(mix[level] * inverse)
    return inverses, ratios


def solve(rhs, mix, inverses, ratios):
    values = []
    for level in range(LEV):
        source = rhs[level]
        if level > 0:
            source = mix[level - 1] * values[-1] if source is None else source + mix[level - 1] * values[-1]
        values.append(source * inverses[level])
    result = [None] * LEV
    result[-1] = values[-1]
    for level in range(LEV - 2, -1, -1):
        result[level] = values[level] + ratios[level] * result[level + 1]
    return result


def first_step_kernel(
    state, prev, mix, vel, rate_in, index, weight, flux, col0a, col0b, col1, row0, row1,
    before, before_side, unit, unit_side, inverse_out, fluxes,
):
    is_atmosphere = lax.axis_index("comp") == 0
    west, east = column_messages((col0a, col0b), col1)
    north, south = row_messages(row0, row1)
    at_lat = lax.axis_index("lat")
    sub = sublanes()
    valid = ((sub < 4) & (at_lat < lax.axis_size("lat") - 1)) | ((sub >= 4) & (at_lat > 0))

    def rim4(level):
        block, odd = 8 * (level // 2), level % 2
        a, b = south[block : block + 8], north[block : block + 8]
        return jnp.where(sub < 4, roll(a, -4 * odd, 0), roll(b, 4 - 4 * odd, 0))

    def rim2(at):
        block, offset = 8 * (at // 8), at % 8
        a, b = south[block : block + 8], north[block : block + 8]
        a, b = roll(a, -offset, 0), roll(b, 6 - offset, 0)
        return jnp.where(sub < 2, a, jnp.where(sub >= 6, b, 0.0))

    def cornered(packed, at):
        a, b = south[AT_WEST : AT_WEST + 8], north[AT_WEST : AT_WEST + 8]
        if at == AT_WEST:
            rim = jnp.where(sub < 4, a, roll(b, 4, 0))
        else:
            rim = jnp.where(sub < 4, roll(a, 4, 0), b)
        return jnp.concatenate([packed[0:ROWS], rim], axis=0)

    west_tile, east_tile = cornered(west, AT_WEST), cornered(east, AT_EAST)
    wide = lanes(24)

    def side(at, width, rows):
        a, b = roll(east_tile[:rows], -at, 1), roll(west_tile[:rows], COLS - width - at, 1)
        lane = wide[:rows]
        return jnp.where(lane < width, a, jnp.where(lane >= COLS - width, b, 0.0))

    def extended(x, rim):
        return jnp.concatenate([x, rim], axis=0)

    own_mix = [extended(mix[level], rim2(AT_MIX + 2 * level)) for level in range(LEV - 1)]
    side_mix = [side(AT_MIX + 2 * level, 2, ROWS) for level in range(LEV - 1)]
    own_vel = [extended(vel[part], rim2(AT_VEL + 2 * part)) for part in range(2)]
    side_vel = [side(AT_VEL + 2 * part, 2, ROWS) for part in range(2)]
    own_weights, side_weights = transport_weights(*own_vel), transport_weights(*side_vel)

    moved, moved_side = [], []
    for level in range(LEV):
        own = extended(state[level], rim4(level))
        a, b = horizontal(own, side(4 * level, 4, 24), own_weights, side_weights, 24)
        moved.append(a)
        moved_side.append(b)
    inverses, ratios = factors(own_mix)
    solved = solve(moved, own_mix, inverses, ratios)
    impulse = solve([1.0] + [None] * (LEV - 1), own_mix, inverses, ratios)
    rate = rate_in[...]

    fluxes[0:ROWS] = flux[...]
    fluxes[ROWS : 2 * ROWS] = west[ROWS:]
    fluxes[2 * ROWS : 3 * ROWS] = east[ROWS:]
    fluxes[3 * ROWS : 4 * ROWS] = north[AT_FLUX:]
    fluxes[4 * ROWS : 5 * ROWS] = south[AT_FLUX:]

    @pl.when(is_atmosphere)
    def _():
        top = solved[0][:ROWS] + flux[...] * impulse[0][:ROWS]
        fluxes[5 * ROWS :] = rate * (regrid_tile(prev[1], index, weight) - top)

    @pl.when(jnp.logical_not(is_atmosphere))
    def _():
        fluxes[5 * ROWS :] = jnp.zeros((ROWS, COLS), jnp.float32)

    for level in range(LEV):
        for out, values in ((before, solved), (unit, impulse)):
            out[level, 0:ROWS] = values[level][:ROWS]
            out[level, ROWS:] = jnp.where(valid, values[level][ROWS:], 0.0)
        inverse_out[level] = inverses[level][:ROWS]
    inverses, ratios = factors(side_mix)
    solved = solve(moved_side, side_mix, inverses, ratios)
    impulse = solve([1.0] + [None] * (LEV - 1), side_mix, inverses, ratios)
    for level in range(LEV):
        before_side[level] = solved[level]
        unit_side[level] = impulse[level]


def second_step_kernel(
    mix, vel, rate_in, index, weight, col0a, col0b, col1, row0, row1,
    before, before_side, unit, unit_side, inverse, fluxes, new_state, series, force, force_side, force1,
):
    is_atmosphere = lax.axis_index("comp") == 0
    sub = sublanes()
    lane = lanes(ROWS)
    tables = [fluxes[0, k * ROWS : (k + 1) * ROWS] for k in range(6)]

    @pl.when(is_atmosphere)
    def _():
        force[0:ROWS] = tables[0]
        force[ROWS:] = jnp.where(sub < 4, tables[4][0:8], tables[3][8:16])
        force_side[...] = jnp.where(lane < 64, tables[2], tables[1])
        force1[...] = tables[5]

    @pl.when(jnp.logical_not(is_atmosphere))
    def _():
        rate = rate_in[...]
        force[0:ROWS] = rate * regrid_tile(tables[0], index, weight)
        force1[...] = rate * regrid_tile(tables[5], index, weight)
        west, east = column_messages((col0a, col0b), col1)
        north, south = row_messages(row0, row1)

        def of_rows(message, table, place):
            index8 = message[AT_INDEX : AT_INDEX + 8].astype(jnp.int32)
            total = gather_cells(table, index8) * message[AT_WEIGHT : AT_WEIGHT + 8]
            total = total + roll(total, 4, 0)
            total = total + roll(total, 2, 0)
            block, offset = 8 * (AT_RATE // 8), AT_RATE % 8
            return roll(message[block : block + 8], place - offset, 0) * roll(total, place, 0)

        force[ROWS:] = jnp.where(sub < 4, of_rows(south, tables[4], 0), of_rows(north, tables[3], 6))

        def of_columns(message, table, place):
            tile = message[0:ROWS]
            total = roll(gather_cells(table, tile.astype(jnp.int32)), AT_WEIGHT - AT_INDEX, 1) * tile
            total = total + roll(total, -4, 1)
            total = total + roll(total, -2, 1)
            return roll(tile, place - AT_RATE, 1) * roll(total, place - AT_WEIGHT, 1)

        force_side[...] = jnp.where(
            lane < 64, of_columns(east, tables[2], 0), of_columns(west, tables[1], COLS - 2)
        )

    own_weights = transport_weights(vel[0], vel[1])
    f, f_side = force[...], force_side[...]
    moved = []
    for level in range(LEV):
        own = before[level] + f * unit[level]
        there = before_side[level] + f_side * unit_side[level]
        if level == 0:
            top = own[:ROWS]
        moved.append(horizontal(own, there, own_weights, None, ROWS)[0])
    moved[0] = moved[0] + force1[...]
    own_mix = [mix[level] for level in range(LEV - 1)]
    inverses = [inverse[level] for level in range(LEV)]
    ratios = [own_mix[level] * inverses[level] for level in range(LEV - 1)]
    solved = solve(moved, own_mix, inverses, ratios)
    for level in range(LEV):
        new_state[level] = solved[level]
    series[0] = jnp.where(is_atmosphere, tables[0], top)
    series[1] = jnp.where(is_atmosphere, tables[5], solved[0])


def call(kernel, shapes, *args, scratch=(), place=pltpu.VMEM):
    return pl.pallas_call(
        kernel,
        out_shape=[s if hasattr(s, "dtype") else jax.ShapeDtypeStruct(s, jnp.float32) for s in shapes],
        in_specs=[pl.BlockSpec(memory_space=place)] * len(args),
        out_specs=[pl.BlockSpec(memory_space=pltpu.VMEM)] * len(shapes),
        scratch_shapes=list(scratch),
        compiler_params=pltpu.CompilerParams(vmem_limit_bytes=16 * 1024 * 1024),
        interpret=INTERPRET,
    )(*args)


def pairs(count, start, wrap, step=2):
    found = []
    for i in range(start, count, step):
        j = i + 1
        if j < count or wrap:
            found += [(i, j % count), (j % count, i)]
    return found


def partners(count):
    return [[i, i + 1] for i in range(0, count, 2)]


def per_device(
    state, prev_surface, mixing, velocity, coupling, sea_mask, interp_index, interp_weight
):
    n_lat, n_lon = lax.axis_size("lat"), lax.axis_size("lon")
    given = (
        state[0], prev_surface, mixing[0], velocity[0],
        coupling[0], sea_mask[0], interp_index[0], interp_weight[0],
    )
    state, prev, mix, vel, couple, mask, index, weight = given
    tile = (ROWS, COLS)
    column_shape = (COL_MESSAGE, COLS)
    to_near, to_far, flux, rate, state, prev, mix, vel, index, weight = call(
        pack_columns_kernel,
        [column_shape, column_shape, tile, tile, state, prev, mix, vel, index, weight],
        *(pltpu.with_memory_space_constraint(x, pltpu.HBM) for x in given), place=pltpu.HBM,
        scratch=[pltpu.VMEM(tile, couple.dtype), pltpu.VMEM(tile, mask.dtype), pltpu.SemaphoreType.DMA((8,))],
    )
    early = lax.ppermute(to_near, "lon", pairs(n_lon, 0, True, 4))
    col1 = lax.ppermute(to_far, "lon", pairs(n_lon, 1, True))
    late = lax.ppermute(to_near, "lon", pairs(n_lon, 2, True, 4))
    col0 = (early, late)
    row_shape = (ROW_MESSAGE, COLS)
    to_near, to_far = call(
        pack_rows_kernel, [row_shape, row_shape],
        state, mix, vel, rate, index, weight, flux, *col0, col1,
    )
    row1 = lax.ppermute(to_far, "lat", pairs(n_lat, 1, False))
    row0 = lax.all_gather(to_near, "lat", axis_index_groups=partners(n_lat))
    wide, narrow = (LEV, 24, COLS), (LEV, ROWS, COLS)
    *parts, fluxes = call(
        first_step_kernel,
        [wide, narrow, wide, narrow, narrow, (6 * ROWS, COLS)],
        state, prev, mix, vel, rate, index, weight, flux, *col0, col1, row0, row1,
    )
    fluxes = lax.all_gather(fluxes, "comp")
    new_state, series = call(
        second_step_kernel, [(LEV, ROWS, COLS), (NSTEP, ROWS, COLS)],
        mix, vel, rate, index, weight, *col0, col1, row0, row1, *parts, fluxes,
        scratch=[pltpu.VMEM(shape, jnp.float32) for shape in ((24, COLS), tile, tile)],
    )
    return new_state[None], series[None]


def solution(mesh):
    in_specs = (
        P("comp", None, "lat", "lon"),
        P(None, "lat", "lon"),
        P("comp", None, "lat", "lon"),
        P("comp", None, "lat", "lon"),
        P("comp", "lat", "lon"),
        P("comp", "lat", "lon"),
        P("comp", None, "lat", "lon"),
        P("comp", None, "lat", "lon"),
    )
    out_specs = (P("comp", None, "lat", "lon"), P("comp", None, "lat", "lon"))

    return jax.shard_map(
        per_device, mesh=mesh, in_specs=in_specs, out_specs=out_specs, check_vma=False
    )
```

```python
import jax
import jax.numpy as jnp
from jax import lax
from jax.experimental import pallas as pl
from jax.experimental.pallas import tpu as pltpu
from jax.sharding import PartitionSpec as P


INTERPRET = False
NSTEP = 2
LEV = 12
ROWS = 16
COLS = 128
smoothing = 0.15

AT_MIX = 4 * LEV
AT_VEL = AT_MIX + 2 * (LEV - 1)
AT_RATE = AT_VEL + 4
AT_WEIGHT = 80
AT_INDEX = 88
AT_FLUX = AT_WEIGHT
AT_WEST = 96
AT_EAST = 100
ROW_MESSAGE = 104
COL_MESSAGE = 2 * ROWS


def lanes(rows):
    return lax.broadcasted_iota(jnp.int32, (rows, COLS), 1)


def sublanes():
    return lax.broadcasted_iota(jnp.int32, (8, COLS), 0)


def roll(x, shift, axis):
    shift %= x.shape[axis]
    return pltpu.roll(x, shift, axis) if shift else x


def gather_cells(table, index):
    sources = [jnp.broadcast_to(table[r : r + 1], (8, COLS)) for r in range(ROWS)]
    blocks = []
    for at in range(0, index.shape[0], 8):
        cell = index[at : at + 8]
        column = lax.bitwise_and(cell, COLS - 1)
        picked = [
            jnp.take_along_axis(source, column, axis=1, mode="promise_in_bounds")
            for source in sources
        ]
        bit = COLS
        while len(picked) > 1:
            chosen = lax.bitwise_and(cell, bit) != 0
            picked = [jnp.where(chosen, b, a) for a, b in zip(picked[::2], picked[1::2])]
            bit *= 2
        blocks.append(picked[0])
    return jnp.concatenate(blocks, axis=0)


def regrid_tile(table, index_ref, weight_ref):
    index = index_ref[...].reshape(4 * ROWS, COLS)
    picked = gather_cells(table, index).reshape(4, ROWS, COLS)
    return jnp.sum(picked * weight_ref[...], axis=0)


def pack_columns_kernel(
    state_hbm, prev_hbm, mix_hbm, vel_hbm, couple_hbm, mask_hbm, index_hbm, weight_hbm,
    msg0, msg1, flux_out, rate_out, state, prev, mix, vel, index, weight, couple, mask, arrived,
):
    moves = [
        pltpu.make_async_copy(source, target, arrived.at[k])
        for k, (source, target) in enumerate(
            (
                (state_hbm, state),
                (mix_hbm, mix),
                (index_hbm, index),
                (weight_hbm, weight),
                (prev_hbm, prev),
                (vel_hbm, vel),
                (couple_hbm, couple),
                (mask_hbm, mask),
            )
        )
    ]
    for move in moves:
        move.start()
    is_atmosphere = lax.axis_index("comp") == 0
    odd = lax.rem(lax.axis_index("lon"), 2) == 1
    lane = lanes(ROWS)
    for move in moves:
        move.wait()
    rate = couple[...] * mask[...].astype(jnp.float32)
    rate_out[...] = rate

    def packed(last):
        total = jnp.zeros((ROWS, COLS), jnp.float32)

        def put(total, x, at, width):
            shift = at - (COLS - width) if last else at
            return jnp.where((lane >= at) & (lane < at + width), roll(x, shift, 1), total)

        for level in range(LEV):
            total = put(total, state[level], 4 * level, 4)
        for level in range(LEV - 1):
            total = put(total, mix[level], AT_MIX + 2 * level, 2)
        for part in range(2):
            total = put(total, vel[part], AT_VEL + 2 * part, 2)
        total = put(total, rate, AT_RATE, 2)
        for j in range(4):
            total = put(total, weight[j], AT_WEIGHT + 2 * j, 2)
            total = put(total, index[j].astype(jnp.float32), AT_INDEX + 2 * j, 2)
        return total

    first, last = packed(False), packed(True)
    msg0[0:ROWS] = jnp.where(odd, first, last)
    msg1[0:ROWS] = jnp.where(odd, last, first)

    @pl.when(is_atmosphere)
    def _():
        flux = rate * (regrid_tile(prev[0], index, weight) - state[0])
        flux_out[...] = flux
        msg0[ROWS:] = flux
        msg1[ROWS:] = flux

    @pl.when(jnp.logical_not(is_atmosphere))
    def _():
        nothing = jnp.zeros((ROWS, COLS), jnp.float32)
        flux_out[...] = nothing
        msg0[ROWS:] = nothing
        msg1[ROWS:] = nothing


def column_messages(got):
    at_lon = lax.axis_index("lon")
    odd = lax.rem(at_lon, 2) == 1
    starts_early = lax.rem(at_lon, 4) < 2
    near = jnp.where(starts_early, got[0][...], got[1][...])
    far = jnp.where(starts_early, got[2][...], got[3][...])
    return jnp.where(odd, near, far), jnp.where(odd, far, near)


def pack_rows_kernel(
    state, mix, vel, rate_in, index, weight, flux, early, late, to_early, to_late, msg0, msg1
):
    odd = lax.rem(lax.axis_index("lat"), 2) == 1
    west, east = column_messages((early, late, to_early, to_late))
    rate = rate_in[...]

    def put(x, at, width):
        head, tail = x[0:width], x[ROWS - width : ROWS]
        msg0[at : at + width] = jnp.where(odd, head, tail)
        msg1[at : at + width] = jnp.where(odd, tail, head)

    for level in range(LEV):
        put(state[level], 4 * level, 4)
    for level in range(LEV - 1):
        put(mix[level], AT_MIX + 2 * level, 2)
    for part in range(2):
        put(vel[part], AT_VEL + 2 * part, 2)
    put(rate, AT_RATE, 2)

    @pl.when(lax.axis_index("comp") == 0)
    def _():
        msg0[AT_FLUX : AT_FLUX + ROWS] = flux[...]
        msg1[AT_FLUX : AT_FLUX + ROWS] = flux[...]

    @pl.when(lax.axis_index("comp") != 0)
    def _():
        for j in range(4):
            put(weight[j], AT_WEIGHT + 2 * j, 2)
            put(index[j].astype(jnp.float32), AT_INDEX + 2 * j, 2)

    put(west[0:ROWS], AT_WEST, 4)
    put(east[0:ROWS], AT_EAST, 4)
    for at in (AT_RATE + 2, AT_RATE + 4):
        msg0[at : at + 2] = jnp.zeros((2, COLS), jnp.float32)
        msg1[at : at + 2] = jnp.zeros((2, COLS), jnp.float32)


def row_messages(got0, got1):
    odd = lax.rem(lax.axis_index("lat"), 2)
    near = got0[1 - odd]
    far = got1[...]
    return jnp.where(odd == 1, near, far), jnp.where(odd == 1, far, near)


def transport_weights(east, north):
    def weights(v):
        near, far = v * (8.0 / 12.0), v * (1.0 / 12.0)
        return (-far, smoothing + near, smoothing - near, far)

    return weights(east), weights(north)


def horizontal(own, side, own_weights, side_weights, own_rows):
    shifts = (2, 1, -1, -2)
    result = own[:own_rows] * (1.0 - 4.0 * smoothing)
    for shift, factor in zip(shifts, own_weights[1]):
        result = result + factor * roll(own, shift, 0)[:own_rows]
    lane = lanes(own_rows)
    side_result = None
    if side_weights is not None:
        side_result = side[:ROWS] * (1.0 - 4.0 * smoothing)
        for shift, factor in zip(shifts, side_weights[1]):
            side_result = side_result + factor * roll(side, shift, 0)[:ROWS]
    for k, shift in enumerate(shifts):
        moved, moved_side = roll(own[:own_rows], shift, 1), roll(side[:own_rows], shift, 1)
        cut = lane < shift if shift > 0 else lane >= COLS + shift
        result = result + own_weights[0][k] * jnp.where(cut, moved_side, moved)
        if side_weights is not None:
            there = jnp.where(cut[:ROWS], moved[:ROWS], moved_side[:ROWS])
            side_result = side_result + side_weights[0][k] * there
    return result, side_result


def factors(mix):
    inverses, ratios = [], []
    for level in range(LEV):
        pivot = 1.0
        if level < LEV - 1:
            pivot = pivot + mix[level]
        if level > 0:
            pivot = pivot + mix[level - 1] * (1.0 - ratios[-1])
        inverse = 1.0 / pivot
        inverses.append(inverse)
        if level < LEV - 1:
            ratios.append(mix[level] * inverse)
    return inverses, ratios


def solve(rhs, mix, inverses, ratios):
    values = []
    for level in range(LEV):
        source = rhs[level]
        if level > 0:
            source = mix[level - 1] * values[-1] if source is None else source + mix[level - 1] * values[-1]
        values.append(source * inverses[level])
    result = [None] * LEV
    result[-1] = values[-1]
    for level in range(LEV - 2, -1, -1):
        result[level] = values[level] + ratios[level] * result[level + 1]
    return result


def rim_of_levels(north, south, level):
    sub, block, odd = sublanes(), 8 * (level // 2), level % 2
    a, b = south[block : block + 8], north[block : block + 8]
    return jnp.where(sub < 4, roll(a, -4 * odd, 0), roll(b, 4 - 4 * odd, 0))


def side_of(west_tile, east_tile, at, width, rows):
    lane = lanes(rows)
    a, b = roll(east_tile[:rows], -at, 1), roll(west_tile[:rows], COLS - width - at, 1)
    return jnp.where(lane < width, a, jnp.where(lane >= COLS - width, b, 0.0))


def prepare_kernel(prev, mix, index, weight, inverse_out, unit_top, seen):
    inverses, ratios = factors([mix[level] for level in range(LEV - 1)])
    for level in range(LEV):
        inverse_out[level] = inverses[level]
    own_mix = [mix[level] for level in range(LEV - 1)]
    unit_top[...] = solve([1.0] + [None] * (LEV - 1), own_mix, inverses, ratios)[0]

    @pl.when(lax.axis_index("comp") == 0)
    def _():
        seen[...] = regrid_tile(prev[1], index, weight)


def top_kernel(
    state, mix, vel, rate, flux, early, late, to_early, to_late, row0, row1, inverse, unit_top, seen,
    fluxes,
):
    @pl.when(lax.axis_index("comp") == 0)
    def _():
        west, east = column_messages((early, late, to_early, to_late))
        north, south = row_messages(row0, row1)
        weights = transport_weights(vel[0], vel[1])
        moved = []
        for level in range(LEV):
            own = jnp.concatenate([state[level], rim_of_levels(north, south, level)], axis=0)
            there = side_of(west[0:ROWS], east[0:ROWS], 4 * level, 4, ROWS)
            moved.append(horizontal(own, there, weights, None, ROWS)[0])
        own_mix = [mix[level] for level in range(LEV - 1)]
        inverses = [inverse[level] for level in range(LEV)]
        ratios = [own_mix[level] * inverses[level] for level in range(LEV - 1)]
        top = solve(moved, own_mix, inverses, ratios)[0] + flux[...] * unit_top[...]
        fluxes[0:ROWS] = flux[...]
        fluxes[ROWS : 2 * ROWS] = west[ROWS:]
        fluxes[2 * ROWS : 3 * ROWS] = east[ROWS:]
        fluxes[3 * ROWS : 4 * ROWS] = north[AT_FLUX : AT_FLUX + ROWS]
        fluxes[4 * ROWS : 5 * ROWS] = south[AT_FLUX : AT_FLUX + ROWS]
        fluxes[5 * ROWS :] = rate[...] * (seen[...] - top)


def first_step_kernel(
    state, mix, vel, early, late, to_early, to_late, row0, row1, before, before_side, unit, unit_side,
):
    west, east = column_messages((early, late, to_early, to_late))
    north, south = row_messages(row0, row1)
    at_lat = lax.axis_index("lat")
    sub = sublanes()
    valid = ((sub < 4) & (at_lat < lax.axis_size("lat") - 1)) | ((sub >= 4) & (at_lat > 0))

    def rim2(at):
        block, offset = 8 * (at // 8), at % 8
        a, b = south[block : block + 8], north[block : block + 8]
        a, b = roll(a, -offset, 0), roll(b, 6 - offset, 0)
        return jnp.where(sub < 2, a, jnp.where(sub >= 6, b, 0.0))

    def cornered(packed, at):
        a, b = south[AT_WEST : AT_WEST + 8], north[AT_WEST : AT_WEST + 8]
        if at == AT_WEST:
            rim = jnp.where(sub < 4, a, roll(b, 4, 0))
        else:
            rim = jnp.where(sub < 4, roll(a, 4, 0), b)
        return jnp.concatenate([packed[0:ROWS], rim], axis=0)

    west_tile, east_tile = cornered(west, AT_WEST), cornered(east, AT_EAST)

    def side(at, width, rows):
        return side_of(west_tile, east_tile, at, width, rows)

    def extended(x, rim):
        return jnp.concatenate([x, rim], axis=0)

    own_mix = [extended(mix[level], rim2(AT_MIX + 2 * level)) for level in range(LEV - 1)]
    side_mix = [side(AT_MIX + 2 * level, 2, ROWS) for level in range(LEV - 1)]
    own_vel = [extended(vel[part], rim2(AT_VEL + 2 * part)) for part in range(2)]
    side_vel = [side(AT_VEL + 2 * part, 2, ROWS) for part in range(2)]
    own_weights, side_weights = transport_weights(*own_vel), transport_weights(*side_vel)

    moved, moved_side = [], []
    for level in range(LEV):
        own = extended(state[level], rim_of_levels(north, south, level))
        a, b = horizontal(own, side(4 * level, 4, 24), own_weights, side_weights, 24)
        moved.append(a)
        moved_side.append(b)
    inverses, ratios = factors(own_mix)
    solved = solve(moved, own_mix, inverses, ratios)
    impulse = solve([1.0] + [None] * (LEV - 1), own_mix, inverses, ratios)
    for level in range(LEV):
        for out, values in ((before, solved), (unit, impulse)):
            out[level, 0:ROWS] = values[level][:ROWS]
            out[level, ROWS:] = jnp.where(valid, values[level][ROWS:], 0.0)
    inverses, ratios = factors(side_mix)
    solved = solve(moved_side, side_mix, inverses, ratios)
    impulse = solve([1.0] + [None] * (LEV - 1), side_mix, inverses, ratios)
    for level in range(LEV):
        before_side[level] = solved[level]
        unit_side[level] = impulse[level]


def second_step_kernel(
    mix, vel, rate_in, index, weight, early, late, to_early, to_late, row0, row1,
    before, before_side, unit, unit_side, inverse, sent, got, new_state, series, force, force_side, force1,
):
    is_atmosphere = lax.axis_index("comp") == 0
    sub = sublanes()
    lane = lanes(ROWS)

    @pl.when(is_atmosphere)
    def _():
        tables = [sent[k * ROWS : (k + 1) * ROWS] for k in range(6)]
        force[0:ROWS] = tables[0]
        force[ROWS:] = jnp.where(sub < 4, tables[4][0:8], tables[3][8:16])
        force_side[...] = jnp.where(lane < 64, tables[2], tables[1])
        force1[...] = tables[5]

    @pl.when(jnp.logical_not(is_atmosphere))
    def _():
        tables = [got[k * ROWS : (k + 1) * ROWS] for k in range(6)]
        rate = rate_in[...]
        force[0:ROWS] = rate * regrid_tile(tables[0], index, weight)
        force1[...] = rate * regrid_tile(tables[5], index, weight)
        west, east = column_messages((early, late, to_early, to_late))
        north, south = row_messages(row0, row1)

        def of_rows(message, table, place):
            index8 = message[AT_INDEX : AT_INDEX + 8].astype(jnp.int32)
            total = gather_cells(table, index8) * message[AT_WEIGHT : AT_WEIGHT + 8]
            total = total + roll(total, 4, 0)
            total = total + roll(total, 2, 0)
            block, offset = 8 * (AT_RATE // 8), AT_RATE % 8
            return roll(message[block : block + 8], place - offset, 0) * roll(total, place, 0)

        force[ROWS:] = jnp.where(sub < 4, of_rows(south, tables[4], 0), of_rows(north, tables[3], 6))

        def of_columns(message, table, place):
            tile = message[0:ROWS]
            total = roll(gather_cells(table, tile.astype(jnp.int32)), AT_WEIGHT - AT_INDEX, 1) * tile
            total = total + roll(total, -4, 1)
            total = total + roll(total, -2, 1)
            return roll(tile, place - AT_RATE, 1) * roll(total, place - AT_WEIGHT, 1)

        force_side[...] = jnp.where(
            lane < 64, of_columns(east, tables[2], 0), of_columns(west, tables[1], COLS - 2)
        )

    own_weights = transport_weights(vel[0], vel[1])
    f, f_side = force[...], force_side[...]
    moved = []
    for level in range(LEV):
        own = before[level] + f * unit[level]
        there = before_side[level] + f_side * unit_side[level]
        if level == 0:
            top = own[:ROWS]
        moved.append(horizontal(own, there, own_weights, None, ROWS)[0])
    moved[0] = moved[0] + force1[...]
    own_mix = [mix[level] for level in range(LEV - 1)]
    inverses = [inverse[level] for level in range(LEV)]
    ratios = [own_mix[level] * inverses[level] for level in range(LEV - 1)]
    solved = solve(moved, own_mix, inverses, ratios)
    for level in range(LEV):
        new_state[level] = solved[level]
    series[0] = jnp.where(is_atmosphere, f[:ROWS], top)
    series[1] = jnp.where(is_atmosphere, force1[...], solved[0])


def call(kernel, shapes, *args, scratch=(), place=pltpu.VMEM):
    return pl.pallas_call(
        kernel,
        out_shape=[s if hasattr(s, "dtype") else jax.ShapeDtypeStruct(s, jnp.float32) for s in shapes],
        in_specs=[pl.BlockSpec(memory_space=place)] * len(args),
        out_specs=[pl.BlockSpec(memory_space=pltpu.VMEM)] * len(shapes),
        scratch_shapes=list(scratch),
        compiler_params=pltpu.CompilerParams(vmem_limit_bytes=16 * 1024 * 1024),
        interpret=INTERPRET,
    )(*args)


def pairs(count, start, step):
    return [pair for i in range(start, count - 1, step) for pair in ((i, i + 1), (i + 1, i))]


def partners(count):
    return [[i, i + 1] for i in range(0, count, 2)]


def per_device(
    state, prev_surface, mixing, velocity, coupling, sea_mask, interp_index, interp_weight
):
    n_lat, n_lon = lax.axis_size("lat"), lax.axis_size("lon")
    given = (
        state[0], prev_surface, mixing[0], velocity[0],
        coupling[0], sea_mask[0], interp_index[0], interp_weight[0],
    )
    state, prev, mix, vel, couple, mask, index, weight = given
    tile = (ROWS, COLS)
    column_shape = (COL_MESSAGE, COLS)
    to_near, to_far, flux, rate, state, prev, mix, vel, index, weight = call(
        pack_columns_kernel,
        [column_shape, column_shape, tile, tile, state, prev, mix, vel, index, weight],
        *(pltpu.with_memory_space_constraint(x, pltpu.HBM) for x in given), place=pltpu.HBM,
        scratch=[pltpu.VMEM(tile, couple.dtype), pltpu.VMEM(tile, mask.dtype), pltpu.SemaphoreType.DMA((8,))],
    )
    joints = range(1, n_lon, 2)
    sent = [((i, (i + 1) % n_lon) if i % 4 == 3 else (i + 1, i)) for i in joints]
    to_early = lax.ppermute(to_far, "lon", sent)
    early = lax.ppermute(to_near, "lon", pairs(n_lon, 0, 4))
    to_late = lax.ppermute(to_far, "lon", [(j, i) for i, j in sent])
    late = lax.ppermute(to_near, "lon", pairs(n_lon, 2, 4))
    columns = (early, late, to_early, to_late)
    row_shape = (ROW_MESSAGE, COLS)
    to_near, to_far = call(
        pack_rows_kernel, [row_shape, row_shape],
        state, mix, vel, rate, index, weight, flux, *columns,
    )
    row1 = lax.ppermute(to_far, "lat", pairs(n_lat, 1, 2))
    row0 = lax.all_gather(to_near, "lat", axis_index_groups=partners(n_lat))
    wide, narrow = (LEV, 24, COLS), (LEV, ROWS, COLS)
    inverse, unit_top, seen = call(prepare_kernel, [narrow, tile, tile], prev, mix, index, weight)
    (fluxes,) = call(
        top_kernel, [(6 * ROWS, COLS)],
        state, mix, vel, rate, flux, *columns, row0, row1, inverse, unit_top, seen,
    )
    got = lax.ppermute(fluxes, "comp", [(0, 1)])
    parts = call(
        first_step_kernel, [wide, narrow, wide, narrow],
        state, mix, vel, *columns, row0, row1,
    )
    new_state, series = call(
        second_step_kernel, [(LEV, ROWS, COLS), (NSTEP, ROWS, COLS)],
        mix, vel, rate, index, weight, *columns, row0, row1, *parts, inverse, fluxes, got,
        scratch=[pltpu.VMEM(shape, jnp.float32) for shape in ((24, COLS), tile, tile)],
    )
    return new_state[None], series[None]


def solution(mesh):
    in_specs = (
        P("comp", None, "lat", "lon"),
        P(None, "lat", "lon"),
        P("comp", None, "lat", "lon"),
        P("comp", None, "lat", "lon"),
        P("comp", "lat", "lon"),
        P("comp", "lat", "lon"),
        P("comp", None, "lat", "lon"),
        P("comp", None, "lat", "lon"),
    )
    out_specs = (P("comp", None, "lat", "lon"), P("comp", None, "lat", "lon"))

    return jax.shard_map(
        per_device, mesh=mesh, in_specs=in_specs, out_specs=out_specs, check_vma=False
    )
```

```python
import jax
import jax.numpy as jnp
from jax import lax
from jax.experimental import pallas as pl
from jax.experimental.pallas import tpu as pltpu
from jax.sharding import PartitionSpec as P


INTERPRET = False
NSTEP = 2
LEV = 12
ROWS = 16
COLS = 128
smoothing = 0.15

AT_MIX = 4 * LEV
AT_VEL = AT_MIX + 2 * (LEV - 1)
AT_RATE = AT_VEL + 4
AT_WEIGHT = 80
AT_INDEX = 88
AT_FLUX = AT_WEIGHT
AT_CORNER = 96
ROW_MESSAGE = 104
COL_MESSAGE = 2 * ROWS


def lanes(rows):
    return lax.broadcasted_iota(jnp.int32, (rows, COLS), 1)


def sublanes():
    return lax.broadcasted_iota(jnp.int32, (8, COLS), 0)


def roll(x, shift, axis):
    shift %= x.shape[axis]
    return pltpu.roll(x, shift, axis) if shift else x


def gather_cells(table, index):
    sources = [jnp.broadcast_to(table[r : r + 1], (8, COLS)) for r in range(ROWS)]
    blocks = []
    for at in range(0, index.shape[0], 8):
        cell = index[at : at + 8]
        column = lax.bitwise_and(cell, COLS - 1)
        picked = [
            jnp.take_along_axis(source, column, axis=1, mode="promise_in_bounds")
            for source in sources
        ]
        bit = COLS
        while len(picked) > 1:
            chosen = lax.bitwise_and(cell, bit) != 0
            picked = [jnp.where(chosen, b, a) for a, b in zip(picked[::2], picked[1::2])]
            bit *= 2
        blocks.append(picked[0])
    return jnp.concatenate(blocks, axis=0)


def regrid_tile(table, index_ref, weight_ref):
    index = index_ref[...].reshape(4 * ROWS, COLS)
    picked = gather_cells(table, index).reshape(4, ROWS, COLS)
    return jnp.sum(picked * weight_ref[...], axis=0)


def pack_columns_kernel(
    state_hbm, prev_hbm, mix_hbm, vel_hbm, couple_hbm, mask_hbm, index_hbm, weight_hbm,
    msg0, msg1, flux_out, rate_out, state, prev, mix, vel, index, weight, couple, mask, arrived,
):
    moves = [
        pltpu.make_async_copy(source, target, arrived.at[k])
        for k, (source, target) in enumerate(
            (
                (state_hbm, state),
                (mix_hbm, mix),
                (index_hbm, index),
                (weight_hbm, weight),
                (prev_hbm, prev),
                (vel_hbm, vel),
                (couple_hbm, couple),
                (mask_hbm, mask),
            )
        )
    ]
    for move in moves:
        move.start()
    is_atmosphere = lax.axis_index("comp") == 0
    odd = lax.rem(lax.axis_index("lon"), 2) == 1
    lane = lanes(ROWS)
    for move in moves:
        move.wait()
    rate = couple[...] * mask[...].astype(jnp.float32)
    rate_out[...] = rate

    def packed(last):
        total = jnp.zeros((ROWS, COLS), jnp.float32)

        def put(total, x, at, width):
            shift = at - (COLS - width) if last else at
            return jnp.where((lane >= at) & (lane < at + width), roll(x, shift, 1), total)

        for level in range(LEV):
            total = put(total, state[level], 4 * level, 4)
        for level in range(LEV - 1):
            total = put(total, mix[level], AT_MIX + 2 * level, 2)
        for part in range(2):
            total = put(total, vel[part], AT_VEL + 2 * part, 2)
        total = put(total, rate, AT_RATE, 2)
        for j in range(4):
            total = put(total, weight[j], AT_WEIGHT + 2 * j, 2)
            total = put(total, index[j].astype(jnp.float32), AT_INDEX + 2 * j, 2)
        return total

    first, last = packed(False), packed(True)
    msg0[0:ROWS] = jnp.where(odd, first, last)
    msg1[0:ROWS] = jnp.where(odd, last, first)

    @pl.when(is_atmosphere)
    def _():
        flux = rate * (regrid_tile(prev[0], index, weight) - state[0])
        flux_out[...] = flux
        msg0[ROWS:] = flux
        msg1[ROWS:] = flux

    @pl.when(jnp.logical_not(is_atmosphere))
    def _():
        nothing = jnp.zeros((ROWS, COLS), jnp.float32)
        flux_out[...] = nothing
        msg0[ROWS:] = nothing
        msg1[ROWS:] = nothing


def starts_early():
    return lax.rem(lax.axis_index("lon"), 4) < 2


def sides(near, far):
    odd = lax.rem(lax.axis_index("lon"), 2) == 1
    return jnp.where(odd, near, far), jnp.where(odd, far, near)


def column_messages(got):
    early = starts_early()
    near = jnp.where(early, got[0][...], got[1][...])
    return sides(near, jnp.where(early, got[2][...], got[3][...]))


def pack_rows(state, mix, vel, rate_in, index, weight, flux, near, msg0, msg1):
    odd = lax.rem(lax.axis_index("lat"), 2) == 1
    rate = rate_in[...]

    def put(x, at, width):
        head, tail = x[0:width], x[ROWS - width : ROWS]
        msg0[at : at + width] = jnp.where(odd, head, tail)
        msg1[at : at + width] = jnp.where(odd, tail, head)

    for level in range(LEV):
        put(state[level], 4 * level, 4)
    for level in range(LEV - 1):
        put(mix[level], AT_MIX + 2 * level, 2)
    for part in range(2):
        put(vel[part], AT_VEL + 2 * part, 2)
    put(rate, AT_RATE, 2)

    @pl.when(lax.axis_index("comp") == 0)
    def _():
        msg0[AT_FLUX : AT_FLUX + ROWS] = flux[...]
        msg1[AT_FLUX : AT_FLUX + ROWS] = flux[...]

    @pl.when(lax.axis_index("comp") != 0)
    def _():
        for j in range(4):
            put(weight[j], AT_WEIGHT + 2 * j, 2)
            put(index[j].astype(jnp.float32), AT_INDEX + 2 * j, 2)

    put(near[0:ROWS], AT_CORNER, 4)
    for at in (AT_RATE + 2, AT_RATE + 4, AT_CORNER + 4, AT_CORNER + 6):
        msg0[at : at + 2] = jnp.zeros((2, COLS), jnp.float32)
        msg1[at : at + 2] = jnp.zeros((2, COLS), jnp.float32)


def pack_rows_early_kernel(*refs):
    @pl.when(starts_early())
    def _():
        pack_rows(*refs)


def pack_rows_late_kernel(*refs):
    @pl.when(jnp.logical_not(starts_early()))
    def _():
        pack_rows(*refs)


def pack_corners_kernel(to_early, to_late, msg):
    early = starts_early()
    sub = sublanes()
    head = jnp.where(early, to_early[0:8], to_late[0:8])
    tail = jnp.where(early, to_early[8:ROWS], to_late[8:ROWS])
    msg[...] = jnp.where(sub < 4, head, tail)


def row_messages(got):
    early = starts_early()
    odd = lax.rem(lax.axis_index("lat"), 2) == 1
    near = jnp.where(early, got[0][...], got[1][...])
    far = jnp.where(early, got[2][...], got[3][...])
    return jnp.where(odd, near, far), jnp.where(odd, far, near)


def transport_weights(east, north):
    def weights(v):
        near, far = v * (8.0 / 12.0), v * (1.0 / 12.0)
        return (-far, smoothing + near, smoothing - near, far)

    return weights(east), weights(north)


def horizontal(own, side, own_weights, side_weights, own_rows):
    shifts = (2, 1, -1, -2)
    result = own[:own_rows] * (1.0 - 4.0 * smoothing)
    for shift, factor in zip(shifts, own_weights[1]):
        result = result + factor * roll(own, shift, 0)[:own_rows]
    lane = lanes(own_rows)
    side_result = None
    if side_weights is not None:
        side_result = side[:ROWS] * (1.0 - 4.0 * smoothing)
        for shift, factor in zip(shifts, side_weights[1]):
            side_result = side_result + factor * roll(side, shift, 0)[:ROWS]
    for k, shift in enumerate(shifts):
        moved, moved_side = roll(own[:own_rows], shift, 1), roll(side[:own_rows], shift, 1)
        cut = lane < shift if shift > 0 else lane >= COLS + shift
        result = result + own_weights[0][k] * jnp.where(cut, moved_side, moved)
        if side_weights is not None:
            there = jnp.where(cut[:ROWS], moved[:ROWS], moved_side[:ROWS])
            side_result = side_result + side_weights[0][k] * there
    return result, side_result


def factors(mix):
    inverses, ratios = [], []
    for level in range(LEV):
        pivot = 1.0
        if level < LEV - 1:
            pivot = pivot + mix[level]
        if level > 0:
            pivot = pivot + mix[level - 1] * (1.0 - ratios[-1])
        inverse = 1.0 / pivot
        inverses.append(inverse)
        if level < LEV - 1:
            ratios.append(mix[level] * inverse)
    return inverses, ratios


def solve(rhs, mix, inverses, ratios):
    values = []
    for level in range(LEV):
        source = rhs[level]
        if level > 0:
            source = mix[level - 1] * values[-1] if source is None else source + mix[level - 1] * values[-1]
        values.append(source * inverses[level])
    result = [None] * LEV
    result[-1] = values[-1]
    for level in range(LEV - 2, -1, -1):
        result[level] = values[level] + ratios[level] * result[level + 1]
    return result


def rim_of_levels(north, south, level):
    sub, block, odd = sublanes(), 8 * (level // 2), level % 2
    a, b = south[block : block + 8], north[block : block + 8]
    return jnp.where(sub < 4, roll(a, -4 * odd, 0), roll(b, 4 - 4 * odd, 0))


def side_of(west_tile, east_tile, at, width, rows):
    lane = lanes(rows)
    a, b = roll(east_tile[:rows], -at, 1), roll(west_tile[:rows], COLS - width - at, 1)
    return jnp.where(lane < width, a, jnp.where(lane >= COLS - width, b, 0.0))


def prepare_kernel(prev, mix, index, weight, inverse_out, unit_top, seen):
    inverses, ratios = factors([mix[level] for level in range(LEV - 1)])
    for level in range(LEV):
        inverse_out[level] = inverses[level]
    own_mix = [mix[level] for level in range(LEV - 1)]
    unit_top[...] = solve([1.0] + [None] * (LEV - 1), own_mix, inverses, ratios)[0]

    @pl.when(lax.axis_index("comp") == 0)
    def _():
        seen[...] = regrid_tile(prev[1], index, weight)


def top_kernel(
    state, mix, vel, rate, flux, early, late, to_early, to_late, row0e, row0l, row1e, row1l, inverse, unit_top, seen,
    fluxes,
):
    @pl.when(lax.axis_index("comp") == 0)
    def _():
        west, east = column_messages((early, late, to_early, to_late))
        north, south = row_messages((row0e, row0l, row1e, row1l))
        weights = transport_weights(vel[0], vel[1])
        moved = []
        for level in range(LEV):
            own = jnp.concatenate([state[level], rim_of_levels(north, south, level)], axis=0)
            there = side_of(west[0:ROWS], east[0:ROWS], 4 * level, 4, ROWS)
            moved.append(horizontal(own, there, weights, None, ROWS)[0])
        own_mix = [mix[level] for level in range(LEV - 1)]
        inverses = [inverse[level] for level in range(LEV)]
        ratios = [own_mix[level] * inverses[level] for level in range(LEV - 1)]
        top = solve(moved, own_mix, inverses, ratios)[0] + flux[...] * unit_top[...]
        fluxes[0:ROWS] = flux[...]
        fluxes[ROWS : 2 * ROWS] = west[ROWS:]
        fluxes[2 * ROWS : 3 * ROWS] = east[ROWS:]
        fluxes[3 * ROWS : 4 * ROWS] = north[AT_FLUX : AT_FLUX + ROWS]
        fluxes[4 * ROWS : 5 * ROWS] = south[AT_FLUX : AT_FLUX + ROWS]
        fluxes[5 * ROWS :] = rate[...] * (seen[...] - top)


def first_step_kernel(
    state, mix, vel, early, late, to_early, to_late, row0e, row0l, row1e, row1l, corner0, corner1,
    before, before_side, unit, unit_side,
):
    west, east = column_messages((early, late, to_early, to_late))
    north, south = row_messages((row0e, row0l, row1e, row1l))
    at_lat = lax.axis_index("lat")
    sub = sublanes()
    valid = ((sub < 4) & (at_lat < lax.axis_size("lat") - 1)) | ((sub >= 4) & (at_lat > 0))

    def rim2(at):
        block, offset = 8 * (at // 8), at % 8
        a, b = south[block : block + 8], north[block : block + 8]
        a, b = roll(a, -offset, 0), roll(b, 6 - offset, 0)
        return jnp.where(sub < 2, a, jnp.where(sub >= 6, b, 0.0))

    odd = lax.rem(at_lat, 2) == 1
    near_rim = jnp.where(sub < 4, south[AT_CORNER:], roll(north[AT_CORNER:], 4, 0))
    chip, other = corner0[1 - lax.rem(at_lat, 2)], corner1[...]
    far_rim = jnp.where((sub < 4) == odd, other, chip)
    west_rim, east_rim = sides(near_rim, far_rim)
    west_tile = jnp.concatenate([west[0:ROWS], west_rim], axis=0)
    east_tile = jnp.concatenate([east[0:ROWS], east_rim], axis=0)

    def side(at, width, rows):
        return side_of(west_tile, east_tile, at, width, rows)

    def extended(x, rim):
        return jnp.concatenate([x, rim], axis=0)

    own_mix = [extended(mix[level], rim2(AT_MIX + 2 * level)) for level in range(LEV - 1)]
    side_mix = [side(AT_MIX + 2 * level, 2, ROWS) for level in range(LEV - 1)]
    own_vel = [extended(vel[part], rim2(AT_VEL + 2 * part)) for part in range(2)]
    side_vel = [side(AT_VEL + 2 * part, 2, ROWS) for part in range(2)]
    own_weights, side_weights = transport_weights(*own_vel), transport_weights(*side_vel)

    moved, moved_side = [], []
    for level in range(LEV):
        own = extended(state[level], rim_of_levels(north, south, level))
        a, b = horizontal(own, side(4 * level, 4, 24), own_weights, side_weights, 24)
        moved.append(a)
        moved_side.append(b)
    inverses, ratios = factors(own_mix)
    solved = solve(moved, own_mix, inverses, ratios)
    impulse = solve([1.0] + [None] * (LEV - 1), own_mix, inverses, ratios)
    for level in range(LEV):
        for out, values in ((before, solved), (unit, impulse)):
            out[level, 0:ROWS] = values[level][:ROWS]
            out[level, ROWS:] = jnp.where(valid, values[level][ROWS:], 0.0)
    inverses, ratios = factors(side_mix)
    solved = solve(moved_side, side_mix, inverses, ratios)
    impulse = solve([1.0] + [None] * (LEV - 1), side_mix, inverses, ratios)
    for level in range(LEV):
        before_side[level] = solved[level]
        unit_side[level] = impulse[level]


def second_step_kernel(
    mix, vel, rate_in, index, weight, early, late, to_early, to_late, row0e, row0l, row1e, row1l,
    before, before_side, unit, unit_side, inverse, sent, got, new_state, series, force, force_side, force1,
):
    is_atmosphere = lax.axis_index("comp") == 0
    sub = sublanes()
    lane = lanes(ROWS)

    @pl.when(is_atmosphere)
    def _():
        tables = [sent[k * ROWS : (k + 1) * ROWS] for k in range(6)]
        force[0:ROWS] = tables[0]
        force[ROWS:] = jnp.where(sub < 4, tables[4][0:8], tables[3][8:16])
        force_side[...] = jnp.where(lane < 64, tables[2], tables[1])
        force1[...] = tables[5]

    @pl.when(jnp.logical_not(is_atmosphere))
    def _():
        tables = [got[k * ROWS : (k + 1) * ROWS] for k in range(6)]
        rate = rate_in[...]
        force[0:ROWS] = rate * regrid_tile(tables[0], index, weight)
        force1[...] = rate * regrid_tile(tables[5], index, weight)
        west, east = column_messages((early, late, to_early, to_late))
        north, south = row_messages((row0e, row0l, row1e, row1l))

        def of_rows(message, table, place):
            index8 = message[AT_INDEX : AT_INDEX + 8].astype(jnp.int32)
            total = gather_cells(table, index8) * message[AT_WEIGHT : AT_WEIGHT + 8]
            total = total + roll(total, 4, 0)
            total = total + roll(total, 2, 0)
            block, offset = 8 * (AT_RATE // 8), AT_RATE % 8
            return roll(message[block : block + 8], place - offset, 0) * roll(total, place, 0)

        force[ROWS:] = jnp.where(sub < 4, of_rows(south, tables[4], 0), of_rows(north, tables[3], 6))

        def of_columns(message, table, place):
            tile = message[0:ROWS]
            total = roll(gather_cells(table, tile.astype(jnp.int32)), AT_WEIGHT - AT_INDEX, 1) * tile
            total = total + roll(total, -4, 1)
            total = total + roll(total, -2, 1)
            return roll(tile, place - AT_RATE, 1) * roll(total, place - AT_WEIGHT, 1)

        force_side[...] = jnp.where(
            lane < 64, of_columns(east, tables[2], 0), of_columns(west, tables[1], COLS - 2)
        )

    own_weights = transport_weights(vel[0], vel[1])
    f, f_side = force[...], force_side[...]
    moved = []
    for level in range(LEV):
        own = before[level] + f * unit[level]
        there = before_side[level] + f_side * unit_side[level]
        if level == 0:
            top = own[:ROWS]
        moved.append(horizontal(own, there, own_weights, None, ROWS)[0])
    moved[0] = moved[0] + force1[...]
    own_mix = [mix[level] for level in range(LEV - 1)]
    inverses = [inverse[level] for level in range(LEV)]
    ratios = [own_mix[level] * inverses[level] for level in range(LEV - 1)]
    solved = solve(moved, own_mix, inverses, ratios)
    for level in range(LEV):
        new_state[level] = solved[level]
    series[0] = jnp.where(is_atmosphere, f[:ROWS], top)
    series[1] = jnp.where(is_atmosphere, force1[...], solved[0])


def call(kernel, shapes, *args, scratch=(), place=pltpu.VMEM):
    return pl.pallas_call(
        kernel,
        out_shape=[s if hasattr(s, "dtype") else jax.ShapeDtypeStruct(s, jnp.float32) for s in shapes],
        in_specs=[pl.BlockSpec(memory_space=place)] * len(args),
        out_specs=[pl.BlockSpec(memory_space=pltpu.VMEM)] * len(shapes),
        scratch_shapes=list(scratch),
        compiler_params=pltpu.CompilerParams(vmem_limit_bytes=16 * 1024 * 1024),
        interpret=INTERPRET,
    )(*args)


def pairs(count, start, step):
    return [pair for i in range(start, count - 1, step) for pair in ((i, i + 1), (i + 1, i))]


def partners(count):
    return [[i, i + 1] for i in range(0, count, 2)]


def per_device(
    state, prev_surface, mixing, velocity, coupling, sea_mask, interp_index, interp_weight
):
    n_lat, n_lon = lax.axis_size("lat"), lax.axis_size("lon")
    given = (
        state[0], prev_surface, mixing[0], velocity[0],
        coupling[0], sea_mask[0], interp_index[0], interp_weight[0],
    )
    state, prev, mix, vel, couple, mask, index, weight = given
    tile = (ROWS, COLS)
    column_shape = (COL_MESSAGE, COLS)
    to_near, to_far, flux, rate, state, prev, mix, vel, index, weight = call(
        pack_columns_kernel,
        [column_shape, column_shape, tile, tile, state, prev, mix, vel, index, weight],
        *(pltpu.with_memory_space_constraint(x, pltpu.HBM) for x in given), place=pltpu.HBM,
        scratch=[pltpu.VMEM(tile, couple.dtype), pltpu.VMEM(tile, mask.dtype), pltpu.SemaphoreType.DMA((8,))],
    )
    row_shape = (ROW_MESSAGE, COLS)
    fields = (state, mix, vel, rate, index, weight, flux)

    def exchange_rows(kernel, near, places):
        to_near, to_far = call(kernel, [row_shape, row_shape], *fields, near)

        def among(found):
            return [(i * n_lon + k, j * n_lon + k) for i, j in found for k in range(n_lon) if k % 4 in places]

        far = lax.ppermute(to_far, ("lat", "lon"), among(pairs(n_lat, 1, 2)))
        near = lax.ppermute(to_near, ("lat", "lon"), among(pairs(n_lat, 0, 2)))
        return near, far

    joints = range(1, n_lon, 2)
    sent = [((i, (i + 1) % n_lon) if i % 4 == 3 else (i + 1, i)) for i in joints]
    to_early = lax.ppermute(to_far, "lon", sent)
    early = lax.ppermute(to_near, "lon", pairs(n_lon, 0, 4))
    row0e, row1e = exchange_rows(pack_rows_early_kernel, early, (0, 1))
    to_late = lax.ppermute(to_far, "lon", [(j, i) for i, j in sent])
    late = lax.ppermute(to_near, "lon", pairs(n_lon, 2, 4))
    row0l, row1l = exchange_rows(pack_rows_late_kernel, late, (2, 3))
    columns = (early, late, to_early, to_late)
    rows = (row0e, row0l, row1e, row1l)
    wide, narrow = (LEV, 24, COLS), (LEV, ROWS, COLS)
    inverse, unit_top, seen = call(prepare_kernel, [narrow, tile, tile], prev, mix, index, weight)
    (fluxes,) = call(
        top_kernel, [(6 * ROWS, COLS)],
        state, mix, vel, rate, flux, *columns, *rows, inverse, unit_top, seen,
    )
    (corner,) = call(pack_corners_kernel, [(8, COLS)], to_early, to_late)
    got = lax.ppermute(fluxes, "comp", [(0, 1)])
    corner1 = lax.ppermute(corner, "lat", pairs(n_lat, 1, 2))
    corner0 = lax.all_gather(corner, "lat", axis_index_groups=partners(n_lat))
    parts = call(
        first_step_kernel, [wide, narrow, wide, narrow],
        state, mix, vel, *columns, *rows, corner0, corner1,
    )
    new_state, series = call(
        second_step_kernel, [(LEV, ROWS, COLS), (NSTEP, ROWS, COLS)],
        mix, vel, rate, index, weight, *columns, *rows, *parts, inverse, fluxes, got,
        scratch=[pltpu.VMEM(shape, jnp.float32) for shape in ((24, COLS), tile, tile)],
    )
    return new_state[None], series[None]


def solution(mesh):
    in_specs = (
        P("comp", None, "lat", "lon"),
        P(None, "lat", "lon"),
        P("comp", None, "lat", "lon"),
        P("comp", None, "lat", "lon"),
        P("comp", "lat", "lon"),
        P("comp", "lat", "lon"),
        P("comp", None, "lat", "lon"),
        P("comp", None, "lat", "lon"),
    )
    out_specs = (P("comp", None, "lat", "lon"), P("comp", None, "lat", "lon"))

    return jax.shard_map(
        per_device, mesh=mesh, in_specs=in_specs, out_specs=out_specs, check_vma=False
    )
```

```python
import jax
import jax.numpy as jnp
from jax import lax
from jax.experimental import pallas as pl
from jax.experimental.pallas import tpu as pltpu
from jax.sharding import PartitionSpec as P


INTERPRET = False
NSTEP = 2
LEV = 12
ROWS = 16
COLS = 128
smoothing = 0.15

AT_MIX = 4 * LEV
AT_VEL = AT_MIX + 2 * (LEV - 1)
AT_RATE = AT_VEL + 4
AT_WEIGHT = 80
AT_INDEX = 88
AT_FLUX = AT_WEIGHT
AT_WEST = 96
AT_EAST = 100
ROW_MESSAGE = 104
COL_MESSAGE = 2 * ROWS


def lanes(rows):
    return lax.broadcasted_iota(jnp.int32, (rows, COLS), 1)


def sublanes():
    return lax.broadcasted_iota(jnp.int32, (8, COLS), 0)


def roll(x, shift, axis):
    shift %= x.shape[axis]
    return pltpu.roll(x, shift, axis) if shift else x


def gather_cells(table, index):
    sources = [jnp.broadcast_to(table[r : r + 1], (8, COLS)) for r in range(ROWS)]
    blocks = []
    for at in range(0, index.shape[0], 8):
        cell = index[at : at + 8]
        column = lax.bitwise_and(cell, COLS - 1)
        picked = [
            jnp.take_along_axis(source, column, axis=1, mode="promise_in_bounds")
            for source in sources
        ]
        bit = COLS
        while len(picked) > 1:
            chosen = lax.bitwise_and(cell, bit) != 0
            picked = [jnp.where(chosen, b, a) for a, b in zip(picked[::2], picked[1::2])]
            bit *= 2
        blocks.append(picked[0])
    return jnp.concatenate(blocks, axis=0)


def regrid_tile(table, index_ref, weight_ref):
    index = index_ref[...].reshape(4 * ROWS, COLS)
    picked = gather_cells(table, index).reshape(4, ROWS, COLS)
    return jnp.sum(picked * weight_ref[...], axis=0)


def pack_columns_kernel(
    state_hbm, prev_hbm, mix_hbm, vel_hbm, couple_hbm, mask_hbm, index_hbm, weight_hbm,
    msg0, msg1, flux_out, rate_out, state, prev, mix, vel, index, weight, couple, mask, arrived,
):
    moves = [
        pltpu.make_async_copy(source, target, arrived.at[k])
        for k, (source, target) in enumerate(
            (
                (index_hbm, index),
                (prev_hbm, prev),
                (weight_hbm, weight),
                (state_hbm, state),
                (mix_hbm, mix),
                (vel_hbm, vel),
                (couple_hbm, couple),
                (mask_hbm, mask),
            )
        )
    ]
    for move in moves:
        move.start()
    is_atmosphere = lax.axis_index("comp") == 0
    odd = lax.rem(lax.axis_index("lon"), 2) == 1
    lane = lanes(ROWS)
    for move in moves[:3]:
        move.wait()

    @pl.when(is_atmosphere)
    def _():
        flux_out[...] = regrid_tile(prev[0], index, weight)

    for move in moves[3:]:
        move.wait()
    rate = couple[...] * mask[...].astype(jnp.float32)
    rate_out[...] = rate

    def packed(last):
        total = jnp.zeros((ROWS, COLS), jnp.float32)

        def put(total, x, at, width):
            shift = at - (COLS - width) if last else at
            return jnp.where((lane >= at) & (lane < at + width), roll(x, shift, 1), total)

        for level in range(LEV):
            total = put(total, state[level], 4 * level, 4)
        for level in range(LEV - 1):
            total = put(total, mix[level], AT_MIX + 2 * level, 2)
        for part in range(2):
            total = put(total, vel[part], AT_VEL + 2 * part, 2)
        total = put(total, rate, AT_RATE, 2)
        for j in range(4):
            total = put(total, weight[j], AT_WEIGHT + 2 * j, 2)
            total = put(total, index[j].astype(jnp.float32), AT_INDEX + 2 * j, 2)
        return total

    first, last = packed(False), packed(True)
    msg0[0:ROWS] = jnp.where(odd, first, last)
    msg1[0:ROWS] = jnp.where(odd, last, first)

    @pl.when(is_atmosphere)
    def _():
        flux = rate * (flux_out[...] - state[0])
        flux_out[...] = flux
        msg0[ROWS:] = flux
        msg1[ROWS:] = flux

    @pl.when(jnp.logical_not(is_atmosphere))
    def _():
        nothing = jnp.zeros((ROWS, COLS), jnp.float32)
        flux_out[...] = nothing
        msg0[ROWS:] = nothing
        msg1[ROWS:] = nothing


def column_messages(got):
    at_lon = lax.axis_index("lon")
    odd = lax.rem(at_lon, 2) == 1
    starts_early = lax.rem(at_lon, 4) < 2
    near = jnp.where(starts_early, got[0][...], got[1][...])
    far = jnp.where(starts_early, got[2][...], got[3][...])
    return jnp.where(odd, near, far), jnp.where(odd, far, near)


def pack_rows_kernel(
    state, mix, vel, rate_in, index, weight, flux, early, late, to_early, to_late, msg0, msg1
):
    odd = lax.rem(lax.axis_index("lat"), 2) == 1
    west, east = column_messages((early, late, to_early, to_late))
    rate = rate_in[...]

    def put(x, at, width):
        head, tail = x[0:width], x[ROWS - width : ROWS]
        msg0[at : at + width] = jnp.where(odd, head, tail)
        msg1[at : at + width] = jnp.where(odd, tail, head)

    for level in range(LEV):
        put(state[level], 4 * level, 4)
    for level in range(LEV - 1):
        put(mix[level], AT_MIX + 2 * level, 2)
    for part in range(2):
        put(vel[part], AT_VEL + 2 * part, 2)
    put(rate, AT_RATE, 2)

    @pl.when(lax.axis_index("comp") == 0)
    def _():
        msg0[AT_FLUX : AT_FLUX + ROWS] = flux[...]
        msg1[AT_FLUX : AT_FLUX + ROWS] = flux[...]

    @pl.when(lax.axis_index("comp") != 0)
    def _():
        for j in range(4):
            put(weight[j], AT_WEIGHT + 2 * j, 2)
            put(index[j].astype(jnp.float32), AT_INDEX + 2 * j, 2)

    put(west[0:ROWS], AT_WEST, 4)
    put(east[0:ROWS], AT_EAST, 4)
    for at in (AT_RATE + 2, AT_RATE + 4):
        msg0[at : at + 2] = jnp.zeros((2, COLS), jnp.float32)
        msg1[at : at + 2] = jnp.zeros((2, COLS), jnp.float32)


def row_messages(got0, got1):
    odd = lax.rem(lax.axis_index("lat"), 2)
    near = got0[1 - odd]
    far = got1[...]
    return jnp.where(odd == 1, near, far), jnp.where(odd == 1, far, near)


def transport_weights(east, north):
    def weights(v):
        near, far = v * (8.0 / 12.0), v * (1.0 / 12.0)
        return (-far, smoothing + near, smoothing - near, far)

    return weights(east), weights(north)


def horizontal(own, side, own_weights, side_weights, own_rows):
    shifts = (2, 1, -1, -2)
    result = own[:own_rows] * (1.0 - 4.0 * smoothing)
    for shift, factor in zip(shifts, own_weights[1]):
        result = result + factor * roll(own, shift, 0)[:own_rows]
    lane = lanes(own_rows)
    side_result = None
    if side_weights is not None:
        side_result = side[:ROWS] * (1.0 - 4.0 * smoothing)
        for shift, factor in zip(shifts, side_weights[1]):
            side_result = side_result + factor * roll(side, shift, 0)[:ROWS]
    for k, shift in enumerate(shifts):
        cut = lane >= COLS - shift if shift > 0 else lane < -shift
        own_part, side_part = own[:own_rows], side[:own_rows]
        moved = roll(jnp.where(cut, side_part, own_part), shift, 1)
        result = result + own_weights[0][k] * moved
        if side_weights is not None:
            there = jnp.where(cut[:ROWS], own_part[:ROWS], side_part[:ROWS])
            side_result = side_result + side_weights[0][k] * roll(there, shift, 1)
    return result, side_result


def factors(mix):
    inverses, ratios = [], []
    for level in range(LEV):
        pivot = 1.0
        if level < LEV - 1:
            pivot = pivot + mix[level]
        if level > 0:
            pivot = pivot + mix[level - 1] * (1.0 - ratios[-1])
        inverse = 1.0 / pivot
        inverses.append(inverse)
        if level < LEV - 1:
            ratios.append(mix[level] * inverse)
    return inverses, ratios


def solve(rhs, mix, inverses, ratios):
    values = []
    for level in range(LEV):
        source = rhs[level]
        if level > 0:
            source = mix[level - 1] * values[-1] if source is None else source + mix[level - 1] * values[-1]
        values.append(source * inverses[level])
    result = [None] * LEV
    result[-1] = values[-1]
    for level in range(LEV - 2, -1, -1):
        result[level] = values[level] + ratios[level] * result[level + 1]
    return result


def rim_of_levels(north, south, level):
    sub, block, odd = sublanes(), 8 * (level // 2), level % 2
    a, b = south[block : block + 8], north[block : block + 8]
    return jnp.where(sub < 4, roll(a, -4 * odd, 0), roll(b, 4 - 4 * odd, 0))


def side_of(west_tile, east_tile, at, width, rows):
    lane = lanes(rows)
    a, b = roll(east_tile[:rows], -at, 1), roll(west_tile[:rows], COLS - width - at, 1)
    return jnp.where(lane < width, a, jnp.where(lane >= COLS - width, b, 0.0))


def prepare_kernel(prev, mix, index, weight, inverse_out, unit_top, seen):
    inverses, ratios = factors([mix[level] for level in range(LEV - 1)])
    for level in range(LEV):
        inverse_out[level] = inverses[level]
    own_mix = [mix[level] for level in range(LEV - 1)]
    unit_top[...] = solve([1.0] + [None] * (LEV - 1), own_mix, inverses, ratios)[0]

    @pl.when(lax.axis_index("comp") == 0)
    def _():
        seen[...] = regrid_tile(prev[1], index, weight)


def top_kernel(
    state, mix, vel, rate, flux, early, late, to_early, to_late, row0, row1, inverse, unit_top, seen,
    fluxes,
):
    @pl.when(lax.axis_index("comp") == 0)
    def _():
        west, east = column_messages((early, late, to_early, to_late))
        north, south = row_messages(row0, row1)
        weights = transport_weights(vel[0], vel[1])
        moved = []
        for level in range(LEV):
            own = jnp.concatenate([state[level], rim_of_levels(north, south, level)], axis=0)
            there = side_of(west[0:ROWS], east[0:ROWS], 4 * level, 4, ROWS)
            moved.append(horizontal(own, there, weights, None, ROWS)[0])
        own_mix = [mix[level] for level in range(LEV - 1)]
        inverses = [inverse[level] for level in range(LEV)]
        ratios = [own_mix[level] * inverses[level] for level in range(LEV - 1)]
        top = solve(moved, own_mix, inverses, ratios)[0] + flux[...] * unit_top[...]
        fluxes[0:ROWS] = flux[...]
        fluxes[ROWS : 2 * ROWS] = west[ROWS:]
        fluxes[2 * ROWS : 3 * ROWS] = east[ROWS:]
        fluxes[3 * ROWS : 4 * ROWS] = north[AT_FLUX : AT_FLUX + ROWS]
        fluxes[4 * ROWS : 5 * ROWS] = south[AT_FLUX : AT_FLUX + ROWS]
        fluxes[5 * ROWS :] = rate[...] * (seen[...] - top)


def first_step_kernel(
    state, mix, vel, early, late, to_early, to_late, row0, row1, before, before_side, unit, unit_side,
):
    west, east = column_messages((early, late, to_early, to_late))
    north, south = row_messages(row0, row1)
    at_lat = lax.axis_index("lat")
    sub = sublanes()
    valid = ((sub < 4) & (at_lat < lax.axis_size("lat") - 1)) | ((sub >= 4) & (at_lat > 0))

    def rim2(at):
        block, offset = 8 * (at // 8), at % 8
        a, b = south[block : block + 8], north[block : block + 8]
        a, b = roll(a, -offset, 0), roll(b, 6 - offset, 0)
        return jnp.where(sub < 2, a, jnp.where(sub >= 6, b, 0.0))

    def cornered(packed, at):
        a, b = south[AT_WEST : AT_WEST + 8], north[AT_WEST : AT_WEST + 8]
        if at == AT_WEST:
            rim = jnp.where(sub < 4, a, roll(b, 4, 0))
        else:
            rim = jnp.where(sub < 4, roll(a, 4, 0), b)
        return jnp.concatenate([packed[0:ROWS], rim], axis=0)

    west_tile, east_tile = cornered(west, AT_WEST), cornered(east, AT_EAST)

    def side(at, width, rows):
        return side_of(west_tile, east_tile, at, width, rows)

    def extended(x, rim):
        return jnp.concatenate([x, rim], axis=0)

    own_mix = [extended(mix[level], rim2(AT_MIX + 2 * level)) for level in range(LEV - 1)]
    side_mix = [side(AT_MIX + 2 * level, 2, ROWS) for level in range(LEV - 1)]
    own_vel = [extended(vel[part], rim2(AT_VEL + 2 * part)) for part in range(2)]
    side_vel = [side(AT_VEL + 2 * part, 2, ROWS) for part in range(2)]
    own_weights, side_weights = transport_weights(*own_vel), transport_weights(*side_vel)

    moved, moved_side = [], []
    for level in range(LEV):
        own = extended(state[level], rim_of_levels(north, south, level))
        a, b = horizontal(own, side(4 * level, 4, 24), own_weights, side_weights, 24)
        moved.append(a)
        moved_side.append(b)
    inverses, ratios = factors(own_mix)
    solved = solve(moved, own_mix, inverses, ratios)
    impulse = solve([1.0] + [None] * (LEV - 1), own_mix, inverses, ratios)
    for level in range(LEV):
        for out, values in ((before, solved), (unit, impulse)):
            out[level, 0:ROWS] = values[level][:ROWS]
            out[level, ROWS:] = jnp.where(valid, values[level][ROWS:], 0.0)
    inverses, ratios = factors(side_mix)
    solved = solve(moved_side, side_mix, inverses, ratios)
    impulse = solve([1.0] + [None] * (LEV - 1), side_mix, inverses, ratios)
    for level in range(LEV):
        before_side[level] = solved[level]
        unit_side[level] = impulse[level]


def second_step_kernel(
    mix, vel, rate_in, index, weight, early, late, to_early, to_late, row0, row1,
    before, before_side, unit, unit_side, inverse, sent, got, new_state, series, force, force_side, force1,
):
    is_atmosphere = lax.axis_index("comp") == 0
    sub = sublanes()
    lane = lanes(ROWS)

    @pl.when(is_atmosphere)
    def _():
        tables = [sent[k * ROWS : (k + 1) * ROWS] for k in range(6)]
        force[0:ROWS] = tables[0]
        force[ROWS:] = jnp.where(sub < 4, tables[4][0:8], tables[3][8:16])
        force_side[...] = jnp.where(lane < 64, tables[2], tables[1])
        force1[...] = tables[5]

    @pl.when(jnp.logical_not(is_atmosphere))
    def _():
        tables = [got[k * ROWS : (k + 1) * ROWS] for k in range(6)]
        rate = rate_in[...]
        force[0:ROWS] = rate * regrid_tile(tables[0], index, weight)
        force1[...] = rate * regrid_tile(tables[5], index, weight)
        west, east = column_messages((early, late, to_early, to_late))
        north, south = row_messages(row0, row1)

        def of_rows(message, table, place):
            index8 = message[AT_INDEX : AT_INDEX + 8].astype(jnp.int32)
            total = gather_cells(table, index8) * message[AT_WEIGHT : AT_WEIGHT + 8]
            total = total + roll(total, 4, 0)
            total = total + roll(total, 2, 0)
            block, offset = 8 * (AT_RATE // 8), AT_RATE % 8
            return roll(message[block : block + 8], place - offset, 0) * roll(total, place, 0)

        force[ROWS:] = jnp.where(sub < 4, of_rows(south, tables[4], 0), of_rows(north, tables[3], 6))

        def of_columns(message, table, place):
            tile = message[0:ROWS]
            total = roll(gather_cells(table, tile.astype(jnp.int32)), AT_WEIGHT - AT_INDEX, 1) * tile
            total = total + roll(total, -4, 1)
            total = total + roll(total, -2, 1)
            return roll(tile, place - AT_RATE, 1) * roll(total, place - AT_WEIGHT, 1)

        force_side[...] = jnp.where(
            lane < 64, of_columns(east, tables[2], 0), of_columns(west, tables[1], COLS - 2)
        )

    own_weights = transport_weights(vel[0], vel[1])
    f, f_side = force[...], force_side[...]
    moved = []
    for level in range(LEV):
        own = before[level] + f * unit[level]
        there = before_side[level] + f_side * unit_side[level]
        if level == 0:
            top = own[:ROWS]
        moved.append(horizontal(own, there, own_weights, None, ROWS)[0])
    moved[0] = moved[0] + force1[...]
    own_mix = [mix[level] for level in range(LEV - 1)]
    inverses = [inverse[level] for level in range(LEV)]
    ratios = [own_mix[level] * inverses[level] for level in range(LEV - 1)]
    solved = solve(moved, own_mix, inverses, ratios)
    for level in range(LEV):
        new_state[level] = solved[level]
    series[0] = jnp.where(is_atmosphere, f[:ROWS], top)
    series[1] = jnp.where(is_atmosphere, force1[...], solved[0])


def call(kernel, shapes, *args, scratch=(), place=pltpu.VMEM):
    return pl.pallas_call(
        kernel,
        out_shape=[s if hasattr(s, "dtype") else jax.ShapeDtypeStruct(s, jnp.float32) for s in shapes],
        in_specs=[pl.BlockSpec(memory_space=place)] * len(args),
        out_specs=[pl.BlockSpec(memory_space=pltpu.VMEM)] * len(shapes),
        scratch_shapes=list(scratch),
        compiler_params=pltpu.CompilerParams(vmem_limit_bytes=16 * 1024 * 1024),
        interpret=INTERPRET,
    )(*args)


def pairs(count, start, step):
    return [pair for i in range(start, count - 1, step) for pair in ((i, i + 1), (i + 1, i))]


def partners(count):
    return [[i, i + 1] for i in range(0, count, 2)]


def per_device(
    state, prev_surface, mixing, velocity, coupling, sea_mask, interp_index, interp_weight
):
    n_lat, n_lon = lax.axis_size("lat"), lax.axis_size("lon")
    given = (
        state[0], prev_surface, mixing[0], velocity[0],
        coupling[0], sea_mask[0], interp_index[0], interp_weight[0],
    )
    state, prev, mix, vel, couple, mask, index, weight = given
    tile = (ROWS, COLS)
    column_shape = (COL_MESSAGE, COLS)
    to_near, to_far, flux, rate, state, prev, mix, vel, index, weight = call(
        pack_columns_kernel,
        [column_shape, column_shape, tile, tile, state, prev, mix, vel, index, weight],
        *(pltpu.with_memory_space_constraint(x, pltpu.HBM) for x in given), place=pltpu.HBM,
        scratch=[pltpu.VMEM(tile, couple.dtype), pltpu.VMEM(tile, mask.dtype), pltpu.SemaphoreType.DMA((8,))],
    )
    joints = range(1, n_lon, 2)
    sent = [((i, (i + 1) % n_lon) if i % 4 == 3 else (i + 1, i)) for i in joints]
    to_early = lax.ppermute(to_far, "lon", sent)
    early = lax.ppermute(to_near, "lon", pairs(n_lon, 0, 4))
    to_late = lax.ppermute(to_far, "lon", [(j, i) for i, j in sent])
    late = lax.ppermute(to_near, "lon", pairs(n_lon, 2, 4))
    columns = (early, late, to_early, to_late)
    row_shape = (ROW_MESSAGE, COLS)
    to_near, to_far = call(
        pack_rows_kernel, [row_shape, row_shape],
        state, mix, vel, rate, index, weight, flux, *columns,
    )
    row1 = lax.ppermute(to_far, "lat", pairs(n_lat, 1, 2))
    row0 = lax.all_gather(to_near, "lat", axis_index_groups=partners(n_lat))
    wide, narrow = (LEV, 24, COLS), (LEV, ROWS, COLS)
    inverse, unit_top, seen = call(prepare_kernel, [narrow, tile, tile], prev, mix, index, weight)
    (fluxes,) = call(
        top_kernel, [(6 * ROWS, COLS)],
        state, mix, vel, rate, flux, *columns, row0, row1, inverse, unit_top, seen,
    )
    got = lax.ppermute(fluxes, "comp", [(0, 1)])
    parts = call(
        first_step_kernel, [wide, narrow, wide, narrow],
        state, mix, vel, *columns, row0, row1,
    )
    new_state, series = call(
        second_step_kernel, [(LEV, ROWS, COLS), (NSTEP, ROWS, COLS)],
        mix, vel, rate, index, weight, *columns, row0, row1, *parts, inverse, fluxes, got,
        scratch=[pltpu.VMEM(shape, jnp.float32) for shape in ((24, COLS), tile, tile)],
    )
    return new_state[None], series[None]


def solution(mesh):
    in_specs = (
        P("comp", None, "lat", "lon"),
        P(None, "lat", "lon"),
        P("comp", None, "lat", "lon"),
        P("comp", None, "lat", "lon"),
        P("comp", "lat", "lon"),
        P("comp", "lat", "lon"),
        P("comp", None, "lat", "lon"),
        P("comp", None, "lat", "lon"),
    )
    out_specs = (P("comp", None, "lat", "lon"), P("comp", None, "lat", "lon"))

    return jax.shard_map(
        per_device, mesh=mesh, in_specs=in_specs, out_specs=out_specs, check_vma=False
    )
```

```python
import jax
import jax.numpy as jnp
from jax import lax
from jax.experimental import pallas as pl
from jax.experimental.pallas import tpu as pltpu
from jax.sharding import PartitionSpec as P


INTERPRET = False
NSTEP = 2
LEV = 12
ROWS = 16
COLS = 128
smoothing = 0.15

AT_MIX = 4 * LEV
AT_VEL = AT_MIX + 2 * (LEV - 1)
AT_RATE = AT_VEL + 4
AT_WEIGHT = 80
AT_INDEX = 88
AT_FLUX = AT_WEIGHT
AT_WEST = 96
AT_EAST = 100
ROW_MESSAGE = 104
COL_MESSAGE = 2 * ROWS


def lanes(rows):
    return lax.broadcasted_iota(jnp.int32, (rows, COLS), 1)


def sublanes():
    return lax.broadcasted_iota(jnp.int32, (8, COLS), 0)


def roll(x, shift, axis):
    shift %= x.shape[axis]
    return pltpu.roll(x, shift, axis) if shift else x


def gather_cells(table, index):
    sources = [jnp.broadcast_to(table[r : r + 1], (8, COLS)) for r in range(ROWS)]
    blocks = []
    for at in range(0, index.shape[0], 8):
        cell = index[at : at + 8]
        column = lax.bitwise_and(cell, COLS - 1)
        picked = [
            jnp.take_along_axis(source, column, axis=1, mode="promise_in_bounds")
            for source in sources
        ]
        bit = COLS
        while len(picked) > 1:
            chosen = lax.bitwise_and(cell, bit) != 0
            picked = [jnp.where(chosen, b, a) for a, b in zip(picked[::2], picked[1::2])]
            bit *= 2
        blocks.append(picked[0])
    return jnp.concatenate(blocks, axis=0)


def regrid_tile(table, index_ref, weight_ref):
    index = index_ref[...].reshape(4 * ROWS, COLS)
    picked = gather_cells(table, index).reshape(4, ROWS, COLS)
    return jnp.sum(picked * weight_ref[...], axis=0)


def pack_columns_kernel(
    state_hbm, prev_hbm, mix_hbm, vel_hbm, couple_hbm, mask_hbm, index_hbm, weight_hbm,
    msg0, msg1, flux_out, rate_out, state, prev, mix, vel, index, weight, couple, mask, arrived,
):
    moves = [
        pltpu.make_async_copy(source, target, arrived.at[k])
        for k, (source, target) in enumerate(
            (
                (index_hbm, index),
                (prev_hbm, prev),
                (weight_hbm, weight),
                (state_hbm, state),
                (mix_hbm, mix),
                (vel_hbm, vel),
                (couple_hbm, couple),
                (mask_hbm, mask),
            )
        )
    ]
    for move in moves:
        move.start()
    is_atmosphere = lax.axis_index("comp") == 0
    odd = lax.rem(lax.axis_index("lon"), 2) == 1
    lane = lanes(ROWS)
    for move in moves[:3]:
        move.wait()

    @pl.when(is_atmosphere)
    def _():
        flux_out[...] = regrid_tile(prev[0], index, weight)

    for move in moves[3:]:
        move.wait()
    rate = couple[...] * mask[...].astype(jnp.float32)
    rate_out[...] = rate

    def packed(last):
        total = jnp.zeros((ROWS, COLS), jnp.float32)

        def put(total, x, at, width):
            shift = at - (COLS - width) if last else at
            return jnp.where((lane >= at) & (lane < at + width), roll(x, shift, 1), total)

        for level in range(LEV):
            total = put(total, state[level], 4 * level, 4)
        for level in range(LEV - 1):
            total = put(total, mix[level], AT_MIX + 2 * level, 2)
        for part in range(2):
            total = put(total, vel[part], AT_VEL + 2 * part, 2)
        total = put(total, rate, AT_RATE, 2)
        for j in range(4):
            total = put(total, weight[j], AT_WEIGHT + 2 * j, 2)
            total = put(total, index[j].astype(jnp.float32), AT_INDEX + 2 * j, 2)
        return total

    first, last = packed(False), packed(True)
    msg0[0:ROWS] = jnp.where(odd, first, last)
    msg1[0:ROWS] = jnp.where(odd, last, first)

    @pl.when(is_atmosphere)
    def _():
        flux = rate * (flux_out[...] - state[0])
        flux_out[...] = flux
        msg0[ROWS:] = flux
        msg1[ROWS:] = flux

    @pl.when(jnp.logical_not(is_atmosphere))
    def _():
        nothing = jnp.zeros((ROWS, COLS), jnp.float32)
        flux_out[...] = nothing
        msg0[ROWS:] = nothing
        msg1[ROWS:] = nothing


def column_messages(got):
    at_lon = lax.axis_index("lon")
    odd = lax.rem(at_lon, 2) == 1
    starts_early = lax.rem(at_lon, 4) < 2
    near = jnp.where(starts_early, got[0][...], got[1][...])
    far = jnp.where(starts_early, got[2][...], got[3][...])
    return jnp.where(odd, near, far), jnp.where(odd, far, near)


def pack_rows_kernel(
    state, mix, vel, rate_in, index, weight, flux, early, late, to_early, to_late, msg0, msg1
):
    odd = lax.rem(lax.axis_index("lat"), 2) == 1
    west, east = column_messages((early, late, to_early, to_late))
    rate = rate_in[...]

    def put(x, at, width):
        head, tail = x[0:width], x[ROWS - width : ROWS]
        msg0[at : at + width] = jnp.where(odd, head, tail)
        msg1[at : at + width] = jnp.where(odd, tail, head)

    for level in range(LEV):
        put(state[level], 4 * level, 4)
    for level in range(LEV - 1):
        put(mix[level], AT_MIX + 2 * level, 2)
    for part in range(2):
        put(vel[part], AT_VEL + 2 * part, 2)
    put(rate, AT_RATE, 2)

    @pl.when(lax.axis_index("comp") == 0)
    def _():
        msg0[AT_FLUX : AT_FLUX + ROWS] = flux[...]
        msg1[AT_FLUX : AT_FLUX + ROWS] = flux[...]

    @pl.when(lax.axis_index("comp") != 0)
    def _():
        for j in range(4):
            put(weight[j], AT_WEIGHT + 2 * j, 2)
            put(index[j].astype(jnp.float32), AT_INDEX + 2 * j, 2)

    put(west[0:ROWS], AT_WEST, 4)
    put(east[0:ROWS], AT_EAST, 4)
    for at in (AT_RATE + 2, AT_RATE + 4):
        msg0[at : at + 2] = jnp.zeros((2, COLS), jnp.float32)
        msg1[at : at + 2] = jnp.zeros((2, COLS), jnp.float32)


def row_messages(got0, got1):
    odd = lax.rem(lax.axis_index("lat"), 2)
    near = got0[1 - odd]
    far = got1[...]
    return jnp.where(odd == 1, near, far), jnp.where(odd == 1, far, near)


def transport_weights(east, north):
    def weights(v):
        near, far = v * (8.0 / 12.0), v * (1.0 / 12.0)
        return (-far, smoothing + near, smoothing - near, far)

    return weights(east), weights(north)


def horizontal(own, side, own_weights, side_weights, own_rows):
    shifts = (2, 1, -1, -2)
    result = own[:own_rows] * (1.0 - 4.0 * smoothing)
    for shift, factor in zip(shifts, own_weights[1]):
        result = result + factor * roll(own, shift, 0)[:own_rows]
    lane = lanes(own_rows)
    side_result = None
    if side_weights is not None:
        side_result = side[:ROWS] * (1.0 - 4.0 * smoothing)
        for shift, factor in zip(shifts, side_weights[1]):
            side_result = side_result + factor * roll(side, shift, 0)[:ROWS]
    for k, shift in enumerate(shifts):
        cut = lane >= COLS - shift if shift > 0 else lane < -shift
        own_part, side_part = own[:own_rows], side[:own_rows]
        moved = roll(jnp.where(cut, side_part, own_part), shift, 1)
        result = result + own_weights[0][k] * moved
        if side_weights is not None:
            there = jnp.where(cut[:ROWS], own_part[:ROWS], side_part[:ROWS])
            side_result = side_result + side_weights[0][k] * roll(there, shift, 1)
    return result, side_result


def factors(mix):
    inverses, ratios = [], []
    for level in range(LEV):
        pivot = 1.0
        if level < LEV - 1:
            pivot = pivot + mix[level]
        if level > 0:
            pivot = pivot + mix[level - 1] * (1.0 - ratios[-1])
        inverse = 1.0 / pivot
        inverses.append(inverse)
        if level < LEV - 1:
            ratios.append(mix[level] * inverse)
    return inverses, ratios


def solve(rhs, mix, inverses, ratios):
    values = []
    for level in range(LEV):
        source = rhs[level]
        if level > 0:
            source = mix[level - 1] * values[-1] if source is None else source + mix[level - 1] * values[-1]
        values.append(source * inverses[level])
    result = [None] * LEV
    result[-1] = values[-1]
    for level in range(LEV - 2, -1, -1):
        result[level] = values[level] + ratios[level] * result[level + 1]
    return result


def rim_of_levels(north, south, level):
    sub, block, odd = sublanes(), 8 * (level // 2), level % 2
    a, b = south[block : block + 8], north[block : block + 8]
    return jnp.where(sub < 4, roll(a, -4 * odd, 0), roll(b, 4 - 4 * odd, 0))


def side_of(west_tile, east_tile, at, width, rows):
    lane = lanes(rows)
    a, b = roll(east_tile[:rows], -at, 1), roll(west_tile[:rows], COLS - width - at, 1)
    return jnp.where(lane < width, a, jnp.where(lane >= COLS - width, b, 0.0))


IMPULSE = [1.0] + [None] * (LEV - 1)


def prepare_kernel(
    prev, mix, index, weight, early, late, to_early, to_late, inverse, inverse_side, unit, unit_side, seen
):
    west, east = column_messages((early, late, to_early, to_late))
    own_mix = [mix[level] for level in range(LEV - 1)]
    side_mix = [side_of(west, east, AT_MIX + 2 * level, 2, ROWS) for level in range(LEV - 1)]
    found = [(factors(m), m) for m in (own_mix, side_mix)]
    for ((inverses, ratios), m), inverse_out, out in zip(
        found, (inverse, inverse_side), (unit, unit_side)
    ):
        impulse = solve(IMPULSE, m, inverses, ratios)
        for level in range(LEV):
            inverse_out[level] = inverses[level]
            out[level] = impulse[level]

    @pl.when(lax.axis_index("comp") == 0)
    def _():
        seen[...] = regrid_tile(prev[1], index, weight)


def stored(inverse, mixes):
    inverses = [inverse[level] for level in range(LEV)]
    return inverses, [mixes[level] * inverses[level] for level in range(LEV - 1)]


def top_step(state, mix, vel, rate, flux, columns, rows, inverse, unit, seen, fluxes):
    west, east = column_messages(columns)
    north, south = row_messages(*rows)
    weights = transport_weights(vel[0], vel[1])
    moved = []
    for level in range(LEV):
        own = jnp.concatenate([state[level], rim_of_levels(north, south, level)], axis=0)
        there = side_of(west[0:ROWS], east[0:ROWS], 4 * level, 4, ROWS)
        moved.append(horizontal(own, there, weights, None, ROWS)[0])
    own_mix = [mix[level] for level in range(LEV - 1)]
    top = solve(moved, own_mix, *stored(inverse, own_mix))[0] + flux[...] * unit[0]
    fluxes[0:ROWS] = flux[...]
    fluxes[ROWS : 2 * ROWS] = west[ROWS:]
    fluxes[2 * ROWS : 3 * ROWS] = east[ROWS:]
    fluxes[3 * ROWS : 4 * ROWS] = north[AT_FLUX : AT_FLUX + ROWS]
    fluxes[4 * ROWS : 5 * ROWS] = south[AT_FLUX : AT_FLUX + ROWS]
    fluxes[5 * ROWS :] = rate[...] * (seen[...] - top)


def halo_step(state, mix, vel, columns, rows, inverse, inverse_side, before, before_side, unit_rim):
    west, east = column_messages(columns)
    north, south = row_messages(*rows)
    at_lat = lax.axis_index("lat")
    sub = sublanes()
    valid = ((sub < 4) & (at_lat < lax.axis_size("lat") - 1)) | ((sub >= 4) & (at_lat > 0))

    def rim2(at):
        block, offset = 8 * (at // 8), at % 8
        a, b = south[block : block + 8], north[block : block + 8]
        a, b = roll(a, -offset, 0), roll(b, 6 - offset, 0)
        return jnp.where(sub < 2, a, jnp.where(sub >= 6, b, 0.0))

    def cornered(packed, at):
        a, b = south[AT_WEST : AT_WEST + 8], north[AT_WEST : AT_WEST + 8]
        if at == AT_WEST:
            rim = jnp.where(sub < 4, a, roll(b, 4, 0))
        else:
            rim = jnp.where(sub < 4, roll(a, 4, 0), b)
        return jnp.concatenate([packed[0:ROWS], rim], axis=0)

    west_tile, east_tile = cornered(west, AT_WEST), cornered(east, AT_EAST)

    def side(at, width, rows):
        return side_of(west_tile, east_tile, at, width, rows)

    own_mix = [mix[level] for level in range(LEV - 1)]
    rim_mix = [rim2(AT_MIX + 2 * level) for level in range(LEV - 1)]
    side_mix = [side(AT_MIX + 2 * level, 2, ROWS) for level in range(LEV - 1)]
    own_vel = [
        jnp.concatenate([vel[part], rim2(AT_VEL + 2 * part)], axis=0) for part in range(2)
    ]
    side_vel = [side(AT_VEL + 2 * part, 2, ROWS) for part in range(2)]
    own_weights, side_weights = transport_weights(*own_vel), transport_weights(*side_vel)
    rim_factors = factors(rim_mix)
    moved, moved_side = [], []
    for level in range(LEV):
        own = jnp.concatenate([state[level], rim_of_levels(north, south, level)], axis=0)
        a, b = horizontal(own, side(4 * level, 4, 24), own_weights, side_weights, 24)
        moved.append(a)
        moved_side.append(b)
    rim = solve([x[ROWS:] for x in moved], rim_mix, *rim_factors)
    impulse = solve(IMPULSE, rim_mix, *rim_factors)
    own = solve([x[:ROWS] for x in moved], own_mix, *stored(inverse, own_mix))
    there = solve(moved_side, side_mix, *stored(inverse_side, side_mix))
    for level in range(LEV):
        before[level, 0:ROWS] = own[level]
        before[level, ROWS:] = jnp.where(valid, rim[level], 0.0)
        before_side[level] = there[level]
        unit_rim[level] = jnp.where(valid, impulse[level], 0.0)


def middle_kernel(
    state, mix, vel, rate, flux, early, late, to_early, to_late, row0, row1,
    inverse, inverse_side, unit, seen, fluxes, before, before_side, unit_rim,
):
    columns, rows = (early, late, to_early, to_late), (row0, row1)

    @pl.when(lax.axis_index("comp") == 0)
    def _():
        top_step(state, mix, vel, rate, flux, columns, rows, inverse, unit, seen, fluxes)

    @pl.when(lax.axis_index("comp") != 0)
    def _():
        halo_step(state, mix, vel, columns, rows, inverse, inverse_side, before, before_side, unit_rim)


def second_step_kernel(
    state, mix, vel, rate_in, index, weight, early, late, to_early, to_late, row0, row1,
    inverse, inverse_side, unit, unit_side, given_before, given_side, given_rim, got,
    new_state, series, own_before, own_side, own_rim,
):
    columns, rows = (early, late, to_early, to_late), (row0, row1)
    sub = sublanes()
    lane = lanes(ROWS)
    tables = [got[0, k * ROWS : (k + 1) * ROWS] for k in range(6)]
    own_mix = [mix[level] for level in range(LEV - 1)]

    def advance(force, force_rim, force_side, force1, before, before_side, unit_rim):
        weights = transport_weights(vel[0], vel[1])
        moved = []
        for level in range(LEV):
            tile = before[level, 0:ROWS] + force * unit[level]
            rim = before[level, ROWS:] + force_rim * unit_rim[level]
            there = before_side[level] + force_side * unit_side[level]
            if level == 0:
                top = tile
            own = jnp.concatenate([tile, rim], axis=0)
            moved.append(horizontal(own, there, weights, None, ROWS)[0])
        moved[0] = moved[0] + force1
        solved = solve(moved, own_mix, *stored(inverse, own_mix))
        for level in range(LEV):
            new_state[level] = solved[level]
        return top, solved[0]

    @pl.when(lax.axis_index("comp") == 0)
    def _():
        halo_step(state, mix, vel, columns, rows, inverse, inverse_side, own_before, own_side, own_rim)
        rim = jnp.where(sub < 4, tables[4][0:8], tables[3][8:16])
        side = jnp.where(lane < 64, tables[2], tables[1])
        advance(tables[0], rim, side, tables[5], own_before, own_side, own_rim)
        series[0] = tables[0]
        series[1] = tables[5]

    @pl.when(lax.axis_index("comp") != 0)
    def _():
        rate = rate_in[...]
        west, east = column_messages(columns)
        north, south = row_messages(*rows)

        def of_rows(message, table, place):
            index8 = message[AT_INDEX : AT_INDEX + 8].astype(jnp.int32)
            total = gather_cells(table, index8) * message[AT_WEIGHT : AT_WEIGHT + 8]
            total = total + roll(total, 4, 0)
            total = total + roll(total, 2, 0)
            block, offset = 8 * (AT_RATE // 8), AT_RATE % 8
            return roll(message[block : block + 8], place - offset, 0) * roll(total, place, 0)

        def of_columns(message, table, place):
            tile = message[0:ROWS]
            total = roll(gather_cells(table, tile.astype(jnp.int32)), AT_WEIGHT - AT_INDEX, 1) * tile
            total = total + roll(total, -4, 1)
            total = total + roll(total, -2, 1)
            return roll(tile, place - AT_RATE, 1) * roll(total, place - AT_WEIGHT, 1)

        rim = jnp.where(sub < 4, of_rows(south, tables[4], 0), of_rows(north, tables[3], 6))
        side = jnp.where(
            lane < 64, of_columns(east, tables[2], 0), of_columns(west, tables[1], COLS - 2)
        )
        force = rate * regrid_tile(tables[0], index, weight)
        force1 = rate * regrid_tile(tables[5], index, weight)
        top, last = advance(force, rim, side, force1, given_before, given_side, given_rim)
        series[0] = top
        series[1] = last


def call(kernel, shapes, *args, scratch=(), place=pltpu.VMEM):
    return pl.pallas_call(
        kernel,
        out_shape=[s if hasattr(s, "dtype") else jax.ShapeDtypeStruct(s, jnp.float32) for s in shapes],
        in_specs=[pl.BlockSpec(memory_space=place)] * len(args),
        out_specs=[pl.BlockSpec(memory_space=pltpu.VMEM)] * len(shapes),
        scratch_shapes=list(scratch),
        compiler_params=pltpu.CompilerParams(vmem_limit_bytes=16 * 1024 * 1024),
        interpret=INTERPRET,
    )(*args)


def pairs(count, start, step):
    return [pair for i in range(start, count - 1, step) for pair in ((i, i + 1), (i + 1, i))]


def partners(count):
    return [[i, i + 1] for i in range(0, count, 2)]


def per_device(
    state, prev_surface, mixing, velocity, coupling, sea_mask, interp_index, interp_weight
):
    n_lat, n_lon = lax.axis_size("lat"), lax.axis_size("lon")
    given = (
        state[0], prev_surface, mixing[0], velocity[0],
        coupling[0], sea_mask[0], interp_index[0], interp_weight[0],
    )
    state, prev, mix, vel, couple, mask, index, weight = given
    tile = (ROWS, COLS)
    column_shape = (COL_MESSAGE, COLS)
    to_near, to_far, flux, rate, state, prev, mix, vel, index, weight = call(
        pack_columns_kernel,
        [column_shape, column_shape, tile, tile, state, prev, mix, vel, index, weight],
        *(pltpu.with_memory_space_constraint(x, pltpu.HBM) for x in given), place=pltpu.HBM,
        scratch=[pltpu.VMEM(tile, couple.dtype), pltpu.VMEM(tile, mask.dtype), pltpu.SemaphoreType.DMA((8,))],
    )
    joints = range(1, n_lon, 2)
    sent = [((i, (i + 1) % n_lon) if i % 4 == 3 else (i + 1, i)) for i in joints]
    to_early = lax.ppermute(to_far, "lon", sent)
    early = lax.ppermute(to_near, "lon", pairs(n_lon, 0, 4))
    to_late = lax.ppermute(to_far, "lon", [(j, i) for i, j in sent])
    late = lax.ppermute(to_near, "lon", pairs(n_lon, 2, 4))
    columns = (early, late, to_early, to_late)
    row_shape = (ROW_MESSAGE, COLS)
    to_near, to_far = call(
        pack_rows_kernel, [row_shape, row_shape],
        state, mix, vel, rate, index, weight, flux, *columns,
    )
    row1 = lax.ppermute(to_far, "lat", pairs(n_lat, 1, 2))
    row0 = lax.all_gather(to_near, "lat", axis_index_groups=partners(n_lat))
    rows = (row0, row1)
    narrow = (LEV, ROWS, COLS)
    parts = [(LEV, 24, COLS), narrow, (LEV, 8, COLS)]
    inverse, inverse_side, unit, unit_side, seen = call(
        prepare_kernel, [narrow] * 4 + [tile], prev, mix, index, weight, *columns
    )
    fluxes, *before = call(
        middle_kernel, [(6 * ROWS, COLS)] + parts,
        state, mix, vel, rate, flux, *columns, *rows, inverse, inverse_side, unit, seen,
    )
    got = lax.all_gather(fluxes, "comp")
    new_state, series = call(
        second_step_kernel, [narrow, (NSTEP, ROWS, COLS)],
        state, mix, vel, rate, index, weight, *columns, *rows,
        inverse, inverse_side, unit, unit_side, *before, got,
        scratch=[pltpu.VMEM(shape, jnp.float32) for shape in parts],
    )
    return new_state[None], series[None]


def solution(mesh):
    in_specs = (
        P("comp", None, "lat", "lon"),
        P(None, "lat", "lon"),
        P("comp", None, "lat", "lon"),
        P("comp", None, "lat", "lon"),
        P("comp", "lat", "lon"),
        P("comp", "lat", "lon"),
        P("comp", None, "lat", "lon"),
        P("comp", None, "lat", "lon"),
    )
    out_specs = (P("comp", None, "lat", "lon"), P("comp", None, "lat", "lon"))

    return jax.shard_map(
        per_device, mesh=mesh, in_specs=in_specs, out_specs=out_specs, check_vma=False
    )
```

```python
import jax
import jax.numpy as jnp
from jax import lax
from jax.experimental import pallas as pl
from jax.experimental.pallas import tpu as pltpu
from jax.sharding import PartitionSpec as P


INTERPRET = False
NSTEP = 2
LEV = 12
ROWS = 16
COLS = 128
smoothing = 0.15

AT_MIX = 4 * LEV
AT_VEL = AT_MIX + 2 * (LEV - 1)
AT_RATE = AT_VEL + 4
AT_WEIGHT = 80
AT_INDEX = 88
AT_FLUX = AT_WEIGHT
AT_WEST = 96
AT_EAST = 100
ROW_MESSAGE = 104
COL_MESSAGE = 2 * ROWS


def lanes(rows):
    return lax.broadcasted_iota(jnp.int32, (rows, COLS), 1)


def sublanes():
    return lax.broadcasted_iota(jnp.int32, (8, COLS), 0)


def roll(x, shift, axis):
    shift %= x.shape[axis]
    return pltpu.roll(x, shift, axis) if shift else x


def gather_cells(table, index):
    sources = [jnp.broadcast_to(table[r : r + 1], (8, COLS)) for r in range(ROWS)]
    blocks = []
    for at in range(0, index.shape[0], 8):
        cell = index[at : at + 8]
        column = lax.bitwise_and(cell, COLS - 1)
        picked = [
            jnp.take_along_axis(source, column, axis=1, mode="promise_in_bounds")
            for source in sources
        ]
        bit = COLS
        while len(picked) > 1:
            chosen = lax.bitwise_and(cell, bit) != 0
            picked = [jnp.where(chosen, b, a) for a, b in zip(picked[::2], picked[1::2])]
            bit *= 2
        blocks.append(picked[0])
    return jnp.concatenate(blocks, axis=0)


def regrid_tile(table, index_ref, weight_ref):
    index = index_ref[...].reshape(4 * ROWS, COLS)
    picked = gather_cells(table, index).reshape(4, ROWS, COLS)
    return jnp.sum(picked * weight_ref[...], axis=0)


def pack_columns_kernel(
    state_hbm, prev_hbm, mix_hbm, vel_hbm, couple_hbm, mask_hbm, index_hbm, weight_hbm,
    msg0, msg1, flux_out, rate_out, state, prev, mix, vel, index, weight, couple, mask, arrived,
):
    moves = [
        pltpu.make_async_copy(source, target, arrived.at[k])
        for k, (source, target) in enumerate(
            (
                (index_hbm, index),
                (prev_hbm, prev),
                (weight_hbm, weight),
                (state_hbm, state),
                (mix_hbm, mix),
                (vel_hbm, vel),
                (couple_hbm, couple),
                (mask_hbm, mask),
            )
        )
    ]
    for move in moves:
        move.start()
    is_atmosphere = lax.axis_index("comp") == 0
    odd = lax.rem(lax.axis_index("lon"), 2) == 1
    lane = lanes(ROWS)
    for move in moves[:3]:
        move.wait()

    @pl.when(is_atmosphere)
    def _():
        flux_out[...] = regrid_tile(prev[0], index, weight)

    for move in moves[3:]:
        move.wait()
    rate = couple[...] * mask[...].astype(jnp.float32)
    rate_out[...] = rate

    def packed(last):
        total = jnp.zeros((ROWS, COLS), jnp.float32)

        def put(total, x, at, width):
            shift = at - (COLS - width) if last else at
            return jnp.where((lane >= at) & (lane < at + width), roll(x, shift, 1), total)

        for level in range(LEV):
            total = put(total, state[level], 4 * level, 4)
        for level in range(LEV - 1):
            total = put(total, mix[level], AT_MIX + 2 * level, 2)
        for part in range(2):
            total = put(total, vel[part], AT_VEL + 2 * part, 2)
        total = put(total, rate, AT_RATE, 2)
        for j in range(4):
            total = put(total, weight[j], AT_WEIGHT + 2 * j, 2)
            total = put(total, index[j].astype(jnp.float32), AT_INDEX + 2 * j, 2)
        return total

    first, last = packed(False), packed(True)
    msg0[0:ROWS] = jnp.where(odd, first, last)
    msg1[0:ROWS] = jnp.where(odd, last, first)

    @pl.when(is_atmosphere)
    def _():
        flux = rate * (flux_out[...] - state[0])
        flux_out[...] = flux
        msg0[ROWS:] = flux
        msg1[ROWS:] = flux

    @pl.when(jnp.logical_not(is_atmosphere))
    def _():
        nothing = jnp.zeros((ROWS, COLS), jnp.float32)
        flux_out[...] = nothing
        msg0[ROWS:] = nothing
        msg1[ROWS:] = nothing


def column_messages(got):
    at_lon = lax.axis_index("lon")
    odd = lax.rem(at_lon, 2) == 1
    starts_early = lax.rem(at_lon, 4) < 2
    near = jnp.where(starts_early, got[0][...], got[1][...])
    far = jnp.where(starts_early, got[2][...], got[3][...])
    return jnp.where(odd, near, far), jnp.where(odd, far, near)


def pack_rows_kernel(
    state, mix, vel, rate_in, index, weight, flux, early, late, to_early, to_late, msg0, msg1
):
    odd = lax.rem(lax.axis_index("lat"), 2) == 1
    west, east = column_messages((early, late, to_early, to_late))
    rate = rate_in[...]

    def put(x, at, width):
        head, tail = x[0:width], x[ROWS - width : ROWS]
        msg0[at : at + width] = jnp.where(odd, head, tail)
        msg1[at : at + width] = jnp.where(odd, tail, head)

    for level in range(LEV):
        put(state[level], 4 * level, 4)
    for level in range(LEV - 1):
        put(mix[level], AT_MIX + 2 * level, 2)
    for part in range(2):
        put(vel[part], AT_VEL + 2 * part, 2)
    put(rate, AT_RATE, 2)

    @pl.when(lax.axis_index("comp") == 0)
    def _():
        msg0[AT_FLUX : AT_FLUX + ROWS] = flux[...]
        msg1[AT_FLUX : AT_FLUX + ROWS] = flux[...]

    @pl.when(lax.axis_index("comp") != 0)
    def _():
        for j in range(4):
            put(weight[j], AT_WEIGHT + 2 * j, 2)
            put(index[j].astype(jnp.float32), AT_INDEX + 2 * j, 2)

    put(west[0:ROWS], AT_WEST, 4)
    put(east[0:ROWS], AT_EAST, 4)
    for at in (AT_RATE + 2, AT_RATE + 4):
        msg0[at : at + 2] = jnp.zeros((2, COLS), jnp.float32)
        msg1[at : at + 2] = jnp.zeros((2, COLS), jnp.float32)


def row_messages(got0, got1):
    odd = lax.rem(lax.axis_index("lat"), 2)
    near = got0[1 - odd]
    far = got1[...]
    return jnp.where(odd == 1, near, far), jnp.where(odd == 1, far, near)


def transport_weights(east, north):
    def weights(v):
        near, far = v * (8.0 / 12.0), v * (1.0 / 12.0)
        return (-far, smoothing + near, smoothing - near, far)

    return weights(east), weights(north)


SHIFTS = (2, 1, -1, -2)


def along_longitude(own, side, weights):
    lane = lanes(own.shape[0])
    result = own * (1.0 - 4.0 * smoothing)
    for shift, factor in zip(SHIFTS, weights[0]):
        cut = lane >= COLS - shift if shift > 0 else lane < -shift
        result = result + factor * roll(jnp.where(cut, side, own), shift, 1)
    return result


def along_latitude(own, weights, rows):
    result = None
    for shift, factor in zip(SHIFTS, weights[1]):
        tap = factor * roll(own, shift, 0)[:rows]
        result = tap if result is None else result + tap
    return result


def factors(mix):
    inverses, ratios = [], []
    for level in range(LEV):
        pivot = 1.0
        if level < LEV - 1:
            pivot = pivot + mix[level]
        if level > 0:
            pivot = pivot + mix[level - 1] * (1.0 - ratios[-1])
        inverse = 1.0 / pivot
        inverses.append(inverse)
        if level < LEV - 1:
            ratios.append(mix[level] * inverse)
    return inverses, ratios


def solve(rhs, mix, inverses, ratios):
    values = []
    for level in range(LEV):
        source = rhs[level]
        if level > 0:
            source = mix[level - 1] * values[-1] if source is None else source + mix[level - 1] * values[-1]
        values.append(source * inverses[level])
    result = [None] * LEV
    result[-1] = values[-1]
    for level in range(LEV - 2, -1, -1):
        result[level] = values[level] + ratios[level] * result[level + 1]
    return result


def rim_of_levels(north, south, level):
    sub, block, odd = sublanes(), 8 * (level // 2), level % 2
    a, b = south[block : block + 8], north[block : block + 8]
    return jnp.where(sub < 4, roll(a, -4 * odd, 0), roll(b, 4 - 4 * odd, 0))


def side_of(west_tile, east_tile, at, width, rows):
    lane = lanes(rows)
    a, b = roll(east_tile[:rows], -at, 1), roll(west_tile[:rows], COLS - width - at, 1)
    return jnp.where(lane < width, a, jnp.where(lane >= COLS - width, b, 0.0))


IMPULSE = [1.0] + [None] * (LEV - 1)


def prepare_own_kernel(prev, mix, index, weight, inverse, unit, seen):
    own_mix = [mix[level] for level in range(LEV - 1)]
    inverses, ratios = factors(own_mix)
    impulse = solve(IMPULSE, own_mix, inverses, ratios)
    for level in range(LEV):
        inverse[level] = inverses[level]
        unit[level] = impulse[level]

    @pl.when(lax.axis_index("comp") == 0)
    def _():
        seen[...] = regrid_tile(prev[1], index, weight)


def prepare_side_kernel(
    state, vel, early, late, to_early, to_late,
    inverse, unit, side_mix, side_state, lon_own, lon_side,
):
    west, east = column_messages((early, late, to_early, to_late))
    own_weights = transport_weights(vel[0], vel[1])
    side_weights = transport_weights(
        *(side_of(west, east, AT_VEL + 2 * part, 2, ROWS) for part in range(2))
    )
    for level in range(LEV):
        there = side_of(west, east, 4 * level, 4, ROWS)
        side_state[level] = there
        lon_own[level] = along_longitude(state[level], there, own_weights)
        lon_side[level] = along_longitude(there, state[level], side_weights)
    mixes = [side_of(west, east, AT_MIX + 2 * level, 2, ROWS) for level in range(LEV - 1)]
    inverses, ratios = factors(mixes)
    impulse = solve(IMPULSE, mixes, inverses, ratios)
    for level in range(LEV):
        inverse[level] = inverses[level]
        unit[level] = impulse[level]
        if level < LEV - 1:
            side_mix[level] = mixes[level]


def stored(inverse, mixes):
    inverses = [inverse[level] for level in range(LEV)]
    return inverses, [mixes[level] * inverses[level] for level in range(LEV - 1)]


def top_step(state, mix, vel, rate, flux, columns, rows, inverse, unit, seen, lon_own, fluxes):
    west, east = column_messages(columns)
    north, south = row_messages(*rows)
    weights = transport_weights(vel[0], vel[1])
    moved = []
    for level in range(LEV):
        own = jnp.concatenate([state[level], rim_of_levels(north, south, level)], axis=0)
        moved.append(lon_own[level] + along_latitude(own, weights, ROWS))
    own_mix = [mix[level] for level in range(LEV - 1)]
    top = solve(moved, own_mix, *stored(inverse, own_mix))[0] + flux[...] * unit[0]
    fluxes[0:ROWS] = flux[...]
    fluxes[ROWS : 2 * ROWS] = west[ROWS:]
    fluxes[2 * ROWS : 3 * ROWS] = east[ROWS:]
    fluxes[3 * ROWS : 4 * ROWS] = north[AT_FLUX : AT_FLUX + ROWS]
    fluxes[4 * ROWS : 5 * ROWS] = south[AT_FLUX : AT_FLUX + ROWS]
    fluxes[5 * ROWS :] = rate[...] * (seen[...] - top)


def halo_step(state, mix, vel, columns, rows, inverse, side, before, before_side, unit_rim):
    west, east = column_messages(columns)
    north, south = row_messages(*rows)
    at_lat = lax.axis_index("lat")
    sub = sublanes()
    valid = ((sub < 4) & (at_lat < lax.axis_size("lat") - 1)) | ((sub >= 4) & (at_lat > 0))

    def rim2(at):
        block, offset = 8 * (at // 8), at % 8
        a, b = south[block : block + 8], north[block : block + 8]
        a, b = roll(a, -offset, 0), roll(b, 6 - offset, 0)
        return jnp.where(sub < 2, a, jnp.where(sub >= 6, b, 0.0))

    inverse_side, side_mix_ref, side_state, lon_own, lon_side = side
    a, b = south[AT_WEST : AT_WEST + 8], north[AT_WEST : AT_WEST + 8]
    west_rim = jnp.where(sub < 4, a, roll(b, 4, 0))
    east_rim = jnp.where(sub < 4, roll(a, 4, 0), b)
    own_mix = [mix[level] for level in range(LEV - 1)]
    side_mix = [side_mix_ref[level] for level in range(LEV - 1)]
    rim_mix = [rim2(AT_MIX + 2 * level) for level in range(LEV - 1)]
    rim_vel = [rim2(AT_VEL + 2 * part) for part in range(2)]
    own_weights = transport_weights(
        *(jnp.concatenate([vel[part], rim_vel[part]], axis=0) for part in range(2))
    )
    rim_weights = transport_weights(*rim_vel)
    side_weights = transport_weights(
        *(side_of(west, east, AT_VEL + 2 * part, 2, ROWS) for part in range(2))
    )
    rim_factors = factors(rim_mix)
    moved, moved_rim, moved_side = [], [], []
    for level in range(LEV):
        rim = rim_of_levels(north, south, level)
        side_rim = side_of(west_rim, east_rim, 4 * level, 4, 8)
        taps = along_latitude(jnp.concatenate([state[level], rim], axis=0), own_weights, 24)
        moved.append(lon_own[level] + taps[:ROWS])
        moved_rim.append(along_longitude(rim, side_rim, rim_weights) + taps[ROWS:])
        there = jnp.concatenate([side_state[level], side_rim], axis=0)
        moved_side.append(lon_side[level] + along_latitude(there, side_weights, ROWS))
    rim = solve(moved_rim, rim_mix, *rim_factors)
    impulse = solve(IMPULSE, rim_mix, *rim_factors)
    own = solve(moved, own_mix, *stored(inverse, own_mix))
    there = solve(moved_side, side_mix, *stored(inverse_side, side_mix))
    for level in range(LEV):
        before[level, 0:ROWS] = own[level]
        before[level, ROWS:] = jnp.where(valid, rim[level], 0.0)
        before_side[level] = there[level]
        unit_rim[level] = jnp.where(valid, impulse[level], 0.0)


def middle_kernel(
    state, mix, vel, rate, flux, early, late, to_early, to_late, row0, row1,
    inverse, unit, seen, inverse_side, side_mix, side_state, lon_own, lon_side,
    fluxes, before, before_side, unit_rim,
):
    columns, rows = (early, late, to_early, to_late), (row0, row1)
    side = (inverse_side, side_mix, side_state, lon_own, lon_side)

    @pl.when(lax.axis_index("comp") == 0)
    def _():
        top_step(state, mix, vel, rate, flux, columns, rows, inverse, unit, seen, lon_own, fluxes)

    @pl.when(lax.axis_index("comp") != 0)
    def _():
        halo_step(state, mix, vel, columns, rows, inverse, side, before, before_side, unit_rim)


def second_step_kernel(
    state, mix, vel, rate_in, index, weight, early, late, to_early, to_late, row0, row1,
    inverse, unit, inverse_side, side_mix, side_state, lon_own, lon_side, unit_side,
    given_before, given_side, given_rim, got,
    new_state, series, own_before, own_side, own_rim,
):
    columns, rows = (early, late, to_early, to_late), (row0, row1)
    sub = sublanes()
    lane = lanes(ROWS)
    tables = [got[0, k * ROWS : (k + 1) * ROWS] for k in range(6)]
    own_mix = [mix[level] for level in range(LEV - 1)]

    def advance(force, force_rim, force_side, force1, before, before_side, unit_rim):
        weights = transport_weights(vel[0], vel[1])
        moved = []
        for level in range(LEV):
            tile = before[level, 0:ROWS] + force * unit[level]
            rim = before[level, ROWS:] + force_rim * unit_rim[level]
            there = before_side[level] + force_side * unit_side[level]
            if level == 0:
                top = tile
            own = jnp.concatenate([tile, rim], axis=0)
            taps = along_latitude(own, weights, ROWS)
            moved.append(along_longitude(tile, there, weights) + taps)
        moved[0] = moved[0] + force1
        solved = solve(moved, own_mix, *stored(inverse, own_mix))
        for level in range(LEV):
            new_state[level] = solved[level]
        return top, solved[0]

    @pl.when(lax.axis_index("comp") == 0)
    def _():
        side = (inverse_side, side_mix, side_state, lon_own, lon_side)
        halo_step(state, mix, vel, columns, rows, inverse, side, own_before, own_side, own_rim)
        rim = jnp.where(sub < 4, tables[4][0:8], tables[3][8:16])
        side = jnp.where(lane < 64, tables[2], tables[1])
        advance(tables[0], rim, side, tables[5], own_before, own_side, own_rim)
        series[0] = tables[0]
        series[1] = tables[5]

    @pl.when(lax.axis_index("comp") != 0)
    def _():
        rate = rate_in[...]
        west, east = column_messages(columns)
        north, south = row_messages(*rows)

        def of_rows(message, table, place):
            index8 = message[AT_INDEX : AT_INDEX + 8].astype(jnp.int32)
            total = gather_cells(table, index8) * message[AT_WEIGHT : AT_WEIGHT + 8]
            total = total + roll(total, 4, 0)
            total = total + roll(total, 2, 0)
            block, offset = 8 * (AT_RATE // 8), AT_RATE % 8
            return roll(message[block : block + 8], place - offset, 0) * roll(total, place, 0)

        def of_columns(message, table, place):
            tile = message[0:ROWS]
            total = roll(gather_cells(table, tile.astype(jnp.int32)), AT_WEIGHT - AT_INDEX, 1) * tile
            total = total + roll(total, -4, 1)
            total = total + roll(total, -2, 1)
            return roll(tile, place - AT_RATE, 1) * roll(total, place - AT_WEIGHT, 1)

        rim = jnp.where(sub < 4, of_rows(south, tables[4], 0), of_rows(north, tables[3], 6))
        side = jnp.where(
            lane < 64, of_columns(east, tables[2], 0), of_columns(west, tables[1], COLS - 2)
        )
        force = rate * regrid_tile(tables[0], index, weight)
        force1 = rate * regrid_tile(tables[5], index, weight)
        top, last = advance(force, rim, side, force1, given_before, given_side, given_rim)
        series[0] = top
        series[1] = last


def call(kernel, shapes, *args, scratch=(), place=pltpu.VMEM):
    return pl.pallas_call(
        kernel,
        out_shape=[s if hasattr(s, "dtype") else jax.ShapeDtypeStruct(s, jnp.float32) for s in shapes],
        in_specs=[pl.BlockSpec(memory_space=place)] * len(args),
        out_specs=[pl.BlockSpec(memory_space=pltpu.VMEM)] * len(shapes),
        scratch_shapes=list(scratch),
        compiler_params=pltpu.CompilerParams(vmem_limit_bytes=16 * 1024 * 1024),
        interpret=INTERPRET,
    )(*args)


def pairs(count, start, step):
    return [pair for i in range(start, count - 1, step) for pair in ((i, i + 1), (i + 1, i))]


def partners(count):
    return [[i, i + 1] for i in range(0, count, 2)]


def per_device(
    state, prev_surface, mixing, velocity, coupling, sea_mask, interp_index, interp_weight
):
    n_lat, n_lon = lax.axis_size("lat"), lax.axis_size("lon")
    given = (
        state[0], prev_surface, mixing[0], velocity[0],
        coupling[0], sea_mask[0], interp_index[0], interp_weight[0],
    )
    state, prev, mix, vel, couple, mask, index, weight = given
    tile = (ROWS, COLS)
    column_shape = (COL_MESSAGE, COLS)
    to_near, to_far, flux, rate, state, prev, mix, vel, index, weight = call(
        pack_columns_kernel,
        [column_shape, column_shape, tile, tile, state, prev, mix, vel, index, weight],
        *(pltpu.with_memory_space_constraint(x, pltpu.HBM) for x in given), place=pltpu.HBM,
        scratch=[pltpu.VMEM(tile, couple.dtype), pltpu.VMEM(tile, mask.dtype), pltpu.SemaphoreType.DMA((8,))],
    )
    joints = range(1, n_lon, 2)
    sent = [((i, (i + 1) % n_lon) if i % 4 == 3 else (i + 1, i)) for i in joints]
    to_early = lax.ppermute(to_far, "lon", sent)
    early = lax.ppermute(to_near, "lon", pairs(n_lon, 0, 4))
    to_late = lax.ppermute(to_far, "lon", [(j, i) for i, j in sent])
    late = lax.ppermute(to_near, "lon", pairs(n_lon, 2, 4))
    columns = (early, late, to_early, to_late)
    row_shape = (ROW_MESSAGE, COLS)
    to_near, to_far = call(
        pack_rows_kernel, [row_shape, row_shape],
        state, mix, vel, rate, index, weight, flux, *columns,
    )
    row1 = lax.ppermute(to_far, "lat", pairs(n_lat, 1, 2))
    row0 = lax.all_gather(to_near, "lat", axis_index_groups=partners(n_lat))
    rows = (row0, row1)
    narrow = (LEV, ROWS, COLS)
    parts = [(LEV, 24, COLS), narrow, (LEV, 8, COLS)]
    inverse, unit, seen = call(prepare_own_kernel, [narrow, narrow, tile], prev, mix, index, weight)
    inverse_side, unit_side, *side = call(
        prepare_side_kernel,
        [narrow, narrow, (LEV - 1, ROWS, COLS), narrow, narrow, narrow], state, vel, *columns,
    )
    known = (inverse_side, *side)
    fluxes, *before = call(
        middle_kernel, [(6 * ROWS, COLS)] + parts,
        state, mix, vel, rate, flux, *columns, *rows, inverse, unit, seen, *known,
    )
    got = lax.all_gather(fluxes, "comp")
    new_state, series = call(
        second_step_kernel, [narrow, (NSTEP, ROWS, COLS)],
        state, mix, vel, rate, index, weight, *columns, *rows,
        inverse, unit, *known, unit_side, *before, got,
        scratch=[pltpu.VMEM(shape, jnp.float32) for shape in parts],
    )
    return new_state[None], series[None]


def solution(mesh):
    in_specs = (
        P("comp", None, "lat", "lon"),
        P(None, "lat", "lon"),
        P("comp", None, "lat", "lon"),
        P("comp", None, "lat", "lon"),
        P("comp", "lat", "lon"),
        P("comp", "lat", "lon"),
        P("comp", None, "lat", "lon"),
        P("comp", None, "lat", "lon"),
    )
    out_specs = (P("comp", None, "lat", "lon"), P("comp", None, "lat", "lon"))

    return jax.shard_map(
        per_device, mesh=mesh, in_specs=in_specs, out_specs=out_specs, check_vma=False
    )
```

```python
import jax
import jax.numpy as jnp
from jax import lax
from jax.experimental import pallas as pl
from jax.experimental.pallas import tpu as pltpu
from jax.sharding import PartitionSpec as P


INTERPRET = False
NSTEP = 2
LEV = 12
ROWS = 16
COLS = 128
smoothing = 0.15

AT_MIX = 4 * LEV
AT_VEL = AT_MIX + 2 * (LEV - 1)
AT_RATE = AT_VEL + 4
AT_WEIGHT = 80
AT_INDEX = 88
AT_FLUX = AT_WEIGHT
AT_WEST = 96
AT_EAST = 100
ROW_MESSAGE = 104
COL_MESSAGE = 2 * ROWS


def lanes(rows):
    return lax.broadcasted_iota(jnp.int32, (rows, COLS), 1)


def sublanes():
    return lax.broadcasted_iota(jnp.int32, (8, COLS), 0)


def roll(x, shift, axis):
    shift %= x.shape[axis]
    return pltpu.roll(x, shift, axis) if shift else x


def gather_cells(table, index):
    sources = [jnp.broadcast_to(table[r : r + 1], (8, COLS)) for r in range(ROWS)]
    blocks = []
    for at in range(0, index.shape[0], 8):
        cell = index[at : at + 8]
        column = lax.bitwise_and(cell, COLS - 1)
        picked = [
            jnp.take_along_axis(source, column, axis=1, mode="promise_in_bounds")
            for source in sources
        ]
        bit = COLS
        while len(picked) > 1:
            chosen = lax.bitwise_and(cell, bit) != 0
            picked = [jnp.where(chosen, b, a) for a, b in zip(picked[::2], picked[1::2])]
            bit *= 2
        blocks.append(picked[0])
    return jnp.concatenate(blocks, axis=0)


def regrid_tile(table, index_ref, weight_ref):
    index = index_ref[...].reshape(4 * ROWS, COLS)
    picked = gather_cells(table, index).reshape(4, ROWS, COLS)
    return jnp.sum(picked * weight_ref[...], axis=0)


def pack_columns_kernel(
    state_hbm, prev_hbm, mix_hbm, vel_hbm, couple_hbm, mask_hbm, index_hbm, weight_hbm,
    msg0, msg1, flux_out, rate_out, state, prev, mix, vel, index, weight, couple, mask, arrived,
):
    moves = [
        pltpu.make_async_copy(source, target, arrived.at[k])
        for k, (source, target) in enumerate(
            (
                (index_hbm, index),
                (prev_hbm, prev),
                (weight_hbm, weight),
                (state_hbm, state),
                (mix_hbm, mix),
                (vel_hbm, vel),
                (couple_hbm, couple),
                (mask_hbm, mask),
            )
        )
    ]
    for move in moves:
        move.start()
    is_atmosphere = lax.axis_index("comp") == 0
    odd = lax.rem(lax.axis_index("lon"), 2) == 1
    lane = lanes(ROWS)
    for move in moves[:3]:
        move.wait()

    @pl.when(is_atmosphere)
    def _():
        flux_out[...] = regrid_tile(prev[0], index, weight)

    for move in moves[3:]:
        move.wait()
    rate = couple[...] * mask[...].astype(jnp.float32)
    rate_out[...] = rate

    def packed(last):
        total = jnp.zeros((ROWS, COLS), jnp.float32)

        def put(total, x, at, width):
            shift = at - (COLS - width) if last else at
            return jnp.where((lane >= at) & (lane < at + width), roll(x, shift, 1), total)

        for level in range(LEV):
            total = put(total, state[level], 4 * level, 4)
        for level in range(LEV - 1):
            total = put(total, mix[level], AT_MIX + 2 * level, 2)
        for part in range(2):
            total = put(total, vel[part], AT_VEL + 2 * part, 2)
        total = put(total, rate, AT_RATE, 2)
        for j in range(4):
            total = put(total, weight[j], AT_WEIGHT + 2 * j, 2)
            total = put(total, index[j].astype(jnp.float32), AT_INDEX + 2 * j, 2)
        return total

    first, last = packed(False), packed(True)
    msg0[0:ROWS] = jnp.where(odd, first, last)
    msg1[0:ROWS] = jnp.where(odd, last, first)

    @pl.when(is_atmosphere)
    def _():
        flux = rate * (flux_out[...] - state[0])
        flux_out[...] = flux
        msg0[ROWS:] = flux
        msg1[ROWS:] = flux

    @pl.when(jnp.logical_not(is_atmosphere))
    def _():
        nothing = jnp.zeros((ROWS, COLS), jnp.float32)
        flux_out[...] = nothing
        msg0[ROWS:] = nothing
        msg1[ROWS:] = nothing


def starts_early():
    return lax.rem(lax.axis_index("lon"), 4) < 2


def sides(near, far):
    odd = lax.rem(lax.axis_index("lon"), 2) == 1
    return jnp.where(odd, near, far), jnp.where(odd, far, near)


def column_messages(got):
    early = starts_early()
    near = jnp.where(early, got[0][...], got[1][...])
    return sides(near, jnp.where(early, got[2][...], got[3][...]))


def pack_rows_kernel(
    state, mix, vel, rate_in, index, weight, flux, early, late, to_early, to_late, msg0, msg1
):
    odd = lax.rem(lax.axis_index("lat"), 2) == 1
    west, east = column_messages((early, late, to_early, to_late))
    rate = rate_in[...]

    def put(x, at, width):
        head, tail = x[0:width], x[ROWS - width : ROWS]
        msg0[at : at + width] = jnp.where(odd, head, tail)
        msg1[at : at + width] = jnp.where(odd, tail, head)

    for level in range(LEV):
        put(state[level], 4 * level, 4)
    for level in range(LEV - 1):
        put(mix[level], AT_MIX + 2 * level, 2)
    for part in range(2):
        put(vel[part], AT_VEL + 2 * part, 2)
    put(rate, AT_RATE, 2)

    @pl.when(lax.axis_index("comp") == 0)
    def _():
        msg0[AT_FLUX : AT_FLUX + ROWS] = flux[...]
        msg1[AT_FLUX : AT_FLUX + ROWS] = flux[...]

    @pl.when(lax.axis_index("comp") != 0)
    def _():
        for j in range(4):
            put(weight[j], AT_WEIGHT + 2 * j, 2)
            put(index[j].astype(jnp.float32), AT_INDEX + 2 * j, 2)

    put(west[0:ROWS], AT_WEST, 4)
    put(east[0:ROWS], AT_EAST, 4)
    for at in (AT_RATE + 2, AT_RATE + 4):
        msg0[at : at + 2] = jnp.zeros((2, COLS), jnp.float32)
        msg1[at : at + 2] = jnp.zeros((2, COLS), jnp.float32)


def row_messages(got0, got1):
    odd = lax.rem(lax.axis_index("lat"), 2)
    near = got0[1 - odd]
    far = got1[...]
    return jnp.where(odd == 1, near, far), jnp.where(odd == 1, far, near)


def transport_weights(east, north):
    def weights(v):
        near, far = v * (8.0 / 12.0), v * (1.0 / 12.0)
        return (-far, smoothing + near, smoothing - near, far)

    return weights(east), weights(north)


SHIFTS = (2, 1, -1, -2)


def along_longitude(own, side, weights):
    lane = lanes(own.shape[0])
    result = own * (1.0 - 4.0 * smoothing)
    for shift, factor in zip(SHIFTS, weights[0]):
        cut = lane >= COLS - shift if shift > 0 else lane < -shift
        result = result + factor * roll(jnp.where(cut, side, own), shift, 1)
    return result


def along_latitude(own, weights, rows):
    result = None
    for shift, factor in zip(SHIFTS, weights[1]):
        tap = factor * roll(own, shift, 0)[:rows]
        result = tap if result is None else result + tap
    return result


def factors(mix):
    inverses, ratios = [], []
    for level in range(LEV):
        pivot = 1.0
        if level < LEV - 1:
            pivot = pivot + mix[level]
        if level > 0:
            pivot = pivot + mix[level - 1] * (1.0 - ratios[-1])
        inverse = 1.0 / pivot
        inverses.append(inverse)
        if level < LEV - 1:
            ratios.append(mix[level] * inverse)
    return inverses, ratios


def solve(rhs, mix, inverses, ratios):
    values = []
    for level in range(LEV):
        source = rhs[level]
        if level > 0:
            source = mix[level - 1] * values[-1] if source is None else source + mix[level - 1] * values[-1]
        values.append(source * inverses[level])
    result = [None] * LEV
    result[-1] = values[-1]
    for level in range(LEV - 2, -1, -1):
        result[level] = values[level] + ratios[level] * result[level + 1]
    return result


def rim_of_levels(north, south, level):
    sub, block, odd = sublanes(), 8 * (level // 2), level % 2
    a, b = south[block : block + 8], north[block : block + 8]
    return jnp.where(sub < 4, roll(a, -4 * odd, 0), roll(b, 4 - 4 * odd, 0))


def side_of(west_tile, east_tile, at, width, rows):
    lane = lanes(rows)
    a, b = roll(east_tile[:rows], -at, 1), roll(west_tile[:rows], COLS - width - at, 1)
    return jnp.where(lane < width, a, jnp.where(lane >= COLS - width, b, 0.0))


IMPULSE = [1.0] + [None] * (LEV - 1)


def prepare_own_kernel(prev, mix, index, weight, inverse, unit, seen):
    own_mix = [mix[level] for level in range(LEV - 1)]
    inverses, ratios = factors(own_mix)
    impulse = solve(IMPULSE, own_mix, inverses, ratios)
    for level in range(LEV):
        inverse[level] = inverses[level]
        unit[level] = impulse[level]

    @pl.when(lax.axis_index("comp") == 0)
    def _():
        seen[...] = regrid_tile(prev[1], index, weight)


def prepare_side(
    state, vel, near, far, inverse, unit, side_mix, side_state, lon_own, lon_side
):
    west, east = sides(near[0:ROWS], far[0:ROWS])
    own_weights = transport_weights(vel[0], vel[1])
    side_weights = transport_weights(
        *(side_of(west, east, AT_VEL + 2 * part, 2, ROWS) for part in range(2))
    )
    for level in range(LEV):
        there = side_of(west, east, 4 * level, 4, ROWS)
        side_state[level] = there
        lon_own[level] = along_longitude(state[level], there, own_weights)
        lon_side[level] = along_longitude(there, state[level], side_weights)
    mixes = [side_of(west, east, AT_MIX + 2 * level, 2, ROWS) for level in range(LEV - 1)]
    inverses, ratios = factors(mixes)
    impulse = solve(IMPULSE, mixes, inverses, ratios)
    for level in range(LEV):
        inverse[level] = inverses[level]
        unit[level] = impulse[level]
        if level < LEV - 1:
            side_mix[level] = mixes[level]


def side_early_kernel(state, vel, near, far, *out):
    @pl.when(starts_early())
    def _():
        prepare_side(state, vel, near, far, *out)


def side_late_kernel(state, vel, near, far, *both):
    @pl.when(jnp.logical_not(starts_early()))
    def _():
        prepare_side(state, vel, near, far, *both[len(both) // 2 :])


def stored(inverse, mixes):
    inverses = [inverse[level] for level in range(LEV)]
    return inverses, [mixes[level] * inverses[level] for level in range(LEV - 1)]


def top_step(state, mix, vel, rate, flux, columns, rows, inverse, unit, seen, lon_own, fluxes):
    west, east = column_messages(columns)
    north, south = row_messages(*rows)
    weights = transport_weights(vel[0], vel[1])
    moved = []
    for level in range(LEV):
        own = jnp.concatenate([state[level], rim_of_levels(north, south, level)], axis=0)
        moved.append(lon_own[level] + along_latitude(own, weights, ROWS))
    own_mix = [mix[level] for level in range(LEV - 1)]
    top = solve(moved, own_mix, *stored(inverse, own_mix))[0] + flux[...] * unit[0]
    fluxes[0:ROWS] = flux[...]
    fluxes[ROWS : 2 * ROWS] = west[ROWS:]
    fluxes[2 * ROWS : 3 * ROWS] = east[ROWS:]
    fluxes[3 * ROWS : 4 * ROWS] = north[AT_FLUX : AT_FLUX + ROWS]
    fluxes[4 * ROWS : 5 * ROWS] = south[AT_FLUX : AT_FLUX + ROWS]
    fluxes[5 * ROWS :] = rate[...] * (seen[...] - top)


def halo_step(state, mix, vel, columns, rows, inverse, side, before, before_side, unit_rim):
    west, east = column_messages(columns)
    north, south = row_messages(*rows)
    at_lat = lax.axis_index("lat")
    sub = sublanes()
    valid = ((sub < 4) & (at_lat < lax.axis_size("lat") - 1)) | ((sub >= 4) & (at_lat > 0))

    def rim2(at):
        block, offset = 8 * (at // 8), at % 8
        a, b = south[block : block + 8], north[block : block + 8]
        a, b = roll(a, -offset, 0), roll(b, 6 - offset, 0)
        return jnp.where(sub < 2, a, jnp.where(sub >= 6, b, 0.0))

    inverse_side, side_mix_ref, side_state, lon_own, lon_side = side
    a, b = south[AT_WEST : AT_WEST + 8], north[AT_WEST : AT_WEST + 8]
    west_rim = jnp.where(sub < 4, a, roll(b, 4, 0))
    east_rim = jnp.where(sub < 4, roll(a, 4, 0), b)
    own_mix = [mix[level] for level in range(LEV - 1)]
    side_mix = [side_mix_ref[level] for level in range(LEV - 1)]
    rim_mix = [rim2(AT_MIX + 2 * level) for level in range(LEV - 1)]
    rim_vel = [rim2(AT_VEL + 2 * part) for part in range(2)]
    own_weights = transport_weights(
        *(jnp.concatenate([vel[part], rim_vel[part]], axis=0) for part in range(2))
    )
    rim_weights = transport_weights(*rim_vel)
    side_weights = transport_weights(
        *(side_of(west, east, AT_VEL + 2 * part, 2, ROWS) for part in range(2))
    )
    rim_factors = factors(rim_mix)
    moved, moved_rim, moved_side = [], [], []
    for level in range(LEV):
        rim = rim_of_levels(north, south, level)
        side_rim = side_of(west_rim, east_rim, 4 * level, 4, 8)
        taps = along_latitude(jnp.concatenate([state[level], rim], axis=0), own_weights, 24)
        moved.append(lon_own[level] + taps[:ROWS])
        moved_rim.append(along_longitude(rim, side_rim, rim_weights) + taps[ROWS:])
        there = jnp.concatenate([side_state[level], side_rim], axis=0)
        moved_side.append(lon_side[level] + along_latitude(there, side_weights, ROWS))
    rim = solve(moved_rim, rim_mix, *rim_factors)
    impulse = solve(IMPULSE, rim_mix, *rim_factors)
    own = solve(moved, own_mix, *stored(inverse, own_mix))
    there = solve(moved_side, side_mix, *stored(inverse_side, side_mix))
    for level in range(LEV):
        before[level, 0:ROWS] = own[level]
        before[level, ROWS:] = jnp.where(valid, rim[level], 0.0)
        before_side[level] = there[level]
        unit_rim[level] = jnp.where(valid, impulse[level], 0.0)


def middle_kernel(
    state, mix, vel, rate, flux, early, late, to_early, to_late, row0, row1,
    inverse, unit, seen, inverse_side, side_mix, side_state, lon_own, lon_side,
    fluxes, before, before_side, unit_rim,
):
    columns, rows = (early, late, to_early, to_late), (row0, row1)
    side = (inverse_side, side_mix, side_state, lon_own, lon_side)

    @pl.when(lax.axis_index("comp") == 0)
    def _():
        top_step(state, mix, vel, rate, flux, columns, rows, inverse, unit, seen, lon_own, fluxes)

    @pl.when(lax.axis_index("comp") != 0)
    def _():
        halo_step(state, mix, vel, columns, rows, inverse, side, before, before_side, unit_rim)


def second_step_kernel(
    state, mix, vel, rate_in, index, weight, early, late, to_early, to_late, row0, row1,
    inverse, unit, inverse_side, side_mix, side_state, lon_own, lon_side, unit_side,
    given_before, given_side, given_rim, got,
    new_state, series, own_before, own_side, own_rim,
):
    columns, rows = (early, late, to_early, to_late), (row0, row1)
    sub = sublanes()
    lane = lanes(ROWS)
    tables = [got[0, k * ROWS : (k + 1) * ROWS] for k in range(6)]
    own_mix = [mix[level] for level in range(LEV - 1)]

    def advance(force, force_rim, force_side, force1, before, before_side, unit_rim):
        weights = transport_weights(vel[0], vel[1])
        moved = []
        for level in range(LEV):
            tile = before[level, 0:ROWS] + force * unit[level]
            rim = before[level, ROWS:] + force_rim * unit_rim[level]
            there = before_side[level] + force_side * unit_side[level]
            if level == 0:
                top = tile
            own = jnp.concatenate([tile, rim], axis=0)
            taps = along_latitude(own, weights, ROWS)
            moved.append(along_longitude(tile, there, weights) + taps)
        moved[0] = moved[0] + force1
        solved = solve(moved, own_mix, *stored(inverse, own_mix))
        for level in range(LEV):
            new_state[level] = solved[level]
        return top, solved[0]

    @pl.when(lax.axis_index("comp") == 0)
    def _():
        side = (inverse_side, side_mix, side_state, lon_own, lon_side)
        halo_step(state, mix, vel, columns, rows, inverse, side, own_before, own_side, own_rim)
        rim = jnp.where(sub < 4, tables[4][0:8], tables[3][8:16])
        side = jnp.where(lane < 64, tables[2], tables[1])
        advance(tables[0], rim, side, tables[5], own_before, own_side, own_rim)
        series[0] = tables[0]
        series[1] = tables[5]

    @pl.when(lax.axis_index("comp") != 0)
    def _():
        rate = rate_in[...]
        west, east = column_messages(columns)
        north, south = row_messages(*rows)

        def of_rows(message, table, place):
            index8 = message[AT_INDEX : AT_INDEX + 8].astype(jnp.int32)
            total = gather_cells(table, index8) * message[AT_WEIGHT : AT_WEIGHT + 8]
            total = total + roll(total, 4, 0)
            total = total + roll(total, 2, 0)
            block, offset = 8 * (AT_RATE // 8), AT_RATE % 8
            return roll(message[block : block + 8], place - offset, 0) * roll(total, place, 0)

        def of_columns(message, table, place):
            tile = message[0:ROWS]
            total = roll(gather_cells(table, tile.astype(jnp.int32)), AT_WEIGHT - AT_INDEX, 1) * tile
            total = total + roll(total, -4, 1)
            total = total + roll(total, -2, 1)
            return roll(tile, place - AT_RATE, 1) * roll(total, place - AT_WEIGHT, 1)

        rim = jnp.where(sub < 4, of_rows(south, tables[4], 0), of_rows(north, tables[3], 6))
        side = jnp.where(
            lane < 64, of_columns(east, tables[2], 0), of_columns(west, tables[1], COLS - 2)
        )
        force = rate * regrid_tile(tables[0], index, weight)
        force1 = rate * regrid_tile(tables[5], index, weight)
        top, last = advance(force, rim, side, force1, given_before, given_side, given_rim)
        series[0] = top
        series[1] = last


def call(kernel, shapes, *args, scratch=(), place=pltpu.VMEM, aliases=None):
    return pl.pallas_call(
        kernel,
        out_shape=[s if hasattr(s, "dtype") else jax.ShapeDtypeStruct(s, jnp.float32) for s in shapes],
        in_specs=[pl.BlockSpec(memory_space=place)] * len(args),
        out_specs=[pl.BlockSpec(memory_space=pltpu.VMEM)] * len(shapes),
        scratch_shapes=list(scratch),
        compiler_params=pltpu.CompilerParams(vmem_limit_bytes=16 * 1024 * 1024),
        input_output_aliases=aliases or {},
        interpret=INTERPRET,
    )(*args)


def pairs(count, start, step):
    return [pair for i in range(start, count - 1, step) for pair in ((i, i + 1), (i + 1, i))]


def partners(count):
    return [[i, i + 1] for i in range(0, count, 2)]


def per_device(
    state, prev_surface, mixing, velocity, coupling, sea_mask, interp_index, interp_weight
):
    n_lat, n_lon = lax.axis_size("lat"), lax.axis_size("lon")
    given = (
        state[0], prev_surface, mixing[0], velocity[0],
        coupling[0], sea_mask[0], interp_index[0], interp_weight[0],
    )
    state, prev, mix, vel, couple, mask, index, weight = given
    tile = (ROWS, COLS)
    column_shape = (COL_MESSAGE, COLS)
    to_near, to_far, flux, rate, state, prev, mix, vel, index, weight = call(
        pack_columns_kernel,
        [column_shape, column_shape, tile, tile, state, prev, mix, vel, index, weight],
        *(pltpu.with_memory_space_constraint(x, pltpu.HBM) for x in given), place=pltpu.HBM,
        scratch=[pltpu.VMEM(tile, couple.dtype), pltpu.VMEM(tile, mask.dtype), pltpu.SemaphoreType.DMA((8,))],
    )
    joints = range(1, n_lon, 2)
    sent = [((i, (i + 1) % n_lon) if i % 4 == 3 else (i + 1, i)) for i in joints]
    to_early = lax.ppermute(to_far, "lon", sent)
    early = lax.ppermute(to_near, "lon", pairs(n_lon, 0, 4))
    to_late = lax.ppermute(to_far, "lon", [(j, i) for i, j in sent])
    late = lax.ppermute(to_near, "lon", pairs(n_lon, 2, 4))
    columns = (early, late, to_early, to_late)
    row_shape = (ROW_MESSAGE, COLS)
    to_near, to_far = call(
        pack_rows_kernel, [row_shape, row_shape],
        state, mix, vel, rate, index, weight, flux, *columns,
    )
    row1 = lax.ppermute(to_far, "lat", pairs(n_lat, 1, 2))
    row0 = lax.all_gather(to_near, "lat", axis_index_groups=partners(n_lat))
    rows = (row0, row1)
    narrow = (LEV, ROWS, COLS)
    parts = [(LEV, 24, COLS), narrow, (LEV, 8, COLS)]
    inverse, unit, seen = call(prepare_own_kernel, [narrow, narrow, tile], prev, mix, index, weight)
    shapes = [narrow, narrow, (LEV - 1, ROWS, COLS), narrow, narrow, narrow]
    side = call(side_early_kernel, shapes, state, vel, early, to_early)
    inverse_side, unit_side, *side = call(
        side_late_kernel, shapes, state, vel, late, to_late, *side,
        aliases={4 + k: k for k in range(len(shapes))},
    )
    known = (inverse_side, *side)
    fluxes, *before = call(
        middle_kernel, [(6 * ROWS, COLS)] + parts,
        state, mix, vel, rate, flux, *columns, *rows, inverse, unit, seen, *known,
    )
    got = lax.all_gather(fluxes, "comp")
    new_state, series = call(
        second_step_kernel, [narrow, (NSTEP, ROWS, COLS)],
        state, mix, vel, rate, index, weight, *columns, *rows,
        inverse, unit, *known, unit_side, *before, got,
        scratch=[pltpu.VMEM(shape, jnp.float32) for shape in parts],
    )
    return new_state[None], series[None]


def solution(mesh):
    in_specs = (
        P("comp", None, "lat", "lon"),
        P(None, "lat", "lon"),
        P("comp", None, "lat", "lon"),
        P("comp", None, "lat", "lon"),
        P("comp", "lat", "lon"),
        P("comp", "lat", "lon"),
        P("comp", None, "lat", "lon"),
        P("comp", None, "lat", "lon"),
    )
    out_specs = (P("comp", None, "lat", "lon"), P("comp", None, "lat", "lon"))

    return jax.shard_map(
        per_device, mesh=mesh, in_specs=in_specs, out_specs=out_specs, check_vma=False
    )
```

```python
import jax
import jax.numpy as jnp
from jax import lax
from jax.experimental import pallas as pl
from jax.experimental.pallas import tpu as pltpu
from jax.sharding import PartitionSpec as P


INTERPRET = False
NSTEP = 2
LEV = 12
ROWS = 16
COLS = 128
smoothing = 0.15

AT_MIX = 4 * LEV
AT_VEL = AT_MIX + 2 * (LEV - 1)
AT_RATE = AT_VEL + 4
AT_WEIGHT = 80
AT_INDEX = 88
AT_FLUX = AT_WEIGHT
AT_WEST = 96
AT_EAST = 100
ROW_MESSAGE = 104
COL_MESSAGE = 2 * ROWS


def lanes(rows):
    return lax.broadcasted_iota(jnp.int32, (rows, COLS), 1)


def sublanes():
    return lax.broadcasted_iota(jnp.int32, (8, COLS), 0)


def roll(x, shift, axis):
    shift %= x.shape[axis]
    return pltpu.roll(x, shift, axis) if shift else x


def gather_cells(table, index):
    sources = [jnp.broadcast_to(table[r : r + 1], (8, COLS)) for r in range(ROWS)]
    blocks = []
    for at in range(0, index.shape[0], 8):
        cell = index[at : at + 8]
        column = lax.bitwise_and(cell, COLS - 1)
        picked = [
            jnp.take_along_axis(source, column, axis=1, mode="promise_in_bounds")
            for source in sources
        ]
        bit = COLS
        while len(picked) > 1:
            chosen = lax.bitwise_and(cell, bit) != 0
            picked = [jnp.where(chosen, b, a) for a, b in zip(picked[::2], picked[1::2])]
            bit *= 2
        blocks.append(picked[0])
    return jnp.concatenate(blocks, axis=0)


def regrid_tile(table, index_ref, weight_ref):
    index = index_ref[...].reshape(4 * ROWS, COLS)
    picked = gather_cells(table, index).reshape(4, ROWS, COLS)
    return jnp.sum(picked * weight_ref[...], axis=0)


def pack_columns_kernel(
    state_hbm, prev_hbm, mix_hbm, vel_hbm, couple_hbm, mask_hbm, index_hbm, weight_hbm,
    msg0, msg1, flux_out, rate_out, state, prev, mix, vel, index, weight, couple, mask, arrived,
):
    moves = [
        pltpu.make_async_copy(source, target, arrived.at[k])
        for k, (source, target) in enumerate(
            (
                (index_hbm, index),
                (prev_hbm, prev),
                (weight_hbm, weight),
                (state_hbm, state),
                (mix_hbm, mix),
                (vel_hbm, vel),
                (couple_hbm, couple),
                (mask_hbm, mask),
            )
        )
    ]
    for move in moves:
        move.start()
    is_atmosphere = lax.axis_index("comp") == 0
    odd = lax.rem(lax.axis_index("lon"), 2) == 1
    lane = lanes(ROWS)
    for move in moves[:3]:
        move.wait()

    @pl.when(is_atmosphere)
    def _():
        flux_out[...] = regrid_tile(prev[0], index, weight)

    for move in moves[3:]:
        move.wait()
    rate = couple[...] * mask[...].astype(jnp.float32)
    rate_out[...] = rate

    def packed(last):
        total = jnp.zeros((ROWS, COLS), jnp.float32)

        def put(total, x, at, width):
            shift = at - (COLS - width) if last else at
            return jnp.where((lane >= at) & (lane < at + width), roll(x, shift, 1), total)

        for level in range(LEV):
            total = put(total, state[level], 4 * level, 4)
        for level in range(LEV - 1):
            total = put(total, mix[level], AT_MIX + 2 * level, 2)
        for part in range(2):
            total = put(total, vel[part], AT_VEL + 2 * part, 2)
        total = put(total, rate, AT_RATE, 2)
        for j in range(4):
            total = put(total, weight[j], AT_WEIGHT + 2 * j, 2)
            total = put(total, index[j].astype(jnp.float32), AT_INDEX + 2 * j, 2)
        return total

    first, last = packed(False), packed(True)
    msg0[0:ROWS] = jnp.where(odd, first, last)
    msg1[0:ROWS] = jnp.where(odd, last, first)

    @pl.when(is_atmosphere)
    def _():
        flux = rate * (flux_out[...] - state[0])
        flux_out[...] = flux
        msg0[ROWS:] = flux
        msg1[ROWS:] = flux

    @pl.when(jnp.logical_not(is_atmosphere))
    def _():
        nothing = jnp.zeros((ROWS, COLS), jnp.float32)
        flux_out[...] = nothing
        msg0[ROWS:] = nothing
        msg1[ROWS:] = nothing


def starts_early():
    return lax.rem(lax.axis_index("lon"), 4) < 2


def sides(near, far):
    odd = lax.rem(lax.axis_index("lon"), 2) == 1
    return jnp.where(odd, near, far), jnp.where(odd, far, near)


def column_messages(got):
    early = starts_early()
    near = jnp.where(early, got[0][...], got[1][...])
    return sides(near, jnp.where(early, got[2][...], got[3][...]))


def pack_rows_kernel(
    state, mix, vel, rate_in, index, weight, flux, early, late, to_early, to_late, msg0, msg1
):
    odd = lax.rem(lax.axis_index("lat"), 2) == 1
    west, east = column_messages((early, late, to_early, to_late))
    rate = rate_in[...]

    def put(x, at, width):
        head, tail = x[0:width], x[ROWS - width : ROWS]
        msg0[at : at + width] = jnp.where(odd, head, tail)
        msg1[at : at + width] = jnp.where(odd, tail, head)

    for level in range(LEV):
        put(state[level], 4 * level, 4)
    for level in range(LEV - 1):
        put(mix[level], AT_MIX + 2 * level, 2)
    for part in range(2):
        put(vel[part], AT_VEL + 2 * part, 2)
    put(rate, AT_RATE, 2)

    @pl.when(lax.axis_index("comp") == 0)
    def _():
        msg0[AT_FLUX : AT_FLUX + ROWS] = flux[...]
        msg1[AT_FLUX : AT_FLUX + ROWS] = flux[...]

    @pl.when(lax.axis_index("comp") != 0)
    def _():
        for j in range(4):
            put(weight[j], AT_WEIGHT + 2 * j, 2)
            put(index[j].astype(jnp.float32), AT_INDEX + 2 * j, 2)

    put(west[0:ROWS], AT_WEST, 4)
    put(east[0:ROWS], AT_EAST, 4)
    for at in (AT_RATE + 2, AT_RATE + 4):
        msg0[at : at + 2] = jnp.zeros((2, COLS), jnp.float32)
        msg1[at : at + 2] = jnp.zeros((2, COLS), jnp.float32)


def row_messages(got0, got1):
    odd = lax.rem(lax.axis_index("lat"), 2)
    near = got0[1 - odd]
    far = got1[...]
    return jnp.where(odd == 1, near, far), jnp.where(odd == 1, far, near)


def transport_weights(east, north):
    def weights(v):
        near, far = v * (8.0 / 12.0), v * (1.0 / 12.0)
        return (-far, smoothing + near, smoothing - near, far)

    return weights(east), weights(north)


SHIFTS = (2, 1, -1, -2)


def along_longitude(own, side, weights):
    lane = lanes(own.shape[0])
    result = own * (1.0 - 4.0 * smoothing)
    for shift, factor in zip(SHIFTS, weights[0]):
        cut = lane >= COLS - shift if shift > 0 else lane < -shift
        result = result + factor * roll(jnp.where(cut, side, own), shift, 1)
    return result


def along_latitude(own, weights, rows):
    result = None
    for shift, factor in zip(SHIFTS, weights[1]):
        tap = factor * roll(own, shift, 0)[:rows]
        result = tap if result is None else result + tap
    return result


def factors(mix):
    inverses, ratios = [], []
    for level in range(LEV):
        pivot = 1.0
        if level < LEV - 1:
            pivot = pivot + mix[level]
        if level > 0:
            pivot = pivot + mix[level - 1] * (1.0 - ratios[-1])
        inverse = 1.0 / pivot
        inverses.append(inverse)
        if level < LEV - 1:
            ratios.append(mix[level] * inverse)
    return inverses, ratios


def solve(rhs, mix, inverses, ratios):
    values = []
    for level in range(LEV):
        source = rhs[level]
        if level > 0:
            source = mix[level - 1] * values[-1] if source is None else source + mix[level - 1] * values[-1]
        values.append(source * inverses[level])
    result = [None] * LEV
    result[-1] = values[-1]
    for level in range(LEV - 2, -1, -1):
        result[level] = values[level] + ratios[level] * result[level + 1]
    return result


def rim_of_levels(north, south, level):
    sub, block, odd = sublanes(), 8 * (level // 2), level % 2
    a, b = south[block : block + 8], north[block : block + 8]
    return jnp.where(sub < 4, roll(a, -4 * odd, 0), roll(b, 4 - 4 * odd, 0))


def side_of(west_tile, east_tile, at, width, rows):
    lane = lanes(rows)
    a, b = roll(east_tile[:rows], -at, 1), roll(west_tile[:rows], COLS - width - at, 1)
    return jnp.where(lane < width, a, jnp.where(lane >= COLS - width, b, 0.0))


IMPULSE = [1.0] + [None] * (LEV - 1)


def prepare_own(prev, mix, index, weight, inverse, unit, seen):
    own_mix = [mix[level] for level in range(LEV - 1)]
    inverses, ratios = factors(own_mix)
    impulse = solve(IMPULSE, own_mix, inverses, ratios)
    for level in range(LEV):
        inverse[level] = inverses[level]
        unit[level] = impulse[level]

    @pl.when(lax.axis_index("comp") == 0)
    def _():
        seen[...] = regrid_tile(prev[1], index, weight)


def own_early_kernel(*refs):
    @pl.when(starts_early())
    def _():
        prepare_own(*refs)


def own_late_kernel(prev, mix, index, weight, *both):
    @pl.when(jnp.logical_not(starts_early()))
    def _():
        prepare_own(prev, mix, index, weight, *both[len(both) // 2 :])


def prepare_side(
    state, vel, near, far, inverse, unit, side_mix, side_state, lon_own, lon_side
):
    west, east = sides(near[0:ROWS], far[0:ROWS])
    own_weights = transport_weights(vel[0], vel[1])
    side_weights = transport_weights(
        *(side_of(west, east, AT_VEL + 2 * part, 2, ROWS) for part in range(2))
    )
    for level in range(LEV):
        there = side_of(west, east, 4 * level, 4, ROWS)
        side_state[level] = there
        lon_own[level] = along_longitude(state[level], there, own_weights)
        lon_side[level] = along_longitude(there, state[level], side_weights)
    mixes = [side_of(west, east, AT_MIX + 2 * level, 2, ROWS) for level in range(LEV - 1)]
    inverses, ratios = factors(mixes)
    impulse = solve(IMPULSE, mixes, inverses, ratios)
    for level in range(LEV):
        inverse[level] = inverses[level]
        unit[level] = impulse[level]
        if level < LEV - 1:
            side_mix[level] = mixes[level]


def side_early_kernel(state, vel, near, far, *out):
    @pl.when(starts_early())
    def _():
        prepare_side(state, vel, near, far, *out)


def side_late_kernel(state, vel, near, far, *both):
    @pl.when(jnp.logical_not(starts_early()))
    def _():
        prepare_side(state, vel, near, far, *both[len(both) // 2 :])


def stored(inverse, mixes):
    inverses = [inverse[level] for level in range(LEV)]
    return inverses, [mixes[level] * inverses[level] for level in range(LEV - 1)]


def top_step(state, mix, vel, rate, flux, columns, rows, inverse, unit, seen, lon_own, fluxes):
    west, east = column_messages(columns)
    north, south = row_messages(*rows)
    weights = transport_weights(vel[0], vel[1])
    moved = []
    for level in range(LEV):
        own = jnp.concatenate([state[level], rim_of_levels(north, south, level)], axis=0)
        moved.append(lon_own[level] + along_latitude(own, weights, ROWS))
    own_mix = [mix[level] for level in range(LEV - 1)]
    top = solve(moved, own_mix, *stored(inverse, own_mix))[0] + flux[...] * unit[0]
    fluxes[0:ROWS] = flux[...]
    fluxes[ROWS : 2 * ROWS] = west[ROWS:]
    fluxes[2 * ROWS : 3 * ROWS] = east[ROWS:]
    fluxes[3 * ROWS : 4 * ROWS] = north[AT_FLUX : AT_FLUX + ROWS]
    fluxes[4 * ROWS : 5 * ROWS] = south[AT_FLUX : AT_FLUX + ROWS]
    fluxes[5 * ROWS :] = rate[...] * (seen[...] - top)


def halo_step(state, mix, vel, columns, rows, inverse, side, before, before_side, unit_rim):
    west, east = column_messages(columns)
    north, south = row_messages(*rows)
    at_lat = lax.axis_index("lat")
    sub = sublanes()
    valid = ((sub < 4) & (at_lat < lax.axis_size("lat") - 1)) | ((sub >= 4) & (at_lat > 0))

    def rim2(at):
        block, offset = 8 * (at // 8), at % 8
        a, b = south[block : block + 8], north[block : block + 8]
        a, b = roll(a, -offset, 0), roll(b, 6 - offset, 0)
        return jnp.where(sub < 2, a, jnp.where(sub >= 6, b, 0.0))

    inverse_side, side_mix_ref, side_state, lon_own, lon_side = side
    a, b = south[AT_WEST : AT_WEST + 8], north[AT_WEST : AT_WEST + 8]
    west_rim = jnp.where(sub < 4, a, roll(b, 4, 0))
    east_rim = jnp.where(sub < 4, roll(a, 4, 0), b)
    own_mix = [mix[level] for level in range(LEV - 1)]
    side_mix = [side_mix_ref[level] for level in range(LEV - 1)]
    rim_mix = [rim2(AT_MIX + 2 * level) for level in range(LEV - 1)]
    rim_vel = [rim2(AT_VEL + 2 * part) for part in range(2)]
    own_weights = transport_weights(
        *(jnp.concatenate([vel[part], rim_vel[part]], axis=0) for part in range(2))
    )
    rim_weights = transport_weights(*rim_vel)
    side_weights = transport_weights(
        *(side_of(west, east, AT_VEL + 2 * part, 2, ROWS) for part in range(2))
    )
    rim_factors = factors(rim_mix)
    moved, moved_rim, moved_side = [], [], []
    for level in range(LEV):
        rim = rim_of_levels(north, south, level)
        side_rim = side_of(west_rim, east_rim, 4 * level, 4, 8)
        taps = along_latitude(jnp.concatenate([state[level], rim], axis=0), own_weights, 24)
        moved.append(lon_own[level] + taps[:ROWS])
        moved_rim.append(along_longitude(rim, side_rim, rim_weights) + taps[ROWS:])
        there = jnp.concatenate([side_state[level], side_rim], axis=0)
        moved_side.append(lon_side[level] + along_latitude(there, side_weights, ROWS))
    rim = solve(moved_rim, rim_mix, *rim_factors)
    impulse = solve(IMPULSE, rim_mix, *rim_factors)
    own = solve(moved, own_mix, *stored(inverse, own_mix))
    there = solve(moved_side, side_mix, *stored(inverse_side, side_mix))
    for level in range(LEV):
        before[level, 0:ROWS] = own[level]
        before[level, ROWS:] = jnp.where(valid, rim[level], 0.0)
        before_side[level] = there[level]
        unit_rim[level] = jnp.where(valid, impulse[level], 0.0)


def middle_kernel(
    state, mix, vel, rate, flux, early, late, to_early, to_late, row0, row1,
    inverse, unit, seen, inverse_side, side_mix, side_state, lon_own, lon_side,
    fluxes, before, before_side, unit_rim,
):
    columns, rows = (early, late, to_early, to_late), (row0, row1)
    side = (inverse_side, side_mix, side_state, lon_own, lon_side)

    @pl.when(lax.axis_index("comp") == 0)
    def _():
        top_step(state, mix, vel, rate, flux, columns, rows, inverse, unit, seen, lon_own, fluxes)

    halo_step(state, mix, vel, columns, rows, inverse, side, before, before_side, unit_rim)


def second_step_kernel(
    mix, vel, rate_in, index, weight, early, late, to_early, to_late, row0, row1,
    inverse, unit, unit_side, before, before_side, unit_rim, got, new_state, series,
):
    columns, rows = (early, late, to_early, to_late), (row0, row1)
    sub = sublanes()
    lane = lanes(ROWS)
    tables = [got[0, k * ROWS : (k + 1) * ROWS] for k in range(6)]
    own_mix = [mix[level] for level in range(LEV - 1)]

    def advance(force, force_rim, force_side, force1):
        weights = transport_weights(vel[0], vel[1])
        moved = []
        for level in range(LEV):
            tile = before[level, 0:ROWS] + force * unit[level]
            rim = before[level, ROWS:] + force_rim * unit_rim[level]
            there = before_side[level] + force_side * unit_side[level]
            if level == 0:
                top = tile
            own = jnp.concatenate([tile, rim], axis=0)
            taps = along_latitude(own, weights, ROWS)
            moved.append(along_longitude(tile, there, weights) + taps)
        moved[0] = moved[0] + force1
        solved = solve(moved, own_mix, *stored(inverse, own_mix))
        for level in range(LEV):
            new_state[level] = solved[level]
        return top, solved[0]

    @pl.when(lax.axis_index("comp") == 0)
    def _():
        rim = jnp.where(sub < 4, tables[4][0:8], tables[3][8:16])
        side = jnp.where(lane < 64, tables[2], tables[1])
        advance(tables[0], rim, side, tables[5])
        series[0] = tables[0]
        series[1] = tables[5]

    @pl.when(lax.axis_index("comp") != 0)
    def _():
        rate = rate_in[...]
        west, east = column_messages(columns)
        north, south = row_messages(*rows)

        def of_rows(message, table, place):
            index8 = message[AT_INDEX : AT_INDEX + 8].astype(jnp.int32)
            total = gather_cells(table, index8) * message[AT_WEIGHT : AT_WEIGHT + 8]
            total = total + roll(total, 4, 0)
            total = total + roll(total, 2, 0)
            block, offset = 8 * (AT_RATE // 8), AT_RATE % 8
            return roll(message[block : block + 8], place - offset, 0) * roll(total, place, 0)

        def of_columns(message, table, place):
            tile = message[0:ROWS]
            total = roll(gather_cells(table, tile.astype(jnp.int32)), AT_WEIGHT - AT_INDEX, 1) * tile
            total = total + roll(total, -4, 1)
            total = total + roll(total, -2, 1)
            return roll(tile, place - AT_RATE, 1) * roll(total, place - AT_WEIGHT, 1)

        rim = jnp.where(sub < 4, of_rows(south, tables[4], 0), of_rows(north, tables[3], 6))
        side = jnp.where(
            lane < 64, of_columns(east, tables[2], 0), of_columns(west, tables[1], COLS - 2)
        )
        force = rate * regrid_tile(tables[0], index, weight)
        force1 = rate * regrid_tile(tables[5], index, weight)
        top, last = advance(force, rim, side, force1)
        series[0] = top
        series[1] = last


def call(kernel, shapes, *args, scratch=(), place=pltpu.VMEM, aliases=None):
    return pl.pallas_call(
        kernel,
        out_shape=[s if hasattr(s, "dtype") else jax.ShapeDtypeStruct(s, jnp.float32) for s in shapes],
        in_specs=[pl.BlockSpec(memory_space=place)] * len(args),
        out_specs=[pl.BlockSpec(memory_space=pltpu.VMEM)] * len(shapes),
        scratch_shapes=list(scratch),
        compiler_params=pltpu.CompilerParams(vmem_limit_bytes=16 * 1024 * 1024),
        input_output_aliases=aliases or {},
        interpret=INTERPRET,
    )(*args)


def pairs(count, start, step):
    return [pair for i in range(start, count - 1, step) for pair in ((i, i + 1), (i + 1, i))]


def partners(count):
    return [[i, i + 1] for i in range(0, count, 2)]


def per_device(
    state, prev_surface, mixing, velocity, coupling, sea_mask, interp_index, interp_weight
):
    n_lat, n_lon = lax.axis_size("lat"), lax.axis_size("lon")
    given = (
        state[0], prev_surface, mixing[0], velocity[0],
        coupling[0], sea_mask[0], interp_index[0], interp_weight[0],
    )
    state, prev, mix, vel, couple, mask, index, weight = given
    tile = (ROWS, COLS)
    column_shape = (COL_MESSAGE, COLS)
    to_near, to_far, flux, rate, state, prev, mix, vel, index, weight = call(
        pack_columns_kernel,
        [column_shape, column_shape, tile, tile, state, prev, mix, vel, index, weight],
        *(pltpu.with_memory_space_constraint(x, pltpu.HBM) for x in given), place=pltpu.HBM,
        scratch=[pltpu.VMEM(tile, couple.dtype), pltpu.VMEM(tile, mask.dtype), pltpu.SemaphoreType.DMA((8,))],
    )
    joints = range(1, n_lon, 2)
    sent = [((i, (i + 1) % n_lon) if i % 4 == 3 else (i + 1, i)) for i in joints]
    to_early = lax.ppermute(to_far, "lon", sent)
    early = lax.ppermute(to_near, "lon", pairs(n_lon, 0, 4))
    narrow = (LEV, ROWS, COLS)
    own_shapes = [narrow, narrow, tile]
    own = call(own_early_kernel, own_shapes, prev, mix, index, weight)
    to_late = lax.ppermute(to_far, "lon", [(j, i) for i, j in sent])
    late = lax.ppermute(to_near, "lon", pairs(n_lon, 2, 4))
    columns = (early, late, to_early, to_late)
    row_shape = (ROW_MESSAGE, COLS)
    to_near, to_far = call(
        pack_rows_kernel, [row_shape, row_shape],
        state, mix, vel, rate, index, weight, flux, *columns,
    )
    row1 = lax.ppermute(to_far, "lat", pairs(n_lat, 1, 2))
    row0 = lax.all_gather(to_near, "lat", axis_index_groups=partners(n_lat))
    rows = (row0, row1)
    parts = [(LEV, 24, COLS), narrow, (LEV, 8, COLS)]
    inverse, unit, seen = call(
        own_late_kernel, own_shapes, prev, mix, index, weight, *own,
        aliases={4 + k: k for k in range(len(own_shapes))},
    )
    shapes = [narrow, narrow, (LEV - 1, ROWS, COLS), narrow, narrow, narrow]
    side = call(side_early_kernel, shapes, state, vel, early, to_early)
    inverse_side, unit_side, *side = call(
        side_late_kernel, shapes, state, vel, late, to_late, *side,
        aliases={4 + k: k for k in range(len(shapes))},
    )
    known = (inverse_side, *side)
    fluxes, *before = call(
        middle_kernel, [(6 * ROWS, COLS)] + parts,
        state, mix, vel, rate, flux, *columns, *rows, inverse, unit, seen, *known,
    )
    got = lax.all_gather(fluxes, "comp")
    new_state, series = call(
        second_step_kernel, [narrow, (NSTEP, ROWS, COLS)],
        mix, vel, rate, index, weight, *columns, *rows, inverse, unit, unit_side, *before, got,
    )
    return new_state[None], series[None]


def solution(mesh):
    in_specs = (
        P("comp", None, "lat", "lon"),
        P(None, "lat", "lon"),
        P("comp", None, "lat", "lon"),
        P("comp", None, "lat", "lon"),
        P("comp", "lat", "lon"),
        P("comp", "lat", "lon"),
        P("comp", None, "lat", "lon"),
        P("comp", None, "lat", "lon"),
    )
    out_specs = (P("comp", None, "lat", "lon"), P("comp", None, "lat", "lon"))

    return jax.shard_map(
        per_device, mesh=mesh, in_specs=in_specs, out_specs=out_specs, check_vma=False
    )
```

```python
import jax
import jax.numpy as jnp
from jax import lax
from jax.experimental import pallas as pl
from jax.experimental.pallas import tpu as pltpu
from jax.sharding import PartitionSpec as P


INTERPRET = False
NSTEP = 2
LEV = 12
ROWS = 16
COLS = 128
smoothing = 0.15

AT_MIX = 4 * LEV
AT_VEL = AT_MIX + 2 * (LEV - 1)
AT_RATE = AT_VEL + 4
AT_WEIGHT = 80
AT_INDEX = 88
AT_FLUX = AT_WEIGHT
AT_WEST = 96
AT_EAST = 100
ROW_MESSAGE = 104
COL_MESSAGE = 2 * ROWS


def lanes(rows):
    return lax.broadcasted_iota(jnp.int32, (rows, COLS), 1)


def sublanes():
    return lax.broadcasted_iota(jnp.int32, (8, COLS), 0)


def roll(x, shift, axis):
    shift %= x.shape[axis]
    return pltpu.roll(x, shift, axis) if shift else x


def gather_cells(table, index):
    sources = [jnp.broadcast_to(table[r : r + 1], (8, COLS)) for r in range(ROWS)]
    blocks = []
    for at in range(0, index.shape[0], 8):
        cell = index[at : at + 8]
        column = lax.bitwise_and(cell, COLS - 1)
        picked = [
            jnp.take_along_axis(source, column, axis=1, mode="promise_in_bounds")
            for source in sources
        ]
        bit = COLS
        while len(picked) > 1:
            chosen = lax.bitwise_and(cell, bit) != 0
            picked = [jnp.where(chosen, b, a) for a, b in zip(picked[::2], picked[1::2])]
            bit *= 2
        blocks.append(picked[0])
    return jnp.concatenate(blocks, axis=0)


def regrid_tile(table, index_ref, weight_ref):
    index = index_ref[...].reshape(4 * ROWS, COLS)
    picked = gather_cells(table, index).reshape(4, ROWS, COLS)
    return jnp.sum(picked * weight_ref[...], axis=0)


def pack_columns(last, state, mix, vel, rate, index, weight, flux, msg):
    lane = lanes(ROWS)

    def packed(at_end):
        total = jnp.zeros((ROWS, COLS), jnp.float32)

        def put(total, x, at, width):
            shift = at - (COLS - width) if at_end else at
            return jnp.where((lane >= at) & (lane < at + width), roll(x, shift, 1), total)

        for level in range(LEV):
            total = put(total, state[level], 4 * level, 4)
        for level in range(LEV - 1):
            total = put(total, mix[level], AT_MIX + 2 * level, 2)
        for part in range(2):
            total = put(total, vel[part], AT_VEL + 2 * part, 2)
        total = put(total, rate[...], AT_RATE, 2)
        for j in range(4):
            total = put(total, weight[j], AT_WEIGHT + 2 * j, 2)
            total = put(total, index[j].astype(jnp.float32), AT_INDEX + 2 * j, 2)
        return total

    @pl.when(last)
    def _():
        msg[0:ROWS] = packed(True)

    @pl.when(jnp.logical_not(last))
    def _():
        msg[0:ROWS] = packed(False)

    msg[ROWS:] = flux[...]


def near_early_kernel(*refs):
    @pl.when(starts_early())
    def _():
        pack_columns(lax.rem(lax.axis_index("lon"), 2) == 0, *refs)


def near_late_kernel(*refs):
    @pl.when(jnp.logical_not(starts_early()))
    def _():
        pack_columns(lax.rem(lax.axis_index("lon"), 2) == 0, *refs)


def pack_columns_kernel(
    state_hbm, prev_hbm, mix_hbm, vel_hbm, couple_hbm, mask_hbm, index_hbm, weight_hbm,
    msg, flux_out, rate_out, state, prev, mix, vel, index, weight, couple, mask, arrived,
):
    moves = [
        pltpu.make_async_copy(source, target, arrived.at[k])
        for k, (source, target) in enumerate(
            (
                (index_hbm, index),
                (prev_hbm, prev),
                (weight_hbm, weight),
                (state_hbm, state),
                (mix_hbm, mix),
                (vel_hbm, vel),
                (couple_hbm, couple),
                (mask_hbm, mask),
            )
        )
    ]
    for move in moves:
        move.start()
    is_atmosphere = lax.axis_index("comp") == 0
    odd = lax.rem(lax.axis_index("lon"), 2) == 1
    for move in moves[:3]:
        move.wait()

    @pl.when(is_atmosphere)
    def _():
        flux_out[...] = regrid_tile(prev[0], index, weight)

    for move in moves[3:]:
        move.wait()
    rate = couple[...] * mask[...].astype(jnp.float32)
    rate_out[...] = rate


    @pl.when(is_atmosphere)
    def _():
        flux_out[...] = rate * (flux_out[...] - state[0])

    @pl.when(jnp.logical_not(is_atmosphere))
    def _():
        flux_out[...] = jnp.zeros((ROWS, COLS), jnp.float32)

    pack_columns(odd, state, mix, vel, rate_out, index, weight, flux_out, msg)


def starts_early():
    return lax.rem(lax.axis_index("lon"), 4) < 2


def sides(near, far):
    odd = lax.rem(lax.axis_index("lon"), 2) == 1
    return jnp.where(odd, near, far), jnp.where(odd, far, near)


def column_messages(got):
    early = starts_early()
    near = jnp.where(early, got[0][...], got[1][...])
    return sides(near, jnp.where(early, got[2][...], got[3][...]))


def pack_rows_kernel(
    state, mix, vel, rate_in, index, weight, flux, early, late, to_early, to_late, msg0, msg1
):
    odd = lax.rem(lax.axis_index("lat"), 2) == 1
    west, east = column_messages((early, late, to_early, to_late))
    rate = rate_in[...]

    def put(x, at, width):
        head, tail = x[0:width], x[ROWS - width : ROWS]
        msg0[at : at + width] = jnp.where(odd, head, tail)
        msg1[at : at + width] = jnp.where(odd, tail, head)

    for level in range(LEV):
        put(state[level], 4 * level, 4)
    for level in range(LEV - 1):
        put(mix[level], AT_MIX + 2 * level, 2)
    for part in range(2):
        put(vel[part], AT_VEL + 2 * part, 2)
    put(rate, AT_RATE, 2)

    @pl.when(lax.axis_index("comp") == 0)
    def _():
        msg0[AT_FLUX : AT_FLUX + ROWS] = flux[...]
        msg1[AT_FLUX : AT_FLUX + ROWS] = flux[...]

    @pl.when(lax.axis_index("comp") != 0)
    def _():
        for j in range(4):
            put(weight[j], AT_WEIGHT + 2 * j, 2)
            put(index[j].astype(jnp.float32), AT_INDEX + 2 * j, 2)

    put(west[0:ROWS], AT_WEST, 4)
    put(east[0:ROWS], AT_EAST, 4)
    for at in (AT_RATE + 2, AT_RATE + 4):
        msg0[at : at + 2] = jnp.zeros((2, COLS), jnp.float32)
        msg1[at : at + 2] = jnp.zeros((2, COLS), jnp.float32)


def row_messages(got0, got1):
    odd = lax.rem(lax.axis_index("lat"), 2)
    near = got0[1 - odd]
    far = got1[...]
    return jnp.where(odd == 1, near, far), jnp.where(odd == 1, far, near)


def transport_weights(east, north):
    def weights(v):
        near, far = v * (8.0 / 12.0), v * (1.0 / 12.0)
        return (-far, smoothing + near, smoothing - near, far)

    return weights(east), weights(north)


SHIFTS = (2, 1, -1, -2)


def along_longitude(own, side, weights):
    lane = lanes(own.shape[0])
    result = own * (1.0 - 4.0 * smoothing)
    for shift, factor in zip(SHIFTS, weights[0]):
        cut = lane >= COLS - shift if shift > 0 else lane < -shift
        result = result + factor * roll(jnp.where(cut, side, own), shift, 1)
    return result


def along_latitude(own, weights, rows):
    result = None
    for shift, factor in zip(SHIFTS, weights[1]):
        tap = factor * roll(own, shift, 0)[:rows]
        result = tap if result is None else result + tap
    return result


def factors(mix):
    inverses, ratios = [], []
    for level in range(LEV):
        pivot = 1.0
        if level < LEV - 1:
            pivot = pivot + mix[level]
        if level > 0:
            pivot = pivot + mix[level - 1] * (1.0 - ratios[-1])
        inverse = 1.0 / pivot
        inverses.append(inverse)
        if level < LEV - 1:
            ratios.append(mix[level] * inverse)
    return inverses, ratios


def solve(rhs, mix, inverses, ratios):
    values = []
    for level in range(LEV):
        source = rhs[level]
        if level > 0:
            source = mix[level - 1] * values[-1] if source is None else source + mix[level - 1] * values[-1]
        values.append(source * inverses[level])
    result = [None] * LEV
    result[-1] = values[-1]
    for level in range(LEV - 2, -1, -1):
        result[level] = values[level] + ratios[level] * result[level + 1]
    return result


def rim_of_levels(north, south, level):
    sub, block, odd = sublanes(), 8 * (level // 2), level % 2
    a, b = south[block : block + 8], north[block : block + 8]
    return jnp.where(sub < 4, roll(a, -4 * odd, 0), roll(b, 4 - 4 * odd, 0))


def side_of(west_tile, east_tile, at, width, rows):
    lane = lanes(rows)
    a, b = roll(east_tile[:rows], -at, 1), roll(west_tile[:rows], COLS - width - at, 1)
    return jnp.where(lane < width, a, jnp.where(lane >= COLS - width, b, 0.0))


IMPULSE = [1.0] + [None] * (LEV - 1)


def prepare_own(prev, mix, index, weight, inverse, unit, seen):
    own_mix = [mix[level] for level in range(LEV - 1)]
    inverses, ratios = factors(own_mix)
    impulse = solve(IMPULSE, own_mix, inverses, ratios)
    for level in range(LEV):
        inverse[level] = inverses[level]
        unit[level] = impulse[level]

    @pl.when(lax.axis_index("comp") == 0)
    def _():
        seen[...] = regrid_tile(prev[1], index, weight)


def own_early_kernel(*refs):
    @pl.when(starts_early())
    def _():
        prepare_own(*refs)


def own_late_kernel(prev, mix, index, weight, *both):
    @pl.when(jnp.logical_not(starts_early()))
    def _():
        prepare_own(prev, mix, index, weight, *both[len(both) // 2 :])


def prepare_side(
    state, vel, near, far, inverse, unit, side_mix, side_state, lon_own, lon_side
):
    west, east = sides(near[0:ROWS], far[0:ROWS])
    own_weights = transport_weights(vel[0], vel[1])
    side_weights = transport_weights(
        *(side_of(west, east, AT_VEL + 2 * part, 2, ROWS) for part in range(2))
    )
    for level in range(LEV):
        there = side_of(west, east, 4 * level, 4, ROWS)
        side_state[level] = there
        lon_own[level] = along_longitude(state[level], there, own_weights)
        lon_side[level] = along_longitude(there, state[level], side_weights)
    mixes = [side_of(west, east, AT_MIX + 2 * level, 2, ROWS) for level in range(LEV - 1)]
    inverses, ratios = factors(mixes)
    impulse = solve(IMPULSE, mixes, inverses, ratios)
    for level in range(LEV):
        inverse[level] = inverses[level]
        unit[level] = impulse[level]
        if level < LEV - 1:
            side_mix[level] = mixes[level]


def side_early_kernel(state, vel, near, far, *out):
    @pl.when(starts_early())
    def _():
        prepare_side(state, vel, near, far, *out)


def side_late_kernel(state, vel, near, far, *both):
    @pl.when(jnp.logical_not(starts_early()))
    def _():
        prepare_side(state, vel, near, far, *both[len(both) // 2 :])


def stored(inverse, mixes):
    inverses = [inverse[level] for level in range(LEV)]
    return inverses, [mixes[level] * inverses[level] for level in range(LEV - 1)]


def halo_step(state, mix, vel, columns, rows, inverse, side, before, before_side, unit_rim):
    west, east = column_messages(columns)
    north, south = row_messages(*rows)
    at_lat = lax.axis_index("lat")
    sub = sublanes()
    valid = ((sub < 4) & (at_lat < lax.axis_size("lat") - 1)) | ((sub >= 4) & (at_lat > 0))

    def rim2(at):
        block, offset = 8 * (at // 8), at % 8
        a, b = south[block : block + 8], north[block : block + 8]
        a, b = roll(a, -offset, 0), roll(b, 6 - offset, 0)
        return jnp.where(sub < 2, a, jnp.where(sub >= 6, b, 0.0))

    inverse_side, side_mix_ref, side_state, lon_own, lon_side = side
    a, b = south[AT_WEST : AT_WEST + 8], north[AT_WEST : AT_WEST + 8]
    west_rim = jnp.where(sub < 4, a, roll(b, 4, 0))
    east_rim = jnp.where(sub < 4, roll(a, 4, 0), b)
    own_mix = [mix[level] for level in range(LEV - 1)]
    side_mix = [side_mix_ref[level] for level in range(LEV - 1)]
    rim_mix = [rim2(AT_MIX + 2 * level) for level in range(LEV - 1)]
    rim_vel = [rim2(AT_VEL + 2 * part) for part in range(2)]
    own_weights = transport_weights(
        *(jnp.concatenate([vel[part], rim_vel[part]], axis=0) for part in range(2))
    )
    rim_weights = transport_weights(*rim_vel)
    side_weights = transport_weights(
        *(side_of(west, east, AT_VEL + 2 * part, 2, ROWS) for part in range(2))
    )
    rim_factors = factors(rim_mix)
    moved, moved_rim, moved_side = [], [], []
    for level in range(LEV):
        rim = rim_of_levels(north, south, level)
        side_rim = side_of(west_rim, east_rim, 4 * level, 4, 8)
        taps = along_latitude(jnp.concatenate([state[level], rim], axis=0), own_weights, 24)
        moved.append(lon_own[level] + taps[:ROWS])
        moved_rim.append(along_longitude(rim, side_rim, rim_weights) + taps[ROWS:])
        there = jnp.concatenate([side_state[level], side_rim], axis=0)
        moved_side.append(lon_side[level] + along_latitude(there, side_weights, ROWS))
    rim = solve(moved_rim, rim_mix, *rim_factors)
    impulse = solve(IMPULSE, rim_mix, *rim_factors)
    own = solve(moved, own_mix, *stored(inverse, own_mix))
    there = solve(moved_side, side_mix, *stored(inverse_side, side_mix))
    for level in range(LEV):
        before[level, 0:ROWS] = own[level]
        before[level, ROWS:] = jnp.where(valid, rim[level], 0.0)
        before_side[level] = there[level]
        unit_rim[level] = jnp.where(valid, impulse[level], 0.0)


def middle_kernel(
    state, mix, vel, rate, flux, early, late, to_early, to_late, row0, row1,
    inverse, unit, seen, inverse_side, side_mix, side_state, lon_own, lon_side,
    fluxes, before, before_side, unit_rim,
):
    columns, rows = (early, late, to_early, to_late), (row0, row1)
    side = (inverse_side, side_mix, side_state, lon_own, lon_side)

    halo_step(state, mix, vel, columns, rows, inverse, side, before, before_side, unit_rim)

    @pl.when(lax.axis_index("comp") == 0)
    def _():
        west, east = column_messages(columns)
        north, south = row_messages(*rows)
        top = before[0, 0:ROWS] + flux[...] * unit[0]
        fluxes[0:ROWS] = flux[...]
        fluxes[ROWS : 2 * ROWS] = west[ROWS:]
        fluxes[2 * ROWS : 3 * ROWS] = east[ROWS:]
        fluxes[3 * ROWS : 4 * ROWS] = north[AT_FLUX : AT_FLUX + ROWS]
        fluxes[4 * ROWS : 5 * ROWS] = south[AT_FLUX : AT_FLUX + ROWS]
        fluxes[5 * ROWS :] = rate[...] * (seen[...] - top)


def second_step_kernel(
    mix, vel, rate_in, index, weight, early, late, to_early, to_late, row0, row1,
    inverse, unit, unit_side, before, before_side, unit_rim, got, new_state, series,
):
    columns, rows = (early, late, to_early, to_late), (row0, row1)
    sub = sublanes()
    lane = lanes(ROWS)
    tables = [got[0, k * ROWS : (k + 1) * ROWS] for k in range(6)]
    own_mix = [mix[level] for level in range(LEV - 1)]

    def advance(force, force_rim, force_side, force1):
        weights = transport_weights(vel[0], vel[1])
        moved = []
        for level in range(LEV):
            tile = before[level, 0:ROWS] + force * unit[level]
            rim = before[level, ROWS:] + force_rim * unit_rim[level]
            there = before_side[level] + force_side * unit_side[level]
            if level == 0:
                top = tile
            own = jnp.concatenate([tile, rim], axis=0)
            taps = along_latitude(own, weights, ROWS)
            moved.append(along_longitude(tile, there, weights) + taps)
        moved[0] = moved[0] + force1
        solved = solve(moved, own_mix, *stored(inverse, own_mix))
        for level in range(LEV):
            new_state[level] = solved[level]
        return top, solved[0]

    @pl.when(lax.axis_index("comp") == 0)
    def _():
        rim = jnp.where(sub < 4, tables[4][0:8], tables[3][8:16])
        side = jnp.where(lane < 64, tables[2], tables[1])
        advance(tables[0], rim, side, tables[5])
        series[0] = tables[0]
        series[1] = tables[5]

    @pl.when(lax.axis_index("comp") != 0)
    def _():
        rate = rate_in[...]
        west, east = column_messages(columns)
        north, south = row_messages(*rows)

        def of_rows(message, table, place):
            index8 = message[AT_INDEX : AT_INDEX + 8].astype(jnp.int32)
            total = gather_cells(table, index8) * message[AT_WEIGHT : AT_WEIGHT + 8]
            total = total + roll(total, 4, 0)
            total = total + roll(total, 2, 0)
            block, offset = 8 * (AT_RATE // 8), AT_RATE % 8
            return roll(message[block : block + 8], place - offset, 0) * roll(total, place, 0)

        def of_columns(message, table, place):
            tile = message[0:ROWS]
            total = roll(gather_cells(table, tile.astype(jnp.int32)), AT_WEIGHT - AT_INDEX, 1) * tile
            total = total + roll(total, -4, 1)
            total = total + roll(total, -2, 1)
            return roll(tile, place - AT_RATE, 1) * roll(total, place - AT_WEIGHT, 1)

        rim = jnp.where(sub < 4, of_rows(south, tables[4], 0), of_rows(north, tables[3], 6))
        side = jnp.where(
            lane < 64, of_columns(east, tables[2], 0), of_columns(west, tables[1], COLS - 2)
        )
        force = rate * regrid_tile(tables[0], index, weight)
        force1 = rate * regrid_tile(tables[5], index, weight)
        top, last = advance(force, rim, side, force1)
        series[0] = top
        series[1] = last


def call(kernel, shapes, *args, scratch=(), place=pltpu.VMEM, aliases=None):
    return pl.pallas_call(
        kernel,
        out_shape=[s if hasattr(s, "dtype") else jax.ShapeDtypeStruct(s, jnp.float32) for s in shapes],
        in_specs=[pl.BlockSpec(memory_space=place)] * len(args),
        out_specs=[pl.BlockSpec(memory_space=pltpu.VMEM)] * len(shapes),
        scratch_shapes=list(scratch),
        compiler_params=pltpu.CompilerParams(vmem_limit_bytes=16 * 1024 * 1024),
        input_output_aliases=aliases or {},
        interpret=INTERPRET,
    )(*args)


def pairs(count, start, step):
    return [pair for i in range(start, count - 1, step) for pair in ((i, i + 1), (i + 1, i))]


def partners(count):
    return [[i, i + 1] for i in range(0, count, 2)]


def per_device(
    state, prev_surface, mixing, velocity, coupling, sea_mask, interp_index, interp_weight
):
    n_lat, n_lon = lax.axis_size("lat"), lax.axis_size("lon")
    given = (
        state[0], prev_surface, mixing[0], velocity[0],
        coupling[0], sea_mask[0], interp_index[0], interp_weight[0],
    )
    state, prev, mix, vel, couple, mask, index, weight = given
    tile = (ROWS, COLS)
    column_shape = (COL_MESSAGE, COLS)
    to_far, flux, rate, state, prev, mix, vel, index, weight = call(
        pack_columns_kernel,
        [column_shape, tile, tile, state, prev, mix, vel, index, weight],
        *(pltpu.with_memory_space_constraint(x, pltpu.HBM) for x in given), place=pltpu.HBM,
        scratch=[pltpu.VMEM(tile, couple.dtype), pltpu.VMEM(tile, mask.dtype), pltpu.SemaphoreType.DMA((8,))],
    )
    joints = range(1, n_lon, 2)
    sent = [((i, (i + 1) % n_lon) if i % 4 == 3 else (i + 1, i)) for i in joints]
    to_early = lax.ppermute(to_far, "lon", sent)
    fields = (state, mix, vel, rate, index, weight, flux)
    (to_near,) = call(near_early_kernel, [column_shape], *fields)
    early = lax.ppermute(to_near, "lon", pairs(n_lon, 0, 4))
    narrow = (LEV, ROWS, COLS)
    own_shapes = [narrow, narrow, tile]
    own = call(own_early_kernel, own_shapes, prev, mix, index, weight)
    to_late = lax.ppermute(to_far, "lon", [(j, i) for i, j in sent])
    (to_near,) = call(near_late_kernel, [column_shape], *fields)
    late = lax.ppermute(to_near, "lon", pairs(n_lon, 2, 4))
    columns = (early, late, to_early, to_late)
    row_shape = (ROW_MESSAGE, COLS)
    to_near, to_far = call(
        pack_rows_kernel, [row_shape, row_shape],
        state, mix, vel, rate, index, weight, flux, *columns,
    )
    row1 = lax.ppermute(to_far, "lat", pairs(n_lat, 1, 2))
    row0 = lax.all_gather(to_near, "lat", axis_index_groups=partners(n_lat))
    rows = (row0, row1)
    parts = [(LEV, 24, COLS), narrow, (LEV, 8, COLS)]
    inverse, unit, seen = call(
        own_late_kernel, own_shapes, prev, mix, index, weight, *own,
        aliases={4 + k: k for k in range(len(own_shapes))},
    )
    shapes = [narrow, narrow, (LEV - 1, ROWS, COLS), narrow, narrow, narrow]
    side = call(side_early_kernel, shapes, state, vel, early, to_early)
    inverse_side, unit_side, *side = call(
        side_late_kernel, shapes, state, vel, late, to_late, *side,
        aliases={4 + k: k for k in range(len(shapes))},
    )
    known = (inverse_side, *side)
    fluxes, *before = call(
        middle_kernel, [(6 * ROWS, COLS)] + parts,
        state, mix, vel, rate, flux, *columns, *rows, inverse, unit, seen, *known,
    )
    got = lax.all_gather(fluxes, "comp")
    new_state, series = call(
        second_step_kernel, [narrow, (NSTEP, ROWS, COLS)],
        mix, vel, rate, index, weight, *columns, *rows, inverse, unit, unit_side, *before, got,
    )
    return new_state[None], series[None]


def solution(mesh):
    in_specs = (
        P("comp", None, "lat", "lon"),
        P(None, "lat", "lon"),
        P("comp", None, "lat", "lon"),
        P("comp", None, "lat", "lon"),
        P("comp", "lat", "lon"),
        P("comp", "lat", "lon"),
        P("comp", None, "lat", "lon"),
        P("comp", None, "lat", "lon"),
    )
    out_specs = (P("comp", None, "lat", "lon"), P("comp", None, "lat", "lon"))

    return jax.shard_map(
        per_device, mesh=mesh, in_specs=in_specs, out_specs=out_specs, check_vma=False
    )
```

```python
import jax
import jax.numpy as jnp
from jax import lax
from jax.experimental import pallas as pl
from jax.experimental.pallas import tpu as pltpu
from jax.sharding import PartitionSpec as P


INTERPRET = False
NSTEP = 2
LEV = 12
ROWS = 16
COLS = 128
smoothing = 0.15

AT_MIX = 4 * LEV
AT_VEL = AT_MIX + 2 * (LEV - 1)
AT_RATE = AT_VEL + 4
AT_WEIGHT = 80
AT_INDEX = 88
AT_FLUX = AT_WEIGHT
AT_WEST = 96
AT_EAST = 100
ROW_MESSAGE = 104
COL_MESSAGE = 2 * ROWS


def lanes(rows):
    return lax.broadcasted_iota(jnp.int32, (rows, COLS), 1)


def sublanes():
    return lax.broadcasted_iota(jnp.int32, (8, COLS), 0)


def roll(x, shift, axis):
    shift %= x.shape[axis]
    return pltpu.roll(x, shift, axis) if shift else x


def gather_cells(table, index):
    sources = [jnp.broadcast_to(table[r : r + 1], (8, COLS)) for r in range(ROWS)]
    blocks = []
    for at in range(0, index.shape[0], 8):
        cell = index[at : at + 8]
        column = lax.bitwise_and(cell, COLS - 1)
        picked = [
            jnp.take_along_axis(source, column, axis=1, mode="promise_in_bounds")
            for source in sources
        ]
        bit = COLS
        while len(picked) > 1:
            chosen = lax.bitwise_and(cell, bit) != 0
            picked = [jnp.where(chosen, b, a) for a, b in zip(picked[::2], picked[1::2])]
            bit *= 2
        blocks.append(picked[0])
    return jnp.concatenate(blocks, axis=0)


def regrid_tile(table, index_ref, weight_ref):
    index = index_ref[...].reshape(4 * ROWS, COLS)
    picked = gather_cells(table, index).reshape(4, ROWS, COLS)
    return jnp.sum(picked * weight_ref[...], axis=0)


def pack_columns(last, state, mix, vel, rate, index, weight, flux, msg):
    lane = lanes(ROWS)

    def packed(at_end):
        total = jnp.zeros((ROWS, COLS), jnp.float32)

        def put(total, x, at, width):
            shift = at - (COLS - width) if at_end else at
            return jnp.where((lane >= at) & (lane < at + width), roll(x, shift, 1), total)

        for level in range(LEV):
            total = put(total, state[level], 4 * level, 4)
        for level in range(LEV - 1):
            total = put(total, mix[level], AT_MIX + 2 * level, 2)
        for part in range(2):
            total = put(total, vel[part], AT_VEL + 2 * part, 2)
        total = put(total, rate[...], AT_RATE, 2)
        for j in range(4):
            total = put(total, weight[j], AT_WEIGHT + 2 * j, 2)
            total = put(total, index[j].astype(jnp.float32), AT_INDEX + 2 * j, 2)
        return total

    @pl.when(last)
    def _():
        msg[0:ROWS] = packed(True)

    @pl.when(jnp.logical_not(last))
    def _():
        msg[0:ROWS] = packed(False)

    msg[ROWS:] = flux[...]


def near_early_kernel(*refs):
    @pl.when(starts_early())
    def _():
        pack_columns(lax.rem(lax.axis_index("lon"), 2) == 0, *refs)


def near_late_kernel(*refs):
    @pl.when(jnp.logical_not(starts_early()))
    def _():
        pack_columns(lax.rem(lax.axis_index("lon"), 2) == 0, *refs)


def pack_columns_kernel(
    state_hbm, prev_hbm, mix_hbm, vel_hbm, couple_hbm, mask_hbm, index_hbm, weight_hbm,
    msg, flux_out, rate_out, state, prev, mix, vel, index, weight, couple, mask, arrived,
):
    moves = [
        pltpu.make_async_copy(source, target, arrived.at[k])
        for k, (source, target) in enumerate(
            (
                (index_hbm, index),
                (prev_hbm, prev),
                (weight_hbm, weight),
                (state_hbm, state),
                (mix_hbm, mix),
                (vel_hbm, vel),
                (couple_hbm, couple),
                (mask_hbm, mask),
            )
        )
    ]
    for move in moves[3:] + moves[:3]:
        move.start()
    is_atmosphere = lax.axis_index("comp") == 0
    odd = lax.rem(lax.axis_index("lon"), 2) == 1
    for move in moves[:3]:
        move.wait()

    @pl.when(is_atmosphere)
    def _():
        flux_out[...] = regrid_tile(prev[0], index, weight)

    for move in moves[3:]:
        move.wait()
    rate = couple[...] * mask[...].astype(jnp.float32)
    rate_out[...] = rate


    @pl.when(is_atmosphere)
    def _():
        flux_out[...] = rate * (flux_out[...] - state[0])

    @pl.when(jnp.logical_not(is_atmosphere))
    def _():
        flux_out[...] = jnp.zeros((ROWS, COLS), jnp.float32)

    pack_columns(odd, state, mix, vel, rate_out, index, weight, flux_out, msg)


def starts_early():
    return lax.rem(lax.axis_index("lon"), 4) < 2


def sides(near, far):
    odd = lax.rem(lax.axis_index("lon"), 2) == 1
    return jnp.where(odd, near, far), jnp.where(odd, far, near)


def column_messages(got):
    early = starts_early()
    near = jnp.where(early, got[0][...], got[1][...])
    return sides(near, jnp.where(early, got[2][...], got[3][...]))


def pack_rows_kernel(
    state, mix, vel, rate_in, index, weight, flux, early, late, to_early, to_late, msg0, msg1
):
    odd = lax.rem(lax.axis_index("lat"), 2) == 1
    west, east = column_messages((early, late, to_early, to_late))
    rate = rate_in[...]

    def put(x, at, width):
        head, tail = x[0:width], x[ROWS - width : ROWS]
        msg0[at : at + width] = jnp.where(odd, head, tail)
        msg1[at : at + width] = jnp.where(odd, tail, head)

    for level in range(LEV):
        put(state[level], 4 * level, 4)
    for level in range(LEV - 1):
        put(mix[level], AT_MIX + 2 * level, 2)
    for part in range(2):
        put(vel[part], AT_VEL + 2 * part, 2)
    put(rate, AT_RATE, 2)

    @pl.when(lax.axis_index("comp") == 0)
    def _():
        msg0[AT_FLUX : AT_FLUX + ROWS] = flux[...]
        msg1[AT_FLUX : AT_FLUX + ROWS] = flux[...]

    @pl.when(lax.axis_index("comp") != 0)
    def _():
        for j in range(4):
            put(weight[j], AT_WEIGHT + 2 * j, 2)
            put(index[j].astype(jnp.float32), AT_INDEX + 2 * j, 2)

    put(west[0:ROWS], AT_WEST, 4)
    put(east[0:ROWS], AT_EAST, 4)
    for at in (AT_RATE + 2, AT_RATE + 4):
        msg0[at : at + 2] = jnp.zeros((2, COLS), jnp.float32)
        msg1[at : at + 2] = jnp.zeros((2, COLS), jnp.float32)


def row_messages(got0, got1):
    odd = lax.rem(lax.axis_index("lat"), 2)
    near = got0[1 - odd]
    far = got1[...]
    return jnp.where(odd == 1, near, far), jnp.where(odd == 1, far, near)


def transport_weights(east, north):
    def weights(v):
        near, far = v * (8.0 / 12.0), v * (1.0 / 12.0)
        return (-far, smoothing + near, smoothing - near, far)

    return weights(east), weights(north)


SHIFTS = (2, 1, -1, -2)


def along_longitude(own, side, weights):
    lane = lanes(own.shape[0])
    result = own * (1.0 - 4.0 * smoothing)
    for shift, factor in zip(SHIFTS, weights[0]):
        cut = lane >= COLS - shift if shift > 0 else lane < -shift
        result = result + factor * roll(jnp.where(cut, side, own), shift, 1)
    return result


def along_latitude(own, weights, rows):
    result = None
    for shift, factor in zip(SHIFTS, weights[1]):
        tap = factor * roll(own, shift, 0)[:rows]
        result = tap if result is None else result + tap
    return result


def factors(mix):
    inverses, ratios = [], []
    for level in range(LEV):
        pivot = 1.0
        if level < LEV - 1:
            pivot = pivot + mix[level]
        if level > 0:
            pivot = pivot + mix[level - 1] * (1.0 - ratios[-1])
        inverse = 1.0 / pivot
        inverses.append(inverse)
        if level < LEV - 1:
            ratios.append(mix[level] * inverse)
    return inverses, ratios


def solve(rhs, mix, inverses, ratios):
    values = []
    for level in range(LEV):
        source = rhs[level]
        if level > 0:
            source = mix[level - 1] * values[-1] if source is None else source + mix[level - 1] * values[-1]
        values.append(source * inverses[level])
    result = [None] * LEV
    result[-1] = values[-1]
    for level in range(LEV - 2, -1, -1):
        result[level] = values[level] + ratios[level] * result[level + 1]
    return result


def rim_of_levels(north, south, level):
    sub, block, odd = sublanes(), 8 * (level // 2), level % 2
    a, b = south[block : block + 8], north[block : block + 8]
    return jnp.where(sub < 4, roll(a, -4 * odd, 0), roll(b, 4 - 4 * odd, 0))


def side_of(west_tile, east_tile, at, width, rows):
    lane = lanes(rows)
    a, b = roll(east_tile[:rows], -at, 1), roll(west_tile[:rows], COLS - width - at, 1)
    return jnp.where(lane < width, a, jnp.where(lane >= COLS - width, b, 0.0))


IMPULSE = [1.0] + [None] * (LEV - 1)


def prepare_own(prev, mix, index, weight, inverse, unit, seen):
    own_mix = [mix[level] for level in range(LEV - 1)]
    inverses, ratios = factors(own_mix)
    impulse = solve(IMPULSE, own_mix, inverses, ratios)
    for level in range(LEV):
        inverse[level] = inverses[level]
        unit[level] = impulse[level]

    @pl.when(lax.axis_index("comp") == 0)
    def _():
        seen[...] = regrid_tile(prev[1], index, weight)


def own_early_kernel(*refs):
    @pl.when(starts_early())
    def _():
        prepare_own(*refs)


def own_late_kernel(prev, mix, index, weight, *both):
    @pl.when(jnp.logical_not(starts_early()))
    def _():
        prepare_own(prev, mix, index, weight, *both[len(both) // 2 :])


def prepare_side(
    state, vel, near, far, inverse, unit, side_mix, side_state, lon_own, lon_side
):
    west, east = sides(near[0:ROWS], far[0:ROWS])
    own_weights = transport_weights(vel[0], vel[1])
    side_weights = transport_weights(
        *(side_of(west, east, AT_VEL + 2 * part, 2, ROWS) for part in range(2))
    )
    for level in range(LEV):
        there = side_of(west, east, 4 * level, 4, ROWS)
        side_state[level] = there
        lon_own[level] = along_longitude(state[level], there, own_weights)
        lon_side[level] = along_longitude(there, state[level], side_weights)
    mixes = [side_of(west, east, AT_MIX + 2 * level, 2, ROWS) for level in range(LEV - 1)]
    inverses, ratios = factors(mixes)
    impulse = solve(IMPULSE, mixes, inverses, ratios)
    for level in range(LEV):
        inverse[level] = inverses[level]
        unit[level] = impulse[level]
        if level < LEV - 1:
            side_mix[level] = mixes[level]


def side_early_kernel(state, vel, near, far, *out):
    @pl.when(starts_early())
    def _():
        prepare_side(state, vel, near, far, *out)


def side_late_kernel(state, vel, near, far, *both):
    @pl.when(jnp.logical_not(starts_early()))
    def _():
        prepare_side(state, vel, near, far, *both[len(both) // 2 :])


def stored(inverse, mixes):
    inverses = [inverse[level] for level in range(LEV)]
    return inverses, [mixes[level] * inverses[level] for level in range(LEV - 1)]


def top_step(state, mix, vel, rate, flux, columns, rows, inverse, unit, seen, lon_own, fluxes):
    west, east = column_messages(columns)
    north, south = row_messages(*rows)
    weights = transport_weights(vel[0], vel[1])
    moved = []
    for level in range(LEV):
        own = jnp.concatenate([state[level], rim_of_levels(north, south, level)], axis=0)
        moved.append(lon_own[level] + along_latitude(own, weights, ROWS))
    own_mix = [mix[level] for level in range(LEV - 1)]
    top = solve(moved, own_mix, *stored(inverse, own_mix))[0] + flux[...] * unit[0]
    fluxes[0:ROWS] = flux[...]
    fluxes[ROWS : 2 * ROWS] = west[ROWS:]
    fluxes[2 * ROWS : 3 * ROWS] = east[ROWS:]
    fluxes[3 * ROWS : 4 * ROWS] = north[AT_FLUX : AT_FLUX + ROWS]
    fluxes[4 * ROWS : 5 * ROWS] = south[AT_FLUX : AT_FLUX + ROWS]
    fluxes[5 * ROWS :] = rate[...] * (seen[...] - top)


def halo_step(state, mix, vel, columns, rows, inverse, side, before, before_side, unit_rim):
    west, east = column_messages(columns)
    north, south = row_messages(*rows)
    at_lat = lax.axis_index("lat")
    sub = sublanes()
    valid = ((sub < 4) & (at_lat < lax.axis_size("lat") - 1)) | ((sub >= 4) & (at_lat > 0))

    def rim2(at):
        block, offset = 8 * (at // 8), at % 8
        a, b = south[block : block + 8], north[block : block + 8]
        a, b = roll(a, -offset, 0), roll(b, 6 - offset, 0)
        return jnp.where(sub < 2, a, jnp.where(sub >= 6, b, 0.0))

    inverse_side, side_mix_ref, side_state, lon_own, lon_side = side
    a, b = south[AT_WEST : AT_WEST + 8], north[AT_WEST : AT_WEST + 8]
    west_rim = jnp.where(sub < 4, a, roll(b, 4, 0))
    east_rim = jnp.where(sub < 4, roll(a, 4, 0), b)
    own_mix = [mix[level] for level in range(LEV - 1)]
    side_mix = [side_mix_ref[level] for level in range(LEV - 1)]
    rim_mix = [rim2(AT_MIX + 2 * level) for level in range(LEV - 1)]
    rim_vel = [rim2(AT_VEL + 2 * part) for part in range(2)]
    own_weights = transport_weights(
        *(jnp.concatenate([vel[part], rim_vel[part]], axis=0) for part in range(2))
    )
    rim_weights = transport_weights(*rim_vel)
    side_weights = transport_weights(
        *(side_of(west, east, AT_VEL + 2 * part, 2, ROWS) for part in range(2))
    )
    rim_factors = factors(rim_mix)
    moved, moved_rim, moved_side = [], [], []
    for level in range(LEV):
        rim = rim_of_levels(north, south, level)
        side_rim = side_of(west_rim, east_rim, 4 * level, 4, 8)
        taps = along_latitude(jnp.concatenate([state[level], rim], axis=0), own_weights, 24)
        moved.append(lon_own[level] + taps[:ROWS])
        moved_rim.append(along_longitude(rim, side_rim, rim_weights) + taps[ROWS:])
        there = jnp.concatenate([side_state[level], side_rim], axis=0)
        moved_side.append(lon_side[level] + along_latitude(there, side_weights, ROWS))
    rim = solve(moved_rim, rim_mix, *rim_factors)
    impulse = solve(IMPULSE, rim_mix, *rim_factors)
    own = solve(moved, own_mix, *stored(inverse, own_mix))
    there = solve(moved_side, side_mix, *stored(inverse_side, side_mix))
    for level in range(LEV):
        before[level, 0:ROWS] = own[level]
        before[level, ROWS:] = jnp.where(valid, rim[level], 0.0)
        before_side[level] = there[level]
        unit_rim[level] = jnp.where(valid, impulse[level], 0.0)


def middle_kernel(
    state, mix, vel, rate, flux, early, late, to_early, to_late, row0, row1,
    inverse, unit, seen, inverse_side, side_mix, side_state, lon_own, lon_side,
    fluxes, before, before_side, unit_rim,
):
    columns, rows = (early, late, to_early, to_late), (row0, row1)
    side = (inverse_side, side_mix, side_state, lon_own, lon_side)

    @pl.when(lax.axis_index("comp") == 0)
    def _():
        top_step(state, mix, vel, rate, flux, columns, rows, inverse, unit, seen, lon_own, fluxes)

    halo_step(state, mix, vel, columns, rows, inverse, side, before, before_side, unit_rim)


def second_step_kernel(
    mix, vel, rate_in, index, weight, early, late, to_early, to_late, row0, row1,
    inverse, unit, unit_side, before, before_side, unit_rim, got, new_state, series,
):
    columns, rows = (early, late, to_early, to_late), (row0, row1)
    sub = sublanes()
    lane = lanes(ROWS)
    tables = [got[0, k * ROWS : (k + 1) * ROWS] for k in range(6)]
    own_mix = [mix[level] for level in range(LEV - 1)]

    def advance(force, force_rim, force_side, force1):
        weights = transport_weights(vel[0], vel[1])
        moved = []
        for level in range(LEV):
            tile = before[level, 0:ROWS] + force * unit[level]
            rim = before[level, ROWS:] + force_rim * unit_rim[level]
            there = before_side[level] + force_side * unit_side[level]
            if level == 0:
                top = tile
            own = jnp.concatenate([tile, rim], axis=0)
            taps = along_latitude(own, weights, ROWS)
            moved.append(along_longitude(tile, there, weights) + taps)
        moved[0] = moved[0] + force1
        solved = solve(moved, own_mix, *stored(inverse, own_mix))
        for level in range(LEV):
            new_state[level] = solved[level]
        return top, solved[0]

    @pl.when(lax.axis_index("comp") == 0)
    def _():
        rim = jnp.where(sub < 4, tables[4][0:8], tables[3][8:16])
        side = jnp.where(lane < 64, tables[2], tables[1])
        advance(tables[0], rim, side, tables[5])
        series[0] = tables[0]
        series[1] = tables[5]

    @pl.when(lax.axis_index("comp") != 0)
    def _():
        rate = rate_in[...]
        west, east = column_messages(columns)
        north, south = row_messages(*rows)

        def of_rows(message, table, place):
            index8 = message[AT_INDEX : AT_INDEX + 8].astype(jnp.int32)
            total = gather_cells(table, index8) * message[AT_WEIGHT : AT_WEIGHT + 8]
            total = total + roll(total, 4, 0)
            total = total + roll(total, 2, 0)
            block, offset = 8 * (AT_RATE // 8), AT_RATE % 8
            return roll(message[block : block + 8], place - offset, 0) * roll(total, place, 0)

        def of_columns(message, table, place):
            tile = message[0:ROWS]
            total = roll(gather_cells(table, tile.astype(jnp.int32)), AT_WEIGHT - AT_INDEX, 1) * tile
            total = total + roll(total, -4, 1)
            total = total + roll(total, -2, 1)
            return roll(tile, place - AT_RATE, 1) * roll(total, place - AT_WEIGHT, 1)

        rim = jnp.where(sub < 4, of_rows(south, tables[4], 0), of_rows(north, tables[3], 6))
        side = jnp.where(
            lane < 64, of_columns(east, tables[2], 0), of_columns(west, tables[1], COLS - 2)
        )
        force = rate * regrid_tile(tables[0], index, weight)
        force1 = rate * regrid_tile(tables[5], index, weight)
        top, last = advance(force, rim, side, force1)
        series[0] = top
        series[1] = last


def call(kernel, shapes, *args, scratch=(), place=pltpu.VMEM, aliases=None):
    return pl.pallas_call(
        kernel,
        out_shape=[s if hasattr(s, "dtype") else jax.ShapeDtypeStruct(s, jnp.float32) for s in shapes],
        in_specs=[pl.BlockSpec(memory_space=place)] * len(args),
        out_specs=[pl.BlockSpec(memory_space=pltpu.VMEM)] * len(shapes),
        scratch_shapes=list(scratch),
        compiler_params=pltpu.CompilerParams(vmem_limit_bytes=16 * 1024 * 1024),
        input_output_aliases=aliases or {},
        interpret=INTERPRET,
    )(*args)


def pairs(count, start, step):
    return [pair for i in range(start, count - 1, step) for pair in ((i, i + 1), (i + 1, i))]


def partners(count):
    return [[i, i + 1] for i in range(0, count, 2)]


def per_device(
    state, prev_surface, mixing, velocity, coupling, sea_mask, interp_index, interp_weight
):
    n_lat, n_lon = lax.axis_size("lat"), lax.axis_size("lon")
    given = (
        state[0], prev_surface, mixing[0], velocity[0],
        coupling[0], sea_mask[0], interp_index[0], interp_weight[0],
    )
    state, prev, mix, vel, couple, mask, index, weight = given
    tile = (ROWS, COLS)
    column_shape = (COL_MESSAGE, COLS)
    to_far, flux, rate, state, prev, mix, vel, index, weight = call(
        pack_columns_kernel,
        [column_shape, tile, tile, state, prev, mix, vel, index, weight],
        *(pltpu.with_memory_space_constraint(x, pltpu.HBM) for x in given), place=pltpu.HBM,
        scratch=[pltpu.VMEM(tile, couple.dtype), pltpu.VMEM(tile, mask.dtype), pltpu.SemaphoreType.DMA((8,))],
    )
    joints = range(1, n_lon, 2)
    sent = [((i, (i + 1) % n_lon) if i % 4 == 3 else (i + 1, i)) for i in joints]
    to_early = lax.ppermute(to_far, "lon", sent)
    fields = (state, mix, vel, rate, index, weight, flux)
    (to_near,) = call(near_early_kernel, [column_shape], *fields)
    early = lax.ppermute(to_near, "lon", pairs(n_lon, 0, 4))
    narrow = (LEV, ROWS, COLS)
    own_shapes = [narrow, narrow, tile]
    own = call(own_early_kernel, own_shapes, prev, mix, index, weight)
    to_late = lax.ppermute(to_far, "lon", [(j, i) for i, j in sent])
    (to_near,) = call(near_late_kernel, [column_shape], *fields)
    late = lax.ppermute(to_near, "lon", pairs(n_lon, 2, 4))
    columns = (early, late, to_early, to_late)
    row_shape = (ROW_MESSAGE, COLS)
    to_near, to_far = call(
        pack_rows_kernel, [row_shape, row_shape],
        state, mix, vel, rate, index, weight, flux, *columns,
    )
    row1 = lax.ppermute(to_far, "lat", pairs(n_lat, 1, 2))
    row0 = lax.all_gather(to_near, "lat", axis_index_groups=partners(n_lat))
    rows = (row0, row1)
    parts = [(LEV, 24, COLS), narrow, (LEV, 8, COLS)]
    inverse, unit, seen = call(
        own_late_kernel, own_shapes, prev, mix, index, weight, *own,
        aliases={4 + k: k for k in range(len(own_shapes))},
    )
    shapes = [narrow, narrow, (LEV - 1, ROWS, COLS), narrow, narrow, narrow]
    side = call(side_early_kernel, shapes, state, vel, early, to_early)
    inverse_side, unit_side, *side = call(
        side_late_kernel, shapes, state, vel, late, to_late, *side,
        aliases={4 + k: k for k in range(len(shapes))},
    )
    known = (inverse_side, *side)
    fluxes, *before = call(
        middle_kernel, [(6 * ROWS, COLS)] + parts,
        state, mix, vel, rate, flux, *columns, *rows, inverse, unit, seen, *known,
    )
    got = lax.all_gather(fluxes, "comp")
    new_state, series = call(
        second_step_kernel, [narrow, (NSTEP, ROWS, COLS)],
        mix, vel, rate, index, weight, *columns, *rows, inverse, unit, unit_side, *before, got,
    )
    return new_state[None], series[None]


def solution(mesh):
    in_specs = (
        P("comp", None, "lat", "lon"),
        P(None, "lat", "lon"),
        P("comp", None, "lat", "lon"),
        P("comp", None, "lat", "lon"),
        P("comp", "lat", "lon"),
        P("comp", "lat", "lon"),
        P("comp", None, "lat", "lon"),
        P("comp", None, "lat", "lon"),
    )
    out_specs = (P("comp", None, "lat", "lon"), P("comp", None, "lat", "lon"))

    return jax.shard_map(
        per_device, mesh=mesh, in_specs=in_specs, out_specs=out_specs, check_vma=False
    )
```
